32 devices in a mesh: seq: 4 (over y, core), head: 8 (over z, x).
Axes of the slice: x: 2, y: 2, z: 4, core: 2. Of those that a mesh axis runs over, the one named last changes fastest.
Arguments:
- queries: bfloat16 [1024, 512], P('seq', 'head'), may hold values from -6 to 6
- key_rows: bfloat16 [1024, 512], P('seq', 'head'), may hold values from -6 to 6
- values: bfloat16 [1024, 1024], P('seq', 'head'), may hold values from -6 to 6
- log_decay: float32 [8, 1024], P('head', 'seq'), may hold values from -0.8 to 0, as said below
- beta_rate: float32 [8, 1024], P('head', 'seq'), may hold values from 0 to 0.95, as said below
- start_states: float32 [4, 8, 128, 128], P('seq', 'head'), may hold values from -4 to 4
- output_grad: bfloat16 [1024, 1024], P('seq', 'head'), may hold values from -6 to 6
Outputs:
- query_grad: float32 [1024, 512], P('seq', 'head')
- key_grad: float32 [1024, 512], P('seq', 'head')
- value_grad: float32 [1024, 1024], P('seq', 'head')
- rate_grad: float32 [8, 1024], P('head', 'seq')
The draws below stay inside these ranges and needn't reach their ends.
Inputs may be any that keep to these rules, and one draw needn't show every extreme that they name: `log_decay`: every entry is at most zero. `beta_rate`: every entry is positive.
All inputs are finite; a program needn't handle non-finite values.
Results may differ from the reference program's by a relative error of at most 0.00035.
Values may be sent and summed in bfloat16 or wider, within the bound.
No kernel may reach another device: no remote copies, remote signals or barrier semaphores. Data moves between devices by JAX's collectives and lax.ppermute only.
A program may use at most 64 MiB of HBM per device.

```python
import jax
import jax.numpy as jnp
from jax import lax

DK = 128
DV = 128
SEC_TOK = 256
OUTPUT_CHANNELS = 8
QK_HEADS = 4
SEQUENCE_LENGTH = 1024
N_SEQ = 4


def head_speeds(key):
    share = 0.5
    return jax.random.uniform(jax.random.fold_in(key, 11), (OUTPUT_CHANNELS, 1)) < share


def draw_log_decay(key, part):
    quick_heads = head_speeds(key)
    stream_tracks = jax.random.split(jax.random.fold_in(key, 23), 5)
    quick_rate = jnp.exp(jax.random.uniform(stream_tracks[0], (OUTPUT_CHANNELS, 1), minval=jnp.log(1.0 / 60.0), maxval=jnp.log(1.0 / 20.0)))
    slow_rate = jnp.exp(jax.random.uniform(stream_tracks[1], (OUTPUT_CHANNELS, 1), minval=jnp.log(0.02 / SEQUENCE_LENGTH), maxval=jnp.log(0.2 / SEQUENCE_LENGTH)))
    channel_velocity = jnp.where(quick_heads, quick_rate, slow_rate)
    rough_multiplier = jax.random.uniform(stream_tracks[2], (OUTPUT_CHANNELS, SEQUENCE_LENGTH), minval=0.5, maxval=1.5)
    pulse_batches = jax.random.uniform(stream_tracks[3], (OUTPUT_CHANNELS, SEQUENCE_LENGTH)) < 2.0 / SEQUENCE_LENGTH
    objective_numbers = jnp.log(jax.random.uniform(stream_tracks[4], (OUTPUT_CHANNELS, SEQUENCE_LENGTH), minval=0.5, maxval=0.8))
    return (-channel_velocity * rough_multiplier + jnp.where(pulse_batches, objective_numbers, 0.0)).astype(jnp.float32)


def draw_beta_rate(key, part):
    quick_heads = head_speeds(key)
    stream_tracks = jax.random.split(jax.random.fold_in(key, 37), 2)
    strong_rate = jax.random.uniform(stream_tracks[0], (OUTPUT_CHANNELS, SEQUENCE_LENGTH), minval=0.3, maxval=0.95)
    weak_rate = jax.random.uniform(stream_tracks[1], (OUTPUT_CHANNELS, SEQUENCE_LENGTH), minval=0.3, maxval=1.5) * (DK / SEC_TOK)
    return jnp.where(quick_heads, strong_rate, weak_rate).astype(jnp.float32)


def level_of(stream_key, dims, shards, smallest, top_value):
    level, own = 1.0, jax.random.fold_in(stream_key, 6)
    for dim, blocks in shards:
        steps = jnp.exp(jax.random.uniform(jax.random.fold_in(own, dim), (blocks,), jnp.float32, smallest / len(shards), top_value / len(shards)))
        level = level * jnp.repeat(steps, dims[dim] // blocks).reshape([-1 if axis == dim else 1 for axis in range(len(dims))])
    return level


def gaussian(key, extent, width, bound, cuts=(), held_as=jnp.bfloat16):
    values = width * jax.random.normal(key, extent, jnp.float32)
    if cuts:
        values = values * level_of(key, extent, cuts, -0.22, 0.18)
    return jnp.clip(values, -bound, bound).astype(held_as)


def setup_inputs(seed: int = 0) -> dict:
    streams_of = jax.random.split(jax.random.key(seed), 8)
    return {
        "queries": gaussian(streams_of[0], (SEQUENCE_LENGTH, QK_HEADS * DK), 1.0, 6.0, ((0, 4), (1, 8))),
        "key_rows": gaussian(streams_of[1], (SEQUENCE_LENGTH, QK_HEADS * DK), 1.0, 6.0, ((0, 4), (1, 8))),
        "values": gaussian(streams_of[2], (SEQUENCE_LENGTH, OUTPUT_CHANNELS * DV), 1.0, 6.0, ((0, 4), (1, 8))),
        "log_decay": draw_log_decay(jax.random.fold_in(streams_of[7], 71), 0),
        "beta_rate": draw_beta_rate(jax.random.fold_in(streams_of[7], 71), 0),
        "start_states": gaussian(streams_of[5], (N_SEQ, OUTPUT_CHANNELS, DV, DK), 0.5, 4.0, ((0, 4), (1, 8)), jnp.float32),
        "output_grad": gaussian(streams_of[6], (SEQUENCE_LENGTH, OUTPUT_CHANNELS * DV), 1.0, 6.0, ((0, 4), (1, 8))),
    }


PRECISE = lax.Precision.HIGHEST

def unit_rows(rows, factor):
    return rows * (factor / jnp.sqrt(lax.optimization_barrier(jnp.sum(rows * rows, -1, keepdims=True)) + 1e-06))

def run_head(state, query_norm, key_norm, value_rows, rates, decays):

    def advance(carried, inputs):
        query_row, key_row, value_row, rate_now, decay_now = inputs
        damped = jnp.exp(decay_now) * carried
        predicted = jnp.dot(damped, key_row, precision=PRECISE)
        carried = damped + rate_now * jnp.outer(value_row - predicted, key_row)
        return (carried, jnp.dot(carried, query_row, precision=PRECISE))
    final, outputs = lax.scan(advance, state, (query_norm, key_norm, value_rows, rates, decays))
    return (outputs, final)

def pair_forward(query_in, key_in, value_in, rate_in, state_in, decays):
    query_norm = unit_rows(query_in, DK ** (-0.5))
    key_norm = unit_rows(key_in, 1.0)
    return jax.vmap(run_head, in_axes=(0, None, None, 0, 0, 0))(state_in, query_norm, key_norm, value_in, rate_in, decays)

def pair_backward(inputs):
    query_in, key_in, value_in, rate_in, state_in, decays, grad_out, later = inputs

    def forward_fn(query_arg, key_arg, value_arg, rate_arg, state_arg):
        return pair_forward(query_arg, key_arg, value_arg, rate_arg, state_arg, decays)
    _, pullback = jax.vjp(forward_fn, query_in, key_in, value_in, rate_in, state_in)
    return pullback((grad_out, later))

def reference(queries, key_rows, values, log_decay, beta_rate, start_states, output_grad):
    groups = OUTPUT_CHANNELS // 2
    query_all = queries.astype(jnp.float32).reshape(N_SEQ, SEC_TOK, groups, DK).transpose(0, 2, 1, 3)
    key_all = key_rows.astype(jnp.float32).reshape(N_SEQ, SEC_TOK, groups, DK).transpose(0, 2, 1, 3)
    value_all = values.astype(jnp.float32).reshape(N_SEQ, SEC_TOK, groups, 2, DV).transpose(0, 2, 3, 1, 4)
    grad_all = output_grad.astype(jnp.float32).reshape(N_SEQ, SEC_TOK, groups, 2, DV).transpose(0, 2, 3, 1, 4)
    rate_all = beta_rate.reshape(groups, 2, N_SEQ, SEC_TOK).transpose(2, 0, 1, 3)
    decay_all = log_decay.reshape(groups, 2, N_SEQ, SEC_TOK).transpose(2, 0, 1, 3)
    state_all = start_states.reshape(N_SEQ, groups, 2, DV, DK)

    def section_step(later, inputs):
        query_sec, key_sec, value_sec, rate_sec, state_sec, decay_sec, grad_sec = inputs
        query_part, key_part, value_part, rate_part, state_part = lax.map(pair_backward, (query_sec, key_sec, value_sec, rate_sec, state_sec, decay_sec, grad_sec, later))
        return (state_part, (query_part, key_part, value_part, rate_part))
    initial = jnp.zeros((groups, 2, DV, DK), jnp.float32)
    _, (query_part, key_part, value_part, rate_part) = lax.scan(section_step, initial, (query_all, key_all, value_all, rate_all, state_all, decay_all, grad_all), reverse=True)
    query_grad = query_part.transpose(0, 2, 1, 3).reshape(SEQUENCE_LENGTH, groups * DK)
    key_grad = key_part.transpose(0, 2, 1, 3).reshape(SEQUENCE_LENGTH, groups * DK)
    value_grad = value_part.transpose(0, 3, 1, 2, 4).reshape(SEQUENCE_LENGTH, OUTPUT_CHANNELS * DV)
    rate_grad = rate_part.transpose(1, 2, 0, 3).reshape(OUTPUT_CHANNELS, SEQUENCE_LENGTH)
    return (query_grad, key_grad, value_grad, rate_grad)
```

```python
import jax
import jax.numpy as jnp
from jax import lax
from jax.experimental import pallas as pl
from jax.experimental.pallas import tpu as pltpu
from jax.sharding import PartitionSpec as P

F32 = jnp.float32
BF16 = jnp.bfloat16
BASE = 16
NN = (((1,), (0,)), ((), ()))
NT = (((1,), (1,)), ((), ()))


def split(x):
    high = x.astype(BF16)
    return (high, (x - high.astype(F32)).astype(BF16))


def mm(left, right, dims=NN):
    left = left if isinstance(left, tuple) else (left if left.dtype == BF16 else split(left))
    right = right if isinstance(right, tuple) else (right if right.dtype == BF16 else split(right))

    def one(a, b):
        return lax.dot_general(a, b, dims, preferred_element_type=F32)

    if isinstance(left, tuple) and isinstance(right, tuple):
        return one(left[0], right[0]) + (one(left[0], right[1]) + one(left[1], right[0]))
    if isinstance(left, tuple):
        return one(left[0], right) + one(left[1], right)
    if isinstance(right, tuple):
        return one(left, right[0]) + one(left, right[1])
    return one(left, right)


def ids(shape):
    return lax.broadcasted_iota(jnp.int32, shape, 0), lax.broadcasted_iota(jnp.int32, shape, 1)


def to_col(row, eye):
    return jnp.sum(jnp.where(eye, row, 0.0), 1, keepdims=True)


def to_row(col, eye):
    return jnp.sum(jnp.where(eye, col, 0.0), 0, keepdims=True)


def base_inverse(nil, base):
    size = nil.shape[0]
    count = size // base
    row, lane = ids((base, size))
    block = lane // base
    packed = jnp.zeros((base, size), F32)
    for b in range(count):
        packed = jnp.where(block == b, nil[b * base : (b + 1) * base, :], packed)
    solved = jnp.where(row == lane % base, 1.0, 0.0)
    for j in range(base - 1):
        factor = jnp.take_along_axis(packed, block * base + j, axis=1)
        factor = jnp.where(row > j, factor, 0.0)
        solved = solved + factor * solved[j : j + 1, :]
    return jnp.concatenate([jnp.where(block == b, solved, 0.0) for b in range(count)], 0)


def half_inverse(nil):
    size = nil.shape[0]
    row, lane = ids((size, size))
    inv = base_inverse(nil, BASE)
    width = BASE
    while width < size:
        factor = 4 if size >= 4 * width else 2
        wide = width * factor
        off = jnp.where((row // wide == lane // wide) & (row // width != lane // width), nil, 0.0)
        inv_s = split(inv)
        step = split(mm(inv_s, off))
        first = inv + mm(step, inv_s)
        if factor == 4:
            first = first + mm(mm(step, step), first)
        inv = first
        width = wide
    return inv


def inverse(nil):
    size = nil.shape[0]
    half = size // 2
    upper = half_inverse(nil[:half, :half])
    lower = half_inverse(nil[half:, half:])
    corner = mm(mm(lower, nil[half:, :half]), upper)
    top = jnp.concatenate([upper, jnp.zeros((half, half), F32)], 1)
    return jnp.concatenate([top, jnp.concatenate([corner, lower], 1)], 0)


def decays(decay_row, row, lane):
    cum_col = jnp.sum(jnp.where(lane <= row, decay_row, 0.0), 1, keepdims=True)
    return cum_col, to_row(cum_col, row == lane)


def map_kernel(q_ref, k_ref, other_ref, g_ref, decay_ref, rate_ref, map_ref, inv_ref, low_ref, score_ref, rows_ref):
    half, length = q_ref.shape
    q_t = jnp.concatenate([q_ref[...], other_ref[0:half, :]], 0)
    k_t = jnp.concatenate([k_ref[...], other_ref[half:, :]], 0)
    width = q_t.shape[0]
    row, lane = ids((length, length))
    eye = row == lane
    cum_col, cum_row = decays(decay_ref[...], row, lane)
    q_f, k_f = q_t.astype(F32), k_t.astype(F32)
    q_scale = width ** (-0.5) / jnp.sqrt(jnp.sum(q_f * q_f, 0, keepdims=True) + 1e-6)
    k_scale = 1.0 / jnp.sqrt(jnp.sum(k_f * k_f, 0, keepdims=True) + 1e-6)
    rate_row = rate_ref[...]
    k_rows = k_f.T.astype(BF16)
    q_rows = q_f.T.astype(BF16)
    spread = jnp.exp(jnp.where(lane <= row, cum_col - cum_row, -1e30))
    low = jnp.where(lane < row, spread, 0.0) * (mm(k_rows, k_t) * (to_col(k_scale, eye) * k_scale))
    inv = inverse(-(to_col(rate_row, eye) * low))
    score = spread * (mm(q_rows, k_t) * (to_col(q_scale, eye) * k_scale))
    grow = jnp.exp(cum_row)
    last = cum_row[:, length - 1 :]
    tail = jnp.exp(last - cum_row)
    w_t = mm(k_t, inv * (rate_row * grow * k_scale), NT)
    side = q_f * (q_scale * grow) - mm(w_t, score, NT)
    w_row, w_lane = ids((width, width))
    map_ref[0:width, :] = jnp.where(w_row == w_lane, jnp.exp(last), 0.0) - mm(w_t * (tail * k_scale), k_rows)
    map_ref[width:, :] = mm(side, g_ref[...])
    inv_ref[...] = inv
    low_ref[...] = low
    score_ref[...] = score
    rows_ref[...] = jnp.concatenate([cum_row, q_scale, k_scale, tail, grow, rate_row, cum_row, cum_row], 0)


def join_kernel(flag_ref, own_ref, got_ref, total_ref, ahead_ref):
    width = own_ref.shape[1]
    low = flag_ref[0] == 1
    own, got = own_ref[...], got_ref[...]
    first = jnp.where(low, own[0:width, :], got[0:width, :])
    second = jnp.where(low, got[width:, :], own[width:, :])
    third = jnp.where(low, own[width:, :], got[width:, :])
    total_ref[...] = mm(first, second) + third
    row, lane = ids((2 * width, width))
    ahead_ref[...] = jnp.where(low, got, jnp.where(row == lane, 1.0, 0.0))


def local_kernel(
    q_ref, k_ref, other_ref, v_ref, g_ref, start_ref, inv_ref, low_ref, score_ref, rows_ref, flag_ref, after_ref,
    u_ref, ut_ref, y_ref, psi_ref, psit_ref, w_ref, sym_ref, dq_ref, dk_ref, start_t_ref,
):
    half, length = q_ref.shape
    q_t = jnp.concatenate([q_ref[...], other_ref[0:half, :]], 0)
    k_t = jnp.concatenate([k_ref[...], other_ref[half:, :]], 0)
    width = q_t.shape[0]
    row, lane = ids((length, length))
    eye = row == lane
    rows = rows_ref[...]
    cum_row, q_scale, k_scale, tail, grow, rate_row = (rows[i : i + 1, :] for i in range(6))
    cum_col = to_col(cum_row, eye)
    q_f, k_f = q_t.astype(F32), k_t.astype(F32)
    k_rows = k_f.T.astype(BF16)
    start = start_ref[...]
    start = jnp.where(flag_ref[0] == 1, start, pltpu.roll(start, half, 1))
    start_t = start.T
    start_ts = split(start_t)
    value = v_ref[...].astype(F32)
    grad = g_ref[...]
    grad_t = grad.astype(F32).T.astype(BF16)
    inv = inv_ref[...]
    base = value - to_col(grow * k_scale, eye) * mm(k_rows, start, NT)
    u = mm(inv * rate_row, base)
    u_s = split(u)
    u_t = u.T
    u_ts = split(u_t)
    w_ref[...] = base - mm(low_ref[...], u_s)
    inv_s = split(inv)
    y_t = mm(mm(grad_t, score_ref[...]), inv_s)
    psi_t = mm(k_t, inv * to_col(tail * k_scale, eye))
    y = y_t.T
    y_ts = split(y_t)
    y_s = split(y)
    both = jnp.exp(-jnp.abs(cum_col - cum_row))
    rate_col = to_col(rate_row, eye)
    decay_low = jnp.where(lane < row, both * -rate_col, 0.0)
    decay_up = jnp.where(lane > row, both * -rate_row, 0.0)
    sym = decay_low * mm(y_s, u_ts) + decay_up * mm(u_s, y_ts)
    d_score = mm(grad, u_ts) * jnp.where(lane <= row, both, 0.0)
    k_n = k_f * k_scale
    q_n = q_f * q_scale
    dq = mm(k_t, d_score * k_scale, NT) + grow * mm(start_ts, grad_t)
    unit = q_f * (q_scale * width**0.5)
    dq_ref[...] = q_scale * (dq - unit * jnp.sum(unit * dq, 0, keepdims=True))
    dk_ref[...] = mm(k_n, sym) + mm(q_n, d_score) - mm(start_ts, y_t * (grow * rate_row))
    u_ref[...] = u
    ut_ref[...] = u_t
    y_ref[...] = y
    psi_ref[...] = psi_t.T
    psit_ref[...] = psi_t
    sym_ref[...] = decay_low + decay_up
    start_t_ref[...] = start_t


def far_kernel(
    flag_ref, got_ref, ahead_ref, k_ref, other_ref, u_ref, ut_ref, y_ref, psi_ref, psit_ref, w_ref, sym_ref, dq_ref,
    dk_ref, start_t_ref, rows_ref, send_ref, keep_ref, value_ref, rate_out_ref,
):
    half, length = k_ref.shape
    k_t = jnp.concatenate([k_ref[...], other_ref[half:, :]], 0)
    width = k_t.shape[0]
    row, lane = ids((length, length))
    eye = row == lane
    rows = rows_ref[...]
    k_scale, tail, grow, rate_row = (rows[i : i + 1, :] for i in range(2, 6))
    ahead = ahead_ref[...]
    got = jnp.where(flag_ref[1] == 1, got_ref[...], 0.0)
    far_t = split(mm(ahead[0:width, :], got) + ahead[width:, :])
    u_s = split(u_ref[...])
    psi_s = split(psi_ref[...])
    psi_t = psit_ref[...]
    uz_t = mm(far_t, ut_ref[...])
    uz = mm(u_s, far_t, NT)
    sz = mm(start_t_ref[...], far_t, NT)
    y = y_ref[...] + mm(psi_s, far_t)
    sym = sym_ref[...] * jnp.where(lane < row, mm(psi_s, uz_t), mm(uz, psi_t))
    k_n = k_t.astype(F32) * k_scale
    dk = dk_ref[...] + mm(k_n, sym) + tail * uz_t - mm(sz, psi_t * (grow * rate_row))
    dk = k_scale * (dk - k_n * jnp.sum(k_n * dk, 0, keepdims=True))
    dq = dq_ref[...]
    keep_ref[...] = jnp.concatenate([dq[0:half, :], dk[0:half, :]], 0)
    send_ref[...] = jnp.concatenate([dq[half:, :], dk[half:, :]], 0)
    value_ref[...] = to_col(rate_row, eye) * y
    rate_out_ref[...] = to_row(jnp.sum(y * w_ref[...], 1, keepdims=True), eye)


def add_kernel(keep_ref, got_ref, q_ref, k_ref):
    half = q_ref.shape[0]
    q_ref[...] = keep_ref[0:half, :] + got_ref[0:half, :]
    k_ref[...] = keep_ref[half:, :] + got_ref[half:, :]


def call(kernel, outs, *args, smem=()):
    return pl.pallas_call(
        kernel,
        out_shape=tuple(jax.ShapeDtypeStruct(shape, F32) for shape in outs),
        in_specs=[
            pl.BlockSpec(memory_space=pltpu.SMEM if i in smem else pltpu.VMEM) for i in range(len(args))
        ],
        out_specs=tuple(pl.BlockSpec(memory_space=pltpu.VMEM) for _ in outs),
        compiler_params=pltpu.CompilerParams(vmem_limit_bytes=24 << 20),
    )(*args)


def swap(x, axis, apart):
    return lax.ppermute(x, axis, [(i, i ^ 1 << apart) for i in range(lax.axis_size(axis))])


def per_device(queries, key_rows, values, log_decay, beta_rate, start_states, output_grad):
    count = lax.axis_size("seq")
    stages = count.bit_length() - 1
    assert count == 1 << stages and stages >= 2
    place = lax.axis_index("seq")
    parity = lax.axis_index("head") % 2
    q_t, k_t = queries.T, key_rows.T
    half, length = q_t.shape
    width = 2 * half
    depth = values.shape[1]
    start = start_states[0, 0]
    other = swap(jnp.concatenate([q_t, k_t], 0), "head", 0)

    section, inv, low, score, rows = call(
        map_kernel,
        [(2 * width, depth), (length, length), (length, length), (length, length), (8, length)],
        q_t, k_t, other, output_grad, log_decay, beta_rate,
    )

    def flags(bit):
        return jnp.stack([1 - (place >> bit) % 2, parity * 0]).astype(jnp.int32)

    got = swap(section, "seq", 0)
    if stages == 2:
        total, ahead = call(
            join_kernel, [(width, depth), (2 * width, depth)], flags(0), section, got, smem=(0,)
        )
    else:
        precise = lax.Precision.HIGHEST
        dot = lambda a, b: jnp.dot(a, b, precision=precise)
        ahead = jnp.concatenate([jnp.eye(width, dtype=F32), jnp.zeros((width, depth), F32)], 0)
        for bit in range(stages - 1):
            if bit:
                got = swap(section, "seq", bit)
            is_low = (place >> bit) % 2 == 0
            upper = jnp.where(is_low, got, section)
            lower = jnp.where(is_low, section, got)
            ahead_low = jnp.concatenate(
                [dot(ahead[:width], got[:width]), dot(ahead[:width], got[width:]) + ahead[width:]], 0
            )
            ahead = jnp.where(is_low, ahead_low, ahead)
            section = jnp.concatenate(
                [dot(lower[:width], upper[:width]), dot(lower[:width], upper[width:]) + lower[width:]], 0
            )
        total = section[width:]
    arrived = swap(total, "seq", stages - 1)

    head_flags = jnp.stack([1 - parity, 1 - (place >> (stages - 1)) % 2]).astype(jnp.int32)
    u, u_t, y, psi, psi_t, w, sym, dq, dk, start_t = call(
        local_kernel,
        [(length, depth), (depth, length), (length, depth), (length, width), (width, length), (length, depth),
         (length, length), (width, length), (width, length), (width, depth)],
        q_t, k_t, other, values, output_grad, start, inv, low, score, rows, head_flags, total, smem=(10,),
    )
    send, keep, value_grad, rate_grad = call(
        far_kernel,
        [(width, length), (width, length), (length, depth), (1, length)],
        head_flags, arrived, ahead, k_t, other, u, u_t, y, psi, psi_t, w, sym, dq, dk, start_t, rows, smem=(0,),
    )
    query_grad, key_grad = call(add_kernel, [(half, length), (half, length)], keep, swap(send, "head", 0))
    return (query_grad.T, key_grad.T, value_grad, rate_grad)


def solution(mesh):
    in_specs = (
        P("seq", "head"),
        P("seq", "head"),
        P("seq", "head"),
        P("head", "seq"),
        P("head", "seq"),
        P("seq", "head", None, None),
        P("seq", "head"),
    )
    out_specs = (P("seq", "head"), P("seq", "head"), P("seq", "head"), P("head", "seq"))
    return jax.shard_map(
        per_device, mesh=mesh, in_specs=in_specs, out_specs=out_specs, check_vma=False
    )
```

```python
import jax
import jax.numpy as jnp
from jax import lax
from jax.experimental import pallas as pl
from jax.experimental.pallas import tpu as pltpu
from jax.sharding import PartitionSpec as P

F32 = jnp.float32
BF16 = jnp.bfloat16
BASE = 16
NN = (((1,), (0,)), ((), ()))
NT = (((1,), (1,)), ((), ()))


def split(x):
    high = x.astype(BF16)
    return (high, (x - high.astype(F32)).astype(BF16))


def mm(left, right, dims=NN):
    left = left if isinstance(left, tuple) else (left if left.dtype == BF16 else split(left))
    right = right if isinstance(right, tuple) else (right if right.dtype == BF16 else split(right))

    def one(a, b):
        return lax.dot_general(a, b, dims, preferred_element_type=F32)

    if isinstance(left, tuple) and isinstance(right, tuple):
        return one(left[0], right[0]) + (one(left[0], right[1]) + one(left[1], right[0]))
    if isinstance(left, tuple):
        return one(left[0], right) + one(left[1], right)
    if isinstance(right, tuple):
        return one(left, right[0]) + one(left, right[1])
    return one(left, right)


def ids(shape):
    return lax.broadcasted_iota(jnp.int32, shape, 0), lax.broadcasted_iota(jnp.int32, shape, 1)


def to_col(row, eye):
    return jnp.sum(jnp.where(eye, row, 0.0), 1, keepdims=True)


def to_row(col, eye):
    return jnp.sum(jnp.where(eye, col, 0.0), 0, keepdims=True)


def base_inverse(nil, base):
    size = nil.shape[0]
    count = size // base
    row, lane = ids((base, size))
    block = lane // base
    packed = jnp.zeros((base, size), F32)
    for b in range(count):
        packed = jnp.where(block == b, nil[b * base : (b + 1) * base, :], packed)
    solved = jnp.where(row == lane % base, 1.0, 0.0)
    for j in range(base - 1):
        factor = jnp.take_along_axis(packed, block * base + j, axis=1)
        factor = jnp.where(row > j, factor, 0.0)
        solved = solved + factor * solved[j : j + 1, :]
    return jnp.concatenate([jnp.where(block == b, solved, 0.0) for b in range(count)], 0)


def half_inverse(nil):
    size = nil.shape[0]
    row, lane = ids((size, size))
    inv = base_inverse(nil, BASE)
    width = BASE
    while width < size:
        factor = 4 if size >= 4 * width else 2
        wide = width * factor
        off = jnp.where((row // wide == lane // wide) & (row // width != lane // width), nil, 0.0)
        inv_s = split(inv)
        step = split(mm(inv_s, off))
        first = inv + mm(step, inv_s)
        if factor == 4:
            first = first + mm(mm(step, step), first)
        inv = first
        width = wide
    return inv


def inverse(nil):
    size = nil.shape[0]
    half = size // 2
    upper = half_inverse(nil[:half, :half])
    lower = half_inverse(nil[half:, half:])
    corner = mm(mm(lower, nil[half:, :half]), upper)
    top = jnp.concatenate([upper, jnp.zeros((half, half), F32)], 1)
    return jnp.concatenate([top, jnp.concatenate([corner, lower], 1)], 0)


def decays(decay_row, row, lane):
    cum_col = jnp.sum(jnp.where(lane <= row, decay_row, 0.0), 1, keepdims=True)
    return cum_col, to_row(cum_col, row == lane)


def prep_kernel(
    flag_ref, q_ref, k_ref, decay_ref, rate_ref, spread_ref, damp_ref, kk_ref, qk_ref, rows_ref, mask_ref,
):
    length = q_ref.shape[1]
    row, lane = ids((length, length))
    cum_col, cum_row = decays(decay_ref[...], row, lane)
    rate_row = rate_ref[...]
    spread = jnp.exp(jnp.where(lane <= row, cum_col - cum_row, -1e30))
    spread_ref[...] = spread
    damp_ref[...] = jnp.where(lane < row, spread, 0.0) * -to_col(rate_row, row == lane)
    k_f, q_f = k_ref[...].astype(F32), q_ref[...].astype(F32)
    kk_ref[...] = mm(k_f.T.astype(BF16), k_ref[...])
    qk_ref[...] = mm(q_f.T.astype(BF16), k_ref[...])
    grow = jnp.exp(cum_row)
    tail = jnp.exp(cum_row[:, length - 1 :] - cum_row)
    k_sum = jnp.sum(k_f * k_f, 0, keepdims=True)
    q_sum = jnp.sum(q_f * q_f, 0, keepdims=True)
    rows_ref[...] = jnp.concatenate([cum_row, grow, tail, rate_row, k_sum, q_sum, cum_row, cum_row], 0)
    mask_ref[...] = jnp.concatenate([jnp.full((1, mask_ref.shape[1]), flag_ref[i], F32) for i in range(8)], 0)


def inverse_kernel(k_ref, other_ref, kk_in_ref, damp_ref, rows_ref, inv_ref, w_ref, map_ref, kk_ref, scale_ref):
    other = other_ref[...]
    other_f = other.astype(F32)
    k_t = jnp.concatenate([k_ref[...], other], 0)
    width, length = k_t.shape
    grow, tail, rate_row, k_sum = (rows_ref[i : i + 1, :] for i in range(1, 5))
    square = k_sum + jnp.sum(other_f * other_f, 0, keepdims=True) + 1e-6
    k_scale = 1.0 / jnp.sqrt(square)
    kk = kk_in_ref[...] + mm(other_f.T.astype(BF16), other)
    inv = inverse(damp_ref[...] * (kk * (k_scale * k_scale)))
    w_t = mm(k_t, inv * (rate_row * grow), NT) * k_scale
    w_row, w_lane = ids((width, width))
    map_ref[...] = jnp.where(w_row == w_lane, grow[:, length - 1 :], 0.0) - mm(w_t * (tail * k_scale), k_t, NT)
    inv_ref[...] = inv
    w_ref[...] = w_t
    kk_ref[...] = kk
    scale_ref[...] = jnp.concatenate([k_scale, square * k_scale], 0)


def shift_kernel(
    q_ref, other_ref, k_other_ref, g_ref, qk_ref, spread_ref, rows_ref, scale_ref, w_ref, shift_ref, score_ref, q_scale_ref
):
    other = other_ref[...]
    other_f = other.astype(F32)
    q_f = jnp.concatenate([q_ref[...].astype(F32), other_f], 0)
    width = q_f.shape[0]
    q_sum = rows_ref[5:6, :] + jnp.sum(other_f * other_f, 0, keepdims=True)
    q_scale = width ** (-0.5) / jnp.sqrt(q_sum + 1e-6)
    score = spread_ref[...] * (qk_ref[...] + mm(other_f.T.astype(BF16), k_other_ref[...]))
    side = q_scale * (q_f * rows_ref[1:2, :] - mm(w_ref[...] * scale_ref[0:1, :], score, NT))
    shift_ref[...] = mm(side, g_ref[...])
    score_ref[...] = score
    q_scale_ref[...] = q_scale


def join_kernel(mask_ref, own_map_ref, own_ref, got_map_ref, got_ref, total_ref):
    low = mask_ref[0:1, :] > 0.0
    own, got = own_ref[...], got_ref[...]
    first = jnp.where(low, own_map_ref[...], got_map_ref[...])
    total_ref[...] = mm(first, jnp.where(low, got, own)) + jnp.where(low, own, got)


def update_kernel(
    mask_ref, q_ref, q_other_ref, k_ref, k_other_ref, v_ref, g_ref, start_ref, inv_ref, spread_ref, rows_ref, scale_ref,
    q_scale_ref, u_ref, base_ref, score_grad_ref, start_t_ref, keep_ref, send_ref,
):
    half, length = q_ref.shape
    q_f = jnp.concatenate([q_ref[...], q_other_ref[...]], 0).astype(F32)
    k_t = jnp.concatenate([k_ref[...], k_other_ref[...]], 0)
    width = k_t.shape[0]
    row, lane = ids((length, length))
    eye = row == lane
    grow, rate_row = rows_ref[1:2, :], rows_ref[3:4, :]
    k_scale, k_norm = scale_ref[0:1, :], scale_ref[1:2, :]
    start = start_ref[...]
    start = jnp.where(mask_ref[2:3, :] > 0.0, start, pltpu.roll(start, half, 1))
    start_t = start.T
    grad = g_ref[...]
    grad_t = grad.astype(F32).T.astype(BF16)
    k_rows = k_t.astype(F32).T.astype(BF16)
    base = v_ref[...].astype(F32) - to_col(grow * k_scale, eye) * mm(k_rows, start, NT)
    u = to_col(k_scale, eye) * mm(inv_ref[...], to_col(k_norm * rate_row, eye) * base)
    score_grad = mm(grad, u, NT) * spread_ref[...]
    q_scale = q_scale_ref[...]
    dq = mm(k_t, score_grad * k_scale, NT) + grow * mm(start_t, grad_t)
    unit = q_f * (q_scale * width**0.5)
    dq = q_scale * (dq - unit * jnp.sum(unit * dq, 0, keepdims=True))
    keep_ref[...] = dq[0:half, :]
    send_ref[...] = dq[half:, :]
    u_ref[...] = u
    base_ref[...] = base
    score_grad_ref[...] = score_grad
    start_t_ref[...] = start_t


def local_kernel(
    q_ref, q_other_ref, k_ref, k_other_ref, g_ref, start_t_ref, inv_ref, score_ref, damp_ref, rows_ref, scale_ref,
    q_scale_ref, u_ref, score_grad_ref, after_ref,
    uh_ref, ul_ref, uth_ref, utl_ref, ph_ref, pl_ref, pth_ref, ptl_ref, gh_ref, gl_ref, kh_ref, kl_ref, y_ref, sym_ref, dk_ref,
):
    length = q_ref.shape[1]
    q_f = jnp.concatenate([q_ref[...], q_other_ref[...]], 0).astype(F32)
    k_t = jnp.concatenate([k_ref[...], k_other_ref[...]], 0)
    row, lane = ids((length, length))
    eye = row == lane
    grow, tail, rate_row = (rows_ref[i : i + 1, :] for i in range(1, 4))
    k_scale, k_norm = scale_ref[0:1, :], scale_ref[1:2, :]
    q_scale = q_scale_ref[...]
    grad_t = g_ref[...].astype(F32).T.astype(BF16)
    inv = inv_ref[...]
    u = u_ref[...]
    u_t = u.T
    u_s, u_ts = split(u), split(u_t)
    score = score_ref[...] * (to_col(q_scale, eye) * k_scale)
    y_t = mm(mm(grad_t, score) * k_scale, inv) * k_norm
    psi_t = mm(k_t, inv * to_col(tail * k_scale * k_scale, eye)) * k_norm
    y = y_t.T
    damp = damp_ref[...]
    sym_decay = damp + damp.T
    sym = sym_decay * jnp.where(lane < row, mm(y, u_ts), mm(u_s, y_t))
    k_s = split(k_t.astype(F32) * k_scale)
    dk_ref[...] = (
        mm(k_s, sym) + mm(q_f * q_scale, score_grad_ref[...]) - mm(start_t_ref[...], y_t * (grow * rate_row))
    )
    uh_ref[...], ul_ref[...] = u_s
    uth_ref[...], utl_ref[...] = u_ts
    ph_ref[...], pl_ref[...] = split(psi_t.T)
    pth_ref[...], ptl_ref[...] = split(psi_t)
    gh_ref[...], gl_ref[...] = split(psi_t * (grow * rate_row))
    kh_ref[...], kl_ref[...] = k_s
    y_ref[...] = y
    sym_ref[...] = sym_decay


def far_kernel(
    mask_ref, got_ref, ahead_map_ref, ahead_ref, k_ref, k_other_ref, uh_ref, ul_ref, uth_ref, utl_ref, ph_ref, pl_ref,
    pth_ref, ptl_ref, gh_ref, gl_ref, kh_ref, kl_ref, sym_ref, dk_ref, start_t_ref, rows_ref, scale_ref,
    send_ref, keep_ref, far_ref,
):
    half, length = k_ref.shape
    k_f = jnp.concatenate([k_ref[...], k_other_ref[...]], 0).astype(F32)
    width = k_f.shape[0]
    row, lane = ids((length, length))
    k_scale = scale_ref[0:1, :]
    w_row, w_lane = ids((width, got_ref.shape[1]))
    low = mask_ref[0:1, :] > 0.0
    got = jnp.where(mask_ref[1:2, :] > 0.0, got_ref[...], 0.0)
    ahead_map = jnp.where(low, ahead_map_ref[...], jnp.where(w_row == w_lane, 1.0, 0.0))
    far = mm(ahead_map, got) + jnp.where(low, ahead_ref[...], 0.0)
    far_s = split(far)
    far_ref[...] = far
    uz_t = mm(far_s, (uth_ref[...], utl_ref[...]))
    uz = mm((uh_ref[...], ul_ref[...]), far_s, NT)
    sz = mm(start_t_ref[...], far_s, NT)
    sym = sym_ref[...] * jnp.where(
        lane < row, mm((ph_ref[...], pl_ref[...]), uz_t), mm(uz, (pth_ref[...], ptl_ref[...]))
    )
    dk = dk_ref[...] + rows_ref[2:3, :] * uz_t - mm(sz, (gh_ref[...], gl_ref[...]))
    dk = dk + mm((kh_ref[...], kl_ref[...]), sym)
    unit = k_f * k_scale
    dk = k_scale * (dk - unit * jnp.sum(unit * dk, 0, keepdims=True))
    keep_ref[...] = dk[0:half, :]
    send_ref[...] = dk[half:, :]


def value_kernel(
    far_ref, ph_ref, pl_ref, y_ref, base_ref, kk_ref, spread_ref, scale_ref, rows_ref, uh_ref, ul_ref, keep_ref, got_ref,
    value_ref, rate_out_ref, q_ref,
):
    length = y_ref.shape[0]
    row, lane = ids((length, length))
    eye = row == lane
    k_scale = scale_ref[0:1, :]
    y = y_ref[...] + mm((ph_ref[...], pl_ref[...]), far_ref[...])
    value_ref[...] = to_col(rows_ref[3:4, :], eye) * y
    low = jnp.where(lane < row, spread_ref[...] * kk_ref[...], 0.0) * (to_col(k_scale, eye) * k_scale)
    write = base_ref[...] - mm(low, (uh_ref[...], ul_ref[...]))
    rate_out_ref[...] = to_row(jnp.sum(y * write, 1, keepdims=True), eye)
    q_ref[...] = keep_ref[...] + got_ref[...]


def add_kernel(keep_ref, got_ref, k_ref):
    k_ref[...] = keep_ref[...] + got_ref[...]


def call(kernel, outs, *args, smem=(), cost=1.0):
    shapes = [out if isinstance(out[0], tuple) else (out, F32) for out in outs]
    return pl.pallas_call(
        kernel,
        out_shape=tuple(jax.ShapeDtypeStruct(shape, kind) for shape, kind in shapes),
        in_specs=[
            pl.BlockSpec(memory_space=pltpu.SMEM if i in smem else pltpu.VMEM) for i in range(len(args))
        ],
        out_specs=tuple(pl.BlockSpec(memory_space=pltpu.VMEM) for _ in outs),
        cost_estimate=pl.CostEstimate(flops=int(cost * 1e9), bytes_accessed=1 << 20, transcendentals=0),
        compiler_params=pltpu.CompilerParams(vmem_limit_bytes=24 << 20),
    )(*args)


def swap(x, axis, apart):
    return lax.ppermute(x, axis, [(i, i ^ 1 << apart) for i in range(lax.axis_size(axis))])


def far_scan(section, count, place):
    def dot(left, right):
        return jnp.dot(left, right, precision=lax.Precision.HIGHEST)

    own_map, own = section
    ahead_map, ahead = jnp.eye(own_map.shape[0], dtype=F32), jnp.zeros_like(own)
    for bit in range(count.bit_length() - 2):
        got_map, got = swap(own_map, "seq", bit), swap(own, "seq", bit)
        low = (place >> bit) % 2 == 0
        ahead = jnp.where(low, dot(ahead_map, got) + ahead, ahead)
        ahead_map = jnp.where(low, dot(ahead_map, got_map), ahead_map)
        low_map, high_map = jnp.where(low, own_map, got_map), jnp.where(low, got_map, own_map)
        own = dot(low_map, jnp.where(low, got, own)) + jnp.where(low, own, got)
        own_map = dot(low_map, high_map)
    return own, ahead_map, ahead


def per_device(queries, key_rows, values, log_decay, beta_rate, start_states, output_grad):
    count = lax.axis_size("seq")
    stages = count.bit_length() - 1
    assert count == 1 << stages and stages >= 2
    place = lax.axis_index("seq")
    parity = lax.axis_index("head") % 2
    q_t, k_t = queries.T, key_rows.T
    half, length = q_t.shape
    width = 2 * half
    depth = values.shape[1]
    start = start_states[0, 0]
    square, tall, wide, thin = (length, length), (length, depth), (width, length), (1, length)
    k_other = swap(k_t, "head", 0)
    q_other = swap(q_t, "head", 0)
    low_first = 1 - place % 2 if stages == 2 else place * 0 + 1
    low_last = 1 - (place >> (stages - 1)) % 2
    flags = jnp.stack([low_first, low_last, 1 - parity] + [parity] * 5).astype(F32)
    spread, damp, kk_own, qk_own, rows, mask = call(
        prep_kernel, [square, square, square, square, (8, length), (8, depth)],
        flags, q_t, k_t, log_decay, beta_rate, smem=(0,),
    )
    inv, w_t, own_map, kk, scale = call(
        inverse_kernel, [square, wide, (width, width), square, (2, length)], k_t, k_other, kk_own, damp, rows
    )
    if stages == 2:
        got_map = swap(own_map, "seq", 0)
    own, score, q_scale = call(
        shift_kernel, [(width, depth), square, thin],
        q_t, q_other, k_other, output_grad, qk_own, spread, rows, scale, w_t,
    )
    if stages == 2:
        got = swap(own, "seq", 0)
        (total,) = call(join_kernel, [(width, depth)], mask, own_map, own, got_map, got)
        ahead_map, ahead = got_map, got
    else:
        total, ahead_map, ahead = far_scan((own_map, own), count, place)
    arrived = swap(total, "seq", stages - 1)
    u, base, score_grad, start_t, keep_q, send_q = call(
        update_kernel, [tall, tall, square, (width, depth), (half, length), (half, length)],
        mask, q_t, q_other, k_t, k_other, values, output_grad, start, inv, spread, rows, scale, q_scale,
    )
    got_q = swap(send_q, "head", 0)
    pairs = [(tall, BF16)] * 2 + [((depth, length), BF16)] * 2 + [((length, width), BF16)] * 2 + [(wide, BF16)] * 6
    *packs, y, sym, dk = call(
        local_kernel, pairs + [tall, square, wide],
        q_t, q_other, k_t, k_other, output_grad, start_t, inv, score, damp, rows, scale, q_scale, u, score_grad, total,
    )
    send, keep, far = call(
        far_kernel, [(half, length), (half, length), (width, depth)],
        mask, arrived, ahead_map, ahead, k_t, k_other, *packs, sym, dk, start_t, rows, scale,
    )
    got_k = swap(send, "head", 0)
    value_grad, rate_grad, query_grad = call(
        value_kernel, [tall, thin, (half, length)],
        far, packs[4], packs[5], y, base, kk, spread, scale, rows, packs[0], packs[1], keep_q, got_q,
    )
    (key_grad,) = call(add_kernel, [(half, length)], keep, got_k)
    return (query_grad.T, key_grad.T, value_grad, rate_grad)


def solution(mesh):
    in_specs = (
        P("seq", "head"),
        P("seq", "head"),
        P("seq", "head"),
        P("head", "seq"),
        P("head", "seq"),
        P("seq", "head", None, None),
        P("seq", "head"),
    )
    out_specs = (P("seq", "head"), P("seq", "head"), P("seq", "head"), P("head", "seq"))

    return jax.shard_map(per_device, mesh=mesh, in_specs=in_specs, out_specs=out_specs, check_vma=False)
```

```python
import jax
import jax.numpy as jnp
from jax import lax
from jax.experimental import pallas as pl
from jax.experimental.pallas import tpu as pltpu
from jax.sharding import PartitionSpec as P

F32 = jnp.float32
BF16 = jnp.bfloat16
BASE = 32
NN = (((1,), (0,)), ((), ()))
NT = (((1,), (1,)), ((), ()))


def split(x):
    high = x.astype(BF16)
    return (high, (x - high.astype(F32)).astype(BF16))


def mm(left, right, dims=NN):
    left = left if isinstance(left, tuple) else (left if left.dtype == BF16 else split(left))
    right = right if isinstance(right, tuple) else (right if right.dtype == BF16 else split(right))

    def one(a, b):
        return lax.dot_general(a, b, dims, preferred_element_type=F32)

    if isinstance(left, tuple) and isinstance(right, tuple):
        return one(left[0], right[0]) + (one(left[0], right[1]) + one(left[1], right[0]))
    if isinstance(left, tuple):
        return one(left[0], right) + one(left[1], right)
    if isinstance(right, tuple):
        return one(left, right[0]) + one(left, right[1])
    return one(left, right)


def ids(shape):
    return lax.broadcasted_iota(jnp.int32, shape, 0), lax.broadcasted_iota(jnp.int32, shape, 1)


def to_col(row, eye):
    return jnp.sum(jnp.where(eye, row, 0.0), 1, keepdims=True)


def to_row(col, eye):
    return jnp.sum(jnp.where(eye, col, 0.0), 0, keepdims=True)


def base_inverse(nil, base):
    size = nil.shape[0]
    count = size // base
    _, lane = ids((base, size))
    block = lane // base
    packed = jnp.zeros((base, size), F32)
    for b in range(count):
        packed = jnp.where(block == b, nil[b * base : (b + 1) * base, :], packed)
    row, lane = ids((8, size))
    first = lane // base * base
    tiles = range(base // 8)
    parts = [packed[8 * t : 8 * t + 8, :] for t in tiles]
    solved = [jnp.where(row + 8 * t == lane - first, 1.0, 0.0) for t in tiles]
    for j in range(base - 1):
        source = solved[j // 8][j % 8 : j % 8 + 1, :]
        for t in tiles[(j + 1) // 8 :]:
            factor = jnp.take_along_axis(parts[t], first + j, axis=1)
            if t == j // 8:
                factor = jnp.where(row + 8 * t > j, factor, 0.0)
            solved[t] = solved[t] + factor * source
    solved = jnp.concatenate(solved, 0)
    return jnp.concatenate([jnp.where(block == b, solved, 0.0) for b in range(count)], 0)


def inverses(nils):
    size = nils[0].shape[0]
    row, lane = ids((size, size))
    found = [base_inverse(nil, BASE) for nil in nils]
    width = BASE
    while width < size:
        factor = 4 if size >= 4 * width else 2
        wide = width * factor
        off = (row // wide == lane // wide) & (row // width != lane // width)
        known = [split(inv) for inv in found]
        steps = [split(mm(inv, jnp.where(off, nil, 0.0))) for inv, nil in zip(known, nils)]
        found = [inv + mm(step, pair) for inv, step, pair in zip(found, steps, known)]
        if factor == 4:
            steps = [mm(step, step) for step in steps]
            found = [inv + mm(step, inv) for inv, step in zip(found, steps)]
        width = wide
    return found


def inverse(nil):
    half = nil.shape[0] // 2
    upper, lower = inverses([nil[:half, :half], nil[half:, half:]])
    corner = mm(mm(lower, nil[half:, :half]), upper)
    top = jnp.concatenate([upper, jnp.zeros((half, half), F32)], 1)
    return jnp.concatenate([top, jnp.concatenate([corner, lower], 1)], 0)


def decays(decay_row, row, lane):
    cum_col = jnp.sum(jnp.where(lane <= row, decay_row, 0.0), 1, keepdims=True)
    return cum_col, to_row(cum_col, row == lane)


def prep_kernel(
    flag_ref, q_ref, k_ref, decay_ref, rate_ref, spread_ref, damp_ref, kk_ref, qk_ref, rows_ref, mask_ref,
):
    length = q_ref.shape[1]
    row, lane = ids((length, length))
    cum_col, cum_row = decays(decay_ref[...], row, lane)
    rate_row = rate_ref[...]
    spread = jnp.exp(jnp.where(lane <= row, cum_col - cum_row, -1e30))
    spread_ref[...] = spread
    damp_ref[...] = jnp.where(lane < row, spread, 0.0) * -to_col(rate_row, row == lane)
    k_f, q_f = k_ref[...].astype(F32), q_ref[...].astype(F32)
    kk_ref[...] = mm(k_f.T.astype(BF16), k_ref[...])
    qk_ref[...] = mm(q_f.T.astype(BF16), k_ref[...])
    grow = jnp.exp(cum_row)
    tail = jnp.exp(cum_row[:, length - 1 :] - cum_row)
    k_sum = jnp.sum(k_f * k_f, 0, keepdims=True)
    q_sum = jnp.sum(q_f * q_f, 0, keepdims=True)
    rows_ref[...] = jnp.concatenate([cum_row, grow, tail, rate_row, k_sum, q_sum, cum_row, cum_row], 0)
    mask_ref[...] = jnp.concatenate([jnp.full((1, mask_ref.shape[1]), flag_ref[i], F32) for i in range(8)], 0)


def inverse_kernel(k_ref, other_ref, kk_in_ref, damp_ref, rows_ref, inv_ref, w_ref, kk_ref, scale_ref):
    other = other_ref[...]
    other_f = other.astype(F32)
    k_t = jnp.concatenate([k_ref[...], other], 0)
    grow, rate_row, k_sum = (rows_ref[i : i + 1, :] for i in (1, 3, 4))
    square = k_sum + jnp.sum(other_f * other_f, 0, keepdims=True) + 1e-6
    k_scale = 1.0 / jnp.sqrt(square)
    kk = kk_in_ref[...] + mm(other_f.T.astype(BF16), other)
    inv = inverse(damp_ref[...] * (kk * (k_scale * k_scale)))
    w_ref[...] = mm(k_t, inv * (rate_row * grow), NT) * k_scale
    inv_ref[...] = inv
    kk_ref[...] = kk
    scale_ref[...] = jnp.concatenate([k_scale, square * k_scale], 0)


def shift_kernel(
    q_ref, other_ref, k_ref, k_other_ref, g_ref, qk_ref, spread_ref, rows_ref, scale_ref, w_ref,
    map_ref, score_ref, q_scale_ref,
):
    other = other_ref[...]
    other_f = other.astype(F32)
    k_t = jnp.concatenate([k_ref[...], k_other_ref[...]], 0)
    q_f = jnp.concatenate([q_ref[...].astype(F32), other_f], 0)
    width, length = k_t.shape
    k_scale, grow, tail = scale_ref[0:1, :], rows_ref[1:2, :], rows_ref[2:3, :]
    score = spread_ref[...] * (qk_ref[...] + mm(other_f.T.astype(BF16), k_other_ref[...]))
    q_sum = rows_ref[5:6, :] + jnp.sum(other_f * other_f, 0, keepdims=True)
    q_scale = width ** (-0.5) / jnp.sqrt(q_sum + 1e-6)
    w_t = w_ref[...] * k_scale
    w_row, w_lane = ids((width, width))
    own_map = jnp.where(w_row == w_lane, grow[:, length - 1 :], 0.0) - mm(w_t * tail, k_t, NT)
    side = q_scale * (q_f * grow - mm(w_t, score, NT))
    map_ref[0:width, :] = own_map
    score_ref[...] = score
    q_scale_ref[...] = q_scale
    map_ref[width:, :] = mm(side, g_ref[...])


def join_kernel(mask_ref, own_ref, got_ref, total_ref):
    width = own_ref.shape[1]
    low = mask_ref[0:1, :] > 0.0
    own, got = own_ref[width:, :], got_ref[width:, :]
    first = jnp.where(low, own_ref[0:width, :], got_ref[0:width, :])
    total_ref[...] = mm(first, jnp.where(low, got, own)) + jnp.where(low, own, got)


def update_kernel(
    mask_ref, q_ref, q_other_ref, k_ref, k_other_ref, v_ref, g_ref, start_ref, inv_ref, spread_ref, rows_ref, scale_ref,
    q_scale_ref, u_ref, base_ref, score_grad_ref, start_t_ref, keep_ref, send_ref,
):
    half, length = q_ref.shape
    q_f = jnp.concatenate([q_ref[...], q_other_ref[...]], 0).astype(F32)
    k_t = jnp.concatenate([k_ref[...], k_other_ref[...]], 0)
    width = k_t.shape[0]
    row, lane = ids((length, length))
    eye = row == lane
    grow, rate_row = rows_ref[1:2, :], rows_ref[3:4, :]
    k_scale, k_norm = scale_ref[0:1, :], scale_ref[1:2, :]
    start = start_ref[...]
    start = jnp.where(mask_ref[2:3, :] > 0.0, start, pltpu.roll(start, half, 1))
    start_t = start.T
    grad = g_ref[...]
    grad_t = grad.astype(F32).T.astype(BF16)
    k_rows = k_t.astype(F32).T.astype(BF16)
    base = v_ref[...].astype(F32) - to_col(grow * k_scale, eye) * mm(k_rows, start, NT)
    u = to_col(k_scale, eye) * mm(inv_ref[...], to_col(k_norm * rate_row, eye) * base)
    score_grad = mm(grad, u, NT) * spread_ref[...]
    q_scale = q_scale_ref[...]
    dq = mm(k_t, score_grad * k_scale, NT) + grow * mm(start_t, grad_t)
    unit = q_f * (q_scale * width**0.5)
    dq = q_scale * (dq - unit * jnp.sum(unit * dq, 0, keepdims=True))
    keep_ref[...] = dq[0:half, :]
    send_ref[...] = dq[half:, :]
    u_ref[...] = u
    base_ref[...] = base
    score_grad_ref[...] = score_grad
    start_t_ref[...] = start_t


def local_kernel(
    mask_ref, q_ref, q_other_ref, k_ref, k_other_ref, g_ref, start_t_ref, inv_ref, score_ref, damp_ref, rows_ref, scale_ref,
    q_scale_ref, u_ref, score_grad_ref, ahead_ref, after_ref,
    uth_ref, utl_ref, ph_ref, pl_ref, gh_ref, gl_ref, kh_ref, kl_ref, sh_ref, sl_ref, ah_ref, al_ref, y_ref, dk_ref,
):
    length = q_ref.shape[1]
    q_f = jnp.concatenate([q_ref[...], q_other_ref[...]], 0).astype(F32)
    k_t = jnp.concatenate([k_ref[...], k_other_ref[...]], 0)
    width = k_t.shape[0]
    eye = jnp.equal(*ids((length, length)))
    grow, tail, rate_row = (rows_ref[i : i + 1, :] for i in range(1, 4))
    k_scale, k_norm = scale_ref[0:1, :], scale_ref[1:2, :]
    low = mask_ref[0:1, :] > 0.0
    ahead_map = jnp.where(low, ahead_ref[0:width, :], jnp.where(jnp.equal(*ids((width, width))), 1.0, 0.0))
    ahead = jnp.where(low, ahead_ref[width:, :], 0.0)
    grad_t = g_ref[...].astype(F32).T.astype(BF16)
    score = score_ref[...] * to_col(q_scale_ref[...], eye)
    u_ts = split(u_ref[...].T)
    inv = inv_ref[...]
    psi_t = mm(k_t, inv * to_col(tail * k_scale * k_scale, eye)) * k_norm
    du_t = mm(grad_t, score) * (k_scale * k_scale)
    psi_s = split(psi_t.T)
    y_t = mm(du_t, inv) * k_norm
    y_t = y_t + mm(ahead.T, psi_t)
    map_s = split(ahead_map)
    psi_far = mm(psi_s, map_s)
    uz_t = mm(ahead, u_ts)
    y = y_t.T
    y_ref[...] = y
    start_s = split(start_t_ref[...])
    inner = damp_ref[...] * mm(y, u_ts)
    k_s = split(k_t.astype(F32) * k_scale)
    dk = mm(q_f * q_scale_ref[...], score_grad_ref[...]) - mm(start_s, y_t * (grow * rate_row)) + tail * uz_t
    ph_ref[...], pl_ref[...] = split(psi_far)
    gh_ref[...], gl_ref[...] = split(psi_far.T * (grow * rate_row))
    inner_s = split(inner)
    dk_ref[...] = dk + (mm(k_s, inner_s) + mm(k_s, inner_s, NT))
    uth_ref[...], utl_ref[...] = u_ts
    kh_ref[...], kl_ref[...] = k_s
    sh_ref[...], sl_ref[...] = start_s
    ah_ref[...], al_ref[...] = map_s


def far_kernel(
    mask_ref, got_ref, k_ref, k_other_ref, damp_ref, rows_ref, scale_ref,
    uth_ref, utl_ref, ph_ref, pl_ref, gh_ref, gl_ref, kh_ref, kl_ref, sh_ref, sl_ref, ah_ref, al_ref, dk_ref,
    send_ref, keep_ref,
):
    half = k_ref.shape[0]
    k_scale = scale_ref[0:1, :]
    got_s = split(jnp.where(mask_ref[1:2, :] > 0.0, got_ref[...], 0.0))
    gu_s = split(mm(got_s, (uth_ref[...], utl_ref[...])))
    sg_s = split(mm((sh_ref[...], sl_ref[...]), got_s, NT))
    inner_s = split(damp_ref[...] * mm((ph_ref[...], pl_ref[...]), gu_s))
    dk = dk_ref[...] + rows_ref[2:3, :] * mm((ah_ref[...], al_ref[...]), gu_s) - mm(sg_s, (gh_ref[...], gl_ref[...]))
    k_s = (kh_ref[...], kl_ref[...])
    dk = dk + (mm(k_s, inner_s) + mm(k_s, inner_s, NT))
    unit = jnp.concatenate([k_ref[...], k_other_ref[...]], 0).astype(F32) * k_scale
    dk = k_scale * (dk - unit * jnp.sum(unit * dk, 0, keepdims=True))
    send_ref[...] = dk[half:, :]
    keep_ref[...] = dk[0:half, :]


def value_kernel(
    mask_ref, got_ref, ph_ref, pl_ref, y_ref, base_ref, kk_ref, spread_ref, scale_ref, rows_ref, u_ref, keep_ref, got_q_ref,
    value_ref, rate_out_ref, q_ref,
):
    length = y_ref.shape[0]
    row, lane = ids((length, length))
    eye = row == lane
    k_scale = scale_ref[0:1, :]
    got = jnp.where(mask_ref[1:2, :] > 0.0, got_ref[...], 0.0)
    low = jnp.where(lane < row, spread_ref[...] * kk_ref[...], 0.0) * (to_col(k_scale, eye) * k_scale)
    y = y_ref[...] + mm((ph_ref[...], pl_ref[...]), got)
    write = base_ref[...] - mm(low, u_ref[...])
    value_ref[...] = to_col(rows_ref[3:4, :], eye) * y
    rate_out_ref[...] = to_row(jnp.sum(y * write, 1, keepdims=True), eye)
    q_ref[...] = keep_ref[...] + got_q_ref[...]


def add_kernel(keep_ref, got_ref, k_ref):
    k_ref[...] = keep_ref[...] + got_ref[...]


def call(kernel, outs, *args, smem=(), cost=1.0):
    shapes = [out if isinstance(out[0], tuple) else (out, F32) for out in outs]
    return pl.pallas_call(
        kernel,
        out_shape=tuple(jax.ShapeDtypeStruct(shape, kind) for shape, kind in shapes),
        in_specs=[
            pl.BlockSpec(memory_space=pltpu.SMEM if i in smem else pltpu.VMEM) for i in range(len(args))
        ],
        out_specs=tuple(pl.BlockSpec(memory_space=pltpu.VMEM) for _ in outs),
        cost_estimate=pl.CostEstimate(flops=int(cost * 1e9), bytes_accessed=1 << 20, transcendentals=0),
        compiler_params=pltpu.CompilerParams(vmem_limit_bytes=24 << 20),
    )(*args)


def swap(x, axis, apart):
    return lax.ppermute(x, axis, [(i, i ^ 1 << apart) for i in range(lax.axis_size(axis))])


def far_scan(section, count, place):
    def dot(left, right):
        return jnp.dot(left, right, precision=lax.Precision.HIGHEST)

    width = section.shape[1]
    own_map, own = section[:width], section[width:]
    ahead_map, ahead = jnp.eye(width, dtype=F32), jnp.zeros_like(own)
    for bit in range(count.bit_length() - 2):
        got = swap(jnp.concatenate([own_map, own], 0), "seq", bit)
        got_map, got = got[:width], got[width:]
        low = (place >> bit) % 2 == 0
        ahead = jnp.where(low, dot(ahead_map, got) + ahead, ahead)
        ahead_map = jnp.where(low, dot(ahead_map, got_map), ahead_map)
        low_map, high_map = jnp.where(low, own_map, got_map), jnp.where(low, got_map, own_map)
        own = dot(low_map, jnp.where(low, got, own)) + jnp.where(low, own, got)
        own_map = dot(low_map, high_map)
    return own, jnp.concatenate([ahead_map, ahead], 0)


def per_device(queries, key_rows, values, log_decay, beta_rate, start_states, output_grad):
    count = lax.axis_size("seq")
    stages = count.bit_length() - 1
    assert count == 1 << stages and stages >= 2
    place = lax.axis_index("seq")
    parity = lax.axis_index("head") % 2
    q_t, k_t = queries.T, key_rows.T
    half, length = q_t.shape
    width = 2 * half
    depth = values.shape[1]
    start = start_states[0, 0]
    square, tall, wide, thin = (length, length), (length, depth), (width, length), (1, length)
    k_other = swap(k_t, "head", 0)
    q_other = swap(q_t, "head", 0)
    low_first = 1 - place % 2 if stages == 2 else place * 0 + 1
    low_last = 1 - (place >> (stages - 1)) % 2
    flags = jnp.stack([low_first, low_last, 1 - parity] + [parity] * 5).astype(F32)
    spread, damp, kk_own, qk_own, rows, mask = call(
        prep_kernel, [square, square, square, square, (8, length), (8, depth)],
        flags, q_t, k_t, log_decay, beta_rate, smem=(0,),
    )
    inv, w_t, kk, scale = call(
        inverse_kernel, [square, wide, square, (2, length)], k_t, k_other, kk_own, damp, rows
    )
    section, score, q_scale = call(
        shift_kernel, [(2 * width, depth), square, thin],
        q_t, q_other, k_t, k_other, output_grad, qk_own, spread, rows, scale, w_t,
    )
    if stages == 2:
        ahead = swap(section, "seq", 0)
        (total,) = call(join_kernel, [(width, depth)], mask, section, ahead)
    else:
        total, ahead = far_scan(section, count, place)
    arrived = swap(total, "seq", stages - 1)
    u, base, score_grad, start_t, keep_q, send_q = call(
        update_kernel, [tall, tall, square, (width, depth), (half, length), (half, length)],
        mask, q_t, q_other, k_t, k_other, values, output_grad, start, inv, spread, rows, scale, q_scale,
    )
    got_q = swap(send_q, "head", 0)
    shapes = [(depth, length), (length, width), wide, wide, (width, depth), (width, width)]
    *packs, y, dk = call(
        local_kernel, [(shape, BF16) for shape in shapes for _ in range(2)] + [tall, wide],
        mask, q_t, q_other, k_t, k_other, output_grad, start_t, inv, score, damp, rows, scale, q_scale, u, score_grad, ahead,
        total,
    )
    send, keep = call(
        far_kernel, [(half, length), (half, length)],
        mask, arrived, k_t, k_other, damp, rows, scale, *packs, dk,
    )
    got_k = swap(send, "head", 0)
    value_grad, rate_grad, query_grad = call(
        value_kernel, [tall, thin, (half, length)],
        mask, arrived, packs[2], packs[3], y, base, kk, spread, scale, rows, u, keep_q, got_q,
    )
    (key_grad,) = call(add_kernel, [(half, length)], keep, got_k)
    return (query_grad.T, key_grad.T, value_grad, rate_grad)


def solution(mesh):
    in_specs = (
        P("seq", "head"),
        P("seq", "head"),
        P("seq", "head"),
        P("head", "seq"),
        P("head", "seq"),
        P("seq", "head", None, None),
        P("seq", "head"),
    )
    out_specs = (P("seq", "head"), P("seq", "head"), P("seq", "head"), P("head", "seq"))

    return jax.shard_map(per_device, mesh=mesh, in_specs=in_specs, out_specs=out_specs, check_vma=False)
```

```python
import jax
import jax.numpy as jnp
from jax import lax
from jax.experimental import pallas as pl
from jax.experimental.pallas import tpu as pltpu
from jax.sharding import PartitionSpec as P

F32 = jnp.float32
BF16 = jnp.bfloat16
BASE = 32
PACK = 128
NN = (((1,), (0,)), ((), ()))
NT = (((1,), (1,)), ((), ()))


def split(x):
    high = x.astype(BF16)
    return (high, (x - high.astype(F32)).astype(BF16))


def mm(left, right, dims=NN):
    left = left if isinstance(left, tuple) else (left if left.dtype == BF16 else split(left))
    right = right if isinstance(right, tuple) else (right if right.dtype == BF16 else split(right))
    deep, out = (0, 1) if dims is NN else (1, 0)

    def one(a, b):
        return lax.dot_general(a, b, dims, preferred_element_type=F32)

    def join(parts, axis):
        return jnp.concatenate(parts, axis)

    pair_left, pair_right = isinstance(left, tuple), isinstance(right, tuple)
    shape = (right[0] if pair_right else right).shape
    shallow, thin = shape[deep] == PACK, shape[out] == PACK
    if pair_left and pair_right:
        high, low = right
        if shallow and thin:
            block = join([join([high, low], out), join([high, jnp.zeros_like(low)], out)], deep)
            both = one(join(left, 1), block)
            return both[:, :PACK] + both[:, PACK:]
        if shallow:
            return one(join(left, 1), join([high, high], deep)) + one(left[0], low)
        if thin:
            both = one(left[0], join(right, out))
            return both[:, :PACK] + both[:, PACK:] + one(left[1], high)
        return one(left[0], high) + (one(left[0], low) + one(left[1], high))
    if pair_left:
        if shallow:
            return one(join(left, 1), join([right, right], deep))
        return one(left[0], right) + one(left[1], right)
    if pair_right:
        if shallow:
            return one(join([left, left], 1), join(right, deep))
        if thin:
            both = one(left, join(right, out))
            return both[:, :PACK] + both[:, PACK:]
        return one(left, right[0]) + one(left, right[1])
    return one(left, right)


def ids(shape):
    return lax.broadcasted_iota(jnp.int32, shape, 0), lax.broadcasted_iota(jnp.int32, shape, 1)


def to_col(row, eye):
    return jnp.sum(jnp.where(eye, row, 0.0), 1, keepdims=True)


def to_row(col, eye):
    return jnp.sum(jnp.where(eye, col, 0.0), 0, keepdims=True)


def base_inverse(nil, base):
    size = nil.shape[0]
    count = size // base
    _, lane = ids((base, size))
    block = lane // base
    packed = jnp.zeros((base, size), F32)
    for b in range(count):
        packed = jnp.where(block == b, nil[b * base : (b + 1) * base, :], packed)
    row, lane = ids((8, size))
    first = lane // base * base
    tiles = range(base // 8)
    parts = [packed[8 * t : 8 * t + 8, :] for t in tiles]
    solved = [jnp.where(row + 8 * t == lane - first, 1.0, 0.0) for t in tiles]
    for j in range(base - 1):
        source = solved[j // 8][j % 8 : j % 8 + 1, :]
        for t in tiles[(j + 1) // 8 :]:
            factor = jnp.take_along_axis(parts[t], first + j, axis=1)
            if t == j // 8:
                factor = jnp.where(row + 8 * t > j, factor, 0.0)
            solved[t] = solved[t] + factor * source
    solved = jnp.concatenate(solved, 0)
    return jnp.concatenate([jnp.where(block == b, solved, 0.0) for b in range(count)], 0)


def inverses(nils):
    size = nils[0].shape[0]
    row, lane = ids((size, size))
    found = [base_inverse(nil, BASE) for nil in nils]
    width = BASE
    while width < size:
        factor = 4 if size >= 4 * width else 2
        wide = width * factor
        off = (row // wide == lane // wide) & (row // width != lane // width)
        known = [split(inv) for inv in found]
        steps = [split(mm(inv, jnp.where(off, nil, 0.0))) for inv, nil in zip(known, nils)]
        found = [inv + mm(step, pair) for inv, step, pair in zip(found, steps, known)]
        if factor == 4:
            steps = [mm(step, step) for step in steps]
            found = [inv + mm(step, inv) for inv, step in zip(found, steps)]
        width = wide
    return found


def decays(decay_row, row, lane):
    cum_col = jnp.sum(jnp.where(lane <= row, decay_row, 0.0), 1, keepdims=True)
    return cum_col, to_row(cum_col, row == lane)


def prep_kernel(
    flag_ref, q_ref, k_ref, decay_ref, rate_ref, spread_ref, damp_ref, kk_ref, qk_ref, rows_ref, mask_ref,
):
    length = q_ref.shape[1]
    row, lane = ids((length, length))
    cum_col, cum_row = decays(decay_ref[...], row, lane)
    rate_row = rate_ref[...]
    spread = jnp.exp(jnp.where(lane <= row, cum_col - cum_row, -1e30))
    spread_ref[...] = spread
    damp_ref[...] = jnp.where(lane < row, spread, 0.0) * -to_col(rate_row, row == lane)
    k_f, q_f = k_ref[...].astype(F32), q_ref[...].astype(F32)
    kk_ref[...] = mm(k_f.T.astype(BF16), k_ref[...])
    qk_ref[...] = mm(q_f.T.astype(BF16), k_ref[...])
    grow = jnp.exp(cum_row)
    tail = jnp.exp(cum_row[:, length - 1 :] - cum_row)
    k_sum = jnp.sum(k_f * k_f, 0, keepdims=True)
    q_sum = jnp.sum(q_f * q_f, 0, keepdims=True)
    rows_ref[...] = jnp.concatenate([cum_row, grow, tail, rate_row, k_sum, q_sum, cum_row, cum_row], 0)
    mask_ref[...] = jnp.concatenate([jnp.full((1, mask_ref.shape[1]), flag_ref[i], F32) for i in range(8)], 0)


def inverse_kernel(k_ref, other_ref, kk_in_ref, damp_ref, rows_ref, inv_ref, w_ref, kk_ref, scale_ref):
    other = other_ref[...]
    other_f = other.astype(F32)
    k_t = jnp.concatenate([k_ref[...], other], 0)
    mid = k_t.shape[1] // 2
    grow, rate_row, k_sum = (rows_ref[i : i + 1, :] for i in (1, 3, 4))
    square = k_sum + jnp.sum(other_f * other_f, 0, keepdims=True) + 1e-6
    k_scale = 1.0 / jnp.sqrt(square)
    kk = kk_in_ref[...] + mm(other_f.T.astype(BF16), other)
    nil = damp_ref[...] * (kk * (k_scale * k_scale))
    upper, lower = inverses([nil[:mid, :mid], nil[mid:, mid:]])
    keys = k_t.astype(F32) * (rate_row * grow)
    corner = nil[mid:, :mid]
    first = mm(keys[:, :mid], upper, NT)
    second = mm(mm(first, corner, NT) + keys[:, mid:], lower, NT)
    w_ref[...] = jnp.concatenate([first, second], 1) * k_scale
    inv_ref[...] = jnp.concatenate(
        [jnp.concatenate([upper, jnp.zeros_like(upper)], 1), jnp.concatenate([corner, lower], 1)], 0
    )
    kk_ref[...] = kk
    scale_ref[...] = jnp.concatenate([k_scale, square * k_scale], 0)


def shift_kernel(
    q_ref, other_ref, k_ref, k_other_ref, g_ref, qk_ref, spread_ref, rows_ref, scale_ref, w_ref, inv_in_ref,
    map_ref, score_ref, q_scale_ref, inv_ref,
):
    other = other_ref[...]
    other_f = other.astype(F32)
    k_t = jnp.concatenate([k_ref[...], k_other_ref[...]], 0)
    q_f = jnp.concatenate([q_ref[...].astype(F32), other_f], 0)
    width, length = k_t.shape
    mid = length // 2
    k_scale, grow, tail = scale_ref[0:1, :], rows_ref[1:2, :], rows_ref[2:3, :]
    score = spread_ref[...] * (qk_ref[...] + mm(other_f.T.astype(BF16), k_other_ref[...]))
    lower = split(inv_in_ref[mid:, mid:])
    corner = mm(lower, inv_in_ref[mid:, :mid])
    w_t = w_ref[...] * k_scale
    w_row, w_lane = ids((width, width))
    side = mm(w_t, score, NT)
    q_sum = rows_ref[5:6, :] + jnp.sum(other_f * other_f, 0, keepdims=True)
    q_scale = width ** (-0.5) / jnp.sqrt(q_sum + 1e-6)
    own_map = jnp.where(w_row == w_lane, grow[:, length - 1 :], 0.0) - mm(w_t * tail, k_t, NT)
    corner = mm(corner, inv_in_ref[:mid, :mid])
    side = q_scale * (q_f * grow - side)
    map_ref[width:, :] = mm(side, g_ref[...])
    map_ref[0:width, :] = own_map
    score_ref[...] = score
    q_scale_ref[...] = q_scale
    inv_ref[0:mid, :] = inv_in_ref[0:mid, :]
    inv_ref[mid:, :] = jnp.concatenate([corner, inv_in_ref[mid:, mid:]], 1)


def join_kernel(mask_ref, own_ref, got_ref, total_ref):
    width = own_ref.shape[1]
    low = mask_ref[0:1, :] > 0.0
    own, got = own_ref[width:, :], got_ref[width:, :]
    first = jnp.where(low, own_ref[0:width, :], got_ref[0:width, :])
    total_ref[...] = mm(first, jnp.where(low, got, own)) + jnp.where(low, own, got)


def update_kernel(
    mask_ref, q_ref, q_other_ref, k_ref, k_other_ref, v_ref, g_ref, start_ref, inv_ref, spread_ref, rows_ref, scale_ref,
    q_scale_ref, u_ref, base_ref, score_grad_ref, start_t_ref, keep_ref, send_ref,
):
    half, length = q_ref.shape
    q_f = jnp.concatenate([q_ref[...], q_other_ref[...]], 0).astype(F32)
    k_t = jnp.concatenate([k_ref[...], k_other_ref[...]], 0)
    width = k_t.shape[0]
    row, lane = ids((length, length))
    eye = row == lane
    grow, rate_row = rows_ref[1:2, :], rows_ref[3:4, :]
    k_scale, k_norm = scale_ref[0:1, :], scale_ref[1:2, :]
    start = start_ref[...]
    start = jnp.where(mask_ref[2:3, :] > 0.0, start, pltpu.roll(start, half, 1))
    start_t = start.T
    grad = g_ref[...]
    grad_t = grad.astype(F32).T.astype(BF16)
    k_rows = k_t.astype(F32).T.astype(BF16)
    base = v_ref[...].astype(F32) - to_col(grow * k_scale, eye) * mm(k_rows, start, NT)
    u = to_col(k_scale, eye) * mm(inv_ref[...], to_col(k_norm * rate_row, eye) * base)
    score_grad = mm(grad, u, NT) * spread_ref[...]
    q_scale = q_scale_ref[...]
    dq = mm(k_t, score_grad * k_scale, NT) + grow * mm(start_t, grad_t)
    unit = q_f * (q_scale * width**0.5)
    dq = q_scale * (dq - unit * jnp.sum(unit * dq, 0, keepdims=True))
    keep_ref[...] = dq[0:half, :]
    send_ref[...] = dq[half:, :]
    u_ref[...] = u
    base_ref[...] = base
    score_grad_ref[...] = score_grad
    start_t_ref[...] = start_t


def local_kernel(
    mask_ref, q_ref, q_other_ref, k_ref, k_other_ref, g_ref, start_t_ref, inv_ref, score_ref, damp_ref, rows_ref, scale_ref,
    q_scale_ref, u_ref, score_grad_ref, ahead_ref, after_ref,
    uth_ref, utl_ref, ph_ref, pl_ref, gh_ref, gl_ref, kh_ref, kl_ref, sh_ref, sl_ref, ah_ref, al_ref, y_ref, dk_ref,
):
    length = q_ref.shape[1]
    q_f = jnp.concatenate([q_ref[...], q_other_ref[...]], 0).astype(F32)
    k_t = jnp.concatenate([k_ref[...], k_other_ref[...]], 0)
    width = k_t.shape[0]
    eye = jnp.equal(*ids((length, length)))
    grow, tail, rate_row = (rows_ref[i : i + 1, :] for i in range(1, 4))
    k_scale, k_norm = scale_ref[0:1, :], scale_ref[1:2, :]
    low = mask_ref[0:1, :] > 0.0
    ahead_map = jnp.where(low, ahead_ref[0:width, :], jnp.where(jnp.equal(*ids((width, width))), 1.0, 0.0))
    ahead = jnp.where(low, ahead_ref[width:, :], 0.0)
    grad_t = g_ref[...].astype(F32).T.astype(BF16)
    score = score_ref[...] * to_col(q_scale_ref[...], eye)
    u_ts = split(u_ref[...].T)
    inv = inv_ref[...]
    psi_t = mm(k_t, inv * to_col(tail * k_scale * k_scale, eye)) * k_norm
    du_t = mm(grad_t, score) * (k_scale * k_scale)
    psi_s = split(psi_t.T)
    y_t = mm(du_t, inv) * k_norm
    y_t = y_t + mm(ahead.T, psi_t)
    map_s = split(ahead_map)
    psi_far = mm(psi_s, map_s)
    uz_t = mm(ahead, u_ts)
    y = y_t.T
    y_ref[...] = y
    start_s = split(start_t_ref[...])
    inner = damp_ref[...] * mm(y, u_ts)
    k_s = split(k_t.astype(F32) * k_scale)
    dk = mm(q_f * q_scale_ref[...], score_grad_ref[...]) - mm(start_s, y_t * (grow * rate_row)) + tail * uz_t
    ph_ref[...], pl_ref[...] = split(psi_far)
    gh_ref[...], gl_ref[...] = split(psi_far.T * (grow * rate_row))
    inner_s = split(inner)
    dk_ref[...] = dk + (mm(k_s, inner_s) + mm(k_s, inner_s, NT))
    uth_ref[...], utl_ref[...] = u_ts
    kh_ref[...], kl_ref[...] = k_s
    sh_ref[...], sl_ref[...] = start_s
    ah_ref[...], al_ref[...] = map_s


def far_kernel(
    mask_ref, got_ref, k_ref, k_other_ref, damp_ref, rows_ref, scale_ref,
    uth_ref, utl_ref, ph_ref, pl_ref, gh_ref, gl_ref, kh_ref, kl_ref, sh_ref, sl_ref, ah_ref, al_ref, dk_ref,
    send_ref, keep_ref,
):
    half = k_ref.shape[0]
    k_scale = scale_ref[0:1, :]
    got_s = split(jnp.where(mask_ref[1:2, :] > 0.0, got_ref[...], 0.0))
    gu_s = split(mm(got_s, (uth_ref[...], utl_ref[...])))
    sg_s = split(mm((sh_ref[...], sl_ref[...]), got_s, NT))
    inner_s = split(damp_ref[...] * mm((ph_ref[...], pl_ref[...]), gu_s))
    dk = dk_ref[...] + rows_ref[2:3, :] * mm((ah_ref[...], al_ref[...]), gu_s) - mm(sg_s, (gh_ref[...], gl_ref[...]))
    k_s = (kh_ref[...], kl_ref[...])
    dk = dk + (mm(k_s, inner_s) + mm(k_s, inner_s, NT))
    unit = jnp.concatenate([k_ref[...], k_other_ref[...]], 0).astype(F32) * k_scale
    dk = k_scale * (dk - unit * jnp.sum(unit * dk, 0, keepdims=True))
    send_ref[...] = dk[half:, :]
    keep_ref[...] = dk[0:half, :]


def value_kernel(
    mask_ref, got_ref, ph_ref, pl_ref, y_ref, base_ref, kk_ref, spread_ref, scale_ref, rows_ref, u_ref, keep_ref, got_q_ref,
    value_ref, rate_out_ref, q_ref,
):
    length = y_ref.shape[0]
    row, lane = ids((length, length))
    eye = row == lane
    k_scale = scale_ref[0:1, :]
    got = jnp.where(mask_ref[1:2, :] > 0.0, got_ref[...], 0.0)
    low = jnp.where(lane < row, spread_ref[...] * kk_ref[...], 0.0) * (to_col(k_scale, eye) * k_scale)
    y = y_ref[...] + mm((ph_ref[...], pl_ref[...]), got)
    write = base_ref[...] - mm(low, u_ref[...])
    value_ref[...] = to_col(rows_ref[3:4, :], eye) * y
    rate_out_ref[...] = to_row(jnp.sum(y * write, 1, keepdims=True), eye)
    q_ref[...] = keep_ref[...] + got_q_ref[...]


def add_kernel(keep_ref, got_ref, k_ref):
    k_ref[...] = keep_ref[...] + got_ref[...]


def call(kernel, outs, *args, smem=(), cost=1.0):
    shapes = [out if isinstance(out[0], tuple) else (out, F32) for out in outs]
    return pl.pallas_call(
        kernel,
        out_shape=tuple(jax.ShapeDtypeStruct(shape, kind) for shape, kind in shapes),
        in_specs=[
            pl.BlockSpec(memory_space=pltpu.SMEM if i in smem else pltpu.VMEM) for i in range(len(args))
        ],
        out_specs=tuple(pl.BlockSpec(memory_space=pltpu.VMEM) for _ in outs),
        cost_estimate=pl.CostEstimate(flops=int(cost * 1e9), bytes_accessed=1 << 20, transcendentals=0),
        compiler_params=pltpu.CompilerParams(vmem_limit_bytes=24 << 20),
    )(*args)


def swap(x, axis, apart):
    return lax.ppermute(x, axis, [(i, i ^ 1 << apart) for i in range(lax.axis_size(axis))])


def far_scan(section, count, place):
    def dot(left, right):
        return jnp.dot(left, right, precision=lax.Precision.HIGHEST)

    width = section.shape[1]
    own_map, own = section[:width], section[width:]
    ahead_map, ahead = jnp.eye(width, dtype=F32), jnp.zeros_like(own)
    for bit in range(count.bit_length() - 2):
        got = swap(jnp.concatenate([own_map, own], 0), "seq", bit)
        got_map, got = got[:width], got[width:]
        low = (place >> bit) % 2 == 0
        ahead = jnp.where(low, dot(ahead_map, got) + ahead, ahead)
        ahead_map = jnp.where(low, dot(ahead_map, got_map), ahead_map)
        low_map, high_map = jnp.where(low, own_map, got_map), jnp.where(low, got_map, own_map)
        own = dot(low_map, jnp.where(low, got, own)) + jnp.where(low, own, got)
        own_map = dot(low_map, high_map)
    return own, jnp.concatenate([ahead_map, ahead], 0)


def per_device(queries, key_rows, values, log_decay, beta_rate, start_states, output_grad):
    count = lax.axis_size("seq")
    stages = count.bit_length() - 1
    assert count == 1 << stages and stages >= 2
    place = lax.axis_index("seq")
    parity = lax.axis_index("head") % 2
    q_t, k_t = queries.T, key_rows.T
    half, length = q_t.shape
    width = 2 * half
    depth = values.shape[1]
    start = start_states[0, 0]
    square, tall, wide, thin = (length, length), (length, depth), (width, length), (1, length)
    k_other = swap(k_t, "head", 0)
    q_other = swap(q_t, "head", 0)
    low_first = 1 - place % 2 if stages == 2 else place * 0 + 1
    low_last = 1 - (place >> (stages - 1)) % 2
    flags = jnp.stack([low_first, low_last, 1 - parity] + [parity] * 5).astype(F32)
    spread, damp, kk_own, qk_own, rows, mask = call(
        prep_kernel, [square, square, square, square, (8, length), (8, depth)],
        flags, q_t, k_t, log_decay, beta_rate, smem=(0,),
    )
    halves, w_t, kk, scale = call(
        inverse_kernel, [square, wide, square, (2, length)], k_t, k_other, kk_own, damp, rows
    )
    section, score, q_scale, inv = call(
        shift_kernel, [(2 * width, depth), square, thin, square],
        q_t, q_other, k_t, k_other, output_grad, qk_own, spread, rows, scale, w_t, halves,
    )
    if stages == 2:
        ahead = swap(section, "seq", 0)
        (total,) = call(join_kernel, [(width, depth)], mask, section, ahead)
    else:
        total, ahead = far_scan(section, count, place)
    arrived = swap(total, "seq", stages - 1)
    u, base, score_grad, start_t, keep_q, send_q = call(
        update_kernel, [tall, tall, square, (width, depth), (half, length), (half, length)],
        mask, q_t, q_other, k_t, k_other, values, output_grad, start, inv, spread, rows, scale, q_scale,
    )
    got_q = swap(send_q, "head", 0)
    shapes = [(depth, length), (length, width), wide, wide, (width, depth), (width, width)]
    *packs, y, dk = call(
        local_kernel, [(shape, BF16) for shape in shapes for _ in range(2)] + [tall, wide],
        mask, q_t, q_other, k_t, k_other, output_grad, start_t, inv, score, damp, rows, scale, q_scale, u, score_grad, ahead,
        total,
    )
    send, keep = call(
        far_kernel, [(half, length), (half, length)],
        mask, arrived, k_t, k_other, damp, rows, scale, *packs, dk,
    )
    got_k = swap(send, "head", 0)
    value_grad, rate_grad, query_grad = call(
        value_kernel, [tall, thin, (half, length)],
        mask, arrived, packs[2], packs[3], y, base, kk, spread, scale, rows, u, keep_q, got_q,
    )
    (key_grad,) = call(add_kernel, [(half, length)], keep, got_k)
    return (query_grad.T, key_grad.T, value_grad, rate_grad)


def solution(mesh):
    in_specs = (
        P("seq", "head"),
        P("seq", "head"),
        P("seq", "head"),
        P("head", "seq"),
        P("head", "seq"),
        P("seq", "head", None, None),
        P("seq", "head"),
    )
    out_specs = (P("seq", "head"), P("seq", "head"), P("seq", "head"), P("head", "seq"))

    return jax.shard_map(per_device, mesh=mesh, in_specs=in_specs, out_specs=out_specs, check_vma=False)
```

```python
import jax
import jax.numpy as jnp
from jax import lax
from jax.experimental import pallas as pl
from jax.experimental.pallas import tpu as pltpu
from jax.sharding import PartitionSpec as P

F32 = jnp.float32
BF16 = jnp.bfloat16
BASE = 32
PACK = 128
NN = (((1,), (0,)), ((), ()))
NT = (((1,), (1,)), ((), ()))


def split(x):
    high = x.astype(BF16)
    return (high, (x - high.astype(F32)).astype(BF16))


def mm(left, right, dims=NN):
    left = left if isinstance(left, tuple) else (left if left.dtype == BF16 else split(left))
    right = right if isinstance(right, tuple) else (right if right.dtype == BF16 else split(right))
    deep, out = (0, 1) if dims is NN else (1, 0)

    def one(a, b):
        return lax.dot_general(a, b, dims, preferred_element_type=F32)

    def join(parts, axis):
        return jnp.concatenate(parts, axis)

    pair_left, pair_right = isinstance(left, tuple), isinstance(right, tuple)
    shape = (right[0] if pair_right else right).shape
    shallow, thin = shape[deep] == PACK, shape[out] == PACK
    rows = (left[0] if pair_left else left).shape[0]
    if pair_left and pair_right:
        high, low = right
        if shallow and thin:
            block = join([join([high, low], out), join([high, jnp.zeros_like(low)], out)], deep)
            both = one(join(left, 1), block)
            return both[:, :PACK] + both[:, PACK:]
        if shallow:
            return one(join(left, 1), join([high, high], deep)) + one(left[0], low)
        if thin:
            both = one(join(left, 0), join(right, out))
            return both[:rows, :PACK] + (both[:rows, PACK:] + both[rows:, :PACK])
        both = one(join(left, 0), high)
        return both[:rows] + (both[rows:] + one(left[0], low))
    if pair_left:
        if shallow:
            return one(join(left, 1), join([right, right], deep))
        both = one(join(left, 0), right)
        return both[:rows] + both[rows:]
    if pair_right:
        if shallow:
            return one(join([left, left], 1), join(right, deep))
        if thin:
            both = one(left, join(right, out))
            return both[:, :PACK] + both[:, PACK:]
        return one(left, right[0]) + one(left, right[1])
    return one(left, right)


def ids(shape):
    return lax.broadcasted_iota(jnp.int32, shape, 0), lax.broadcasted_iota(jnp.int32, shape, 1)


def to_col(row, eye):
    return jnp.sum(jnp.where(eye, row, 0.0), 1, keepdims=True)


def to_row(col, eye):
    return jnp.sum(jnp.where(eye, col, 0.0), 0, keepdims=True)


def base_inverse(nil, base):
    size = nil.shape[0]
    count = size // base
    _, lane = ids((base, size))
    block = lane // base
    packed = jnp.zeros((base, size), F32)
    for b in range(count):
        packed = jnp.where(block == b, nil[b * base : (b + 1) * base, :], packed)
    row, lane = ids((8, size))
    first = lane // base * base
    tiles = range(base // 8)
    parts = [packed[8 * t : 8 * t + 8, :] for t in tiles]
    solved = [jnp.where(row + 8 * t == lane - first, 1.0, 0.0) for t in tiles]
    for j in range(base - 1):
        source = solved[j // 8][j % 8 : j % 8 + 1, :]
        for t in tiles[(j + 1) // 8 :]:
            factor = jnp.take_along_axis(parts[t], first + j, axis=1)
            if t == j // 8:
                factor = jnp.where(row + 8 * t > j, factor, 0.0)
            solved[t] = solved[t] + factor * source
    solved = jnp.concatenate(solved, 0)
    return jnp.concatenate([jnp.where(block == b, solved, 0.0) for b in range(count)], 0)


def inverses(nils):
    size = nils[0].shape[0]
    row, lane = ids((size, size))
    found = [base_inverse(nil, BASE) for nil in nils]
    width = BASE
    while width < size:
        factor = 4 if size >= 4 * width else 2
        wide = width * factor
        off = (row // wide == lane // wide) & (row // width != lane // width)
        known = [split(inv) for inv in found]
        steps = [split(mm(inv, jnp.where(off, nil, 0.0))) for inv, nil in zip(known, nils)]
        found = [inv + mm(step, pair) for inv, step, pair in zip(found, steps, known)]
        if factor == 4:
            steps = [mm(step, step) for step in steps]
            found = [inv + mm(step, inv) for inv, step in zip(found, steps)]
        width = wide
    return found


def decays(decay_row, row, lane):
    cum_col = jnp.sum(jnp.where(lane <= row, decay_row, 0.0), 1, keepdims=True)
    return cum_col, to_row(cum_col, row == lane)


def prep_kernel(
    flag_ref, q_ref, k_ref, decay_ref, rate_ref, spread_ref, damp_ref, kk_ref, qk_ref, rows_ref, mask_ref,
):
    length = q_ref.shape[1]
    row, lane = ids((length, length))
    cum_col, cum_row = decays(decay_ref[...], row, lane)
    rate_row = rate_ref[...]
    spread = jnp.exp(jnp.where(lane <= row, cum_col - cum_row, -1e30))
    spread_ref[...] = spread
    damp_ref[...] = jnp.where(lane < row, spread, 0.0) * -to_col(rate_row, row == lane)
    k_f, q_f = k_ref[...].astype(F32), q_ref[...].astype(F32)
    kk_ref[...] = mm(k_f.T.astype(BF16), k_ref[...])
    qk_ref[...] = mm(q_f.T.astype(BF16), k_ref[...])
    grow = jnp.exp(cum_row)
    tail = jnp.exp(cum_row[:, length - 1 :] - cum_row)
    k_sum = jnp.sum(k_f * k_f, 0, keepdims=True)
    q_sum = jnp.sum(q_f * q_f, 0, keepdims=True)
    rows_ref[...] = jnp.concatenate([cum_row, grow, tail, rate_row, k_sum, q_sum, cum_row, cum_row], 0)
    mask_ref[...] = jnp.concatenate([jnp.full((1, mask_ref.shape[1]), flag_ref[i], F32) for i in range(8)], 0)


def inverse_kernel(k_ref, other_ref, kk_in_ref, damp_ref, rows_ref, inv_ref, w_ref, kk_ref, scale_ref):
    other = other_ref[...]
    other_f = other.astype(F32)
    k_t = jnp.concatenate([k_ref[...], other], 0)
    mid = k_t.shape[1] // 2
    grow, rate_row, k_sum = (rows_ref[i : i + 1, :] for i in (1, 3, 4))
    square = k_sum + jnp.sum(other_f * other_f, 0, keepdims=True) + 1e-6
    k_scale = 1.0 / jnp.sqrt(square)
    kk = kk_in_ref[...] + mm(other_f.T.astype(BF16), other)
    nil = damp_ref[...] * (kk * (k_scale * k_scale))
    upper, lower = inverses([nil[:mid, :mid], nil[mid:, mid:]])
    keys = k_t.astype(F32) * (rate_row * grow)
    corner = nil[mid:, :mid]
    first = mm(keys[:, :mid], upper, NT)
    second = mm(mm(first, corner, NT) + keys[:, mid:], lower, NT)
    w_ref[...] = jnp.concatenate([first, second], 1) * k_scale
    inv_ref[...] = jnp.concatenate(
        [jnp.concatenate([upper, jnp.zeros_like(upper)], 1), jnp.concatenate([corner, lower], 1)], 0
    )
    kk_ref[...] = kk
    scale_ref[...] = jnp.concatenate([k_scale, square * k_scale], 0)


def shift_kernel(
    q_ref, other_ref, k_ref, k_other_ref, g_ref, qk_ref, spread_ref, rows_ref, scale_ref, w_ref, inv_in_ref,
    map_ref, score_ref, q_scale_ref, inv_ref,
):
    other = other_ref[...]
    other_f = other.astype(F32)
    k_t = jnp.concatenate([k_ref[...], k_other_ref[...]], 0)
    q_f = jnp.concatenate([q_ref[...].astype(F32), other_f], 0)
    width, length = k_t.shape
    mid = length // 2
    k_scale, grow, tail = scale_ref[0:1, :], rows_ref[1:2, :], rows_ref[2:3, :]
    score = spread_ref[...] * (qk_ref[...] + mm(other_f.T.astype(BF16), k_other_ref[...]))
    lower = split(inv_in_ref[mid:, mid:])
    corner = mm(lower, inv_in_ref[mid:, :mid])
    w_t = w_ref[...] * k_scale
    w_row, w_lane = ids((width, width))
    side = mm(w_t, score, NT)
    q_sum = rows_ref[5:6, :] + jnp.sum(other_f * other_f, 0, keepdims=True)
    q_scale = width ** (-0.5) / jnp.sqrt(q_sum + 1e-6)
    own_map = jnp.where(w_row == w_lane, grow[:, length - 1 :], 0.0) - mm(w_t * tail, k_t, NT)
    corner = mm(corner, inv_in_ref[:mid, :mid])
    side = q_scale * (q_f * grow - side)
    map_ref[width:, :] = mm(side, g_ref[...])
    map_ref[0:width, :] = own_map
    score_ref[...] = score
    q_scale_ref[...] = q_scale
    inv_ref[0:mid, :] = inv_in_ref[0:mid, :]
    inv_ref[mid:, :] = jnp.concatenate([corner, inv_in_ref[mid:, mid:]], 1)


def join_kernel(mask_ref, own_ref, got_ref, total_ref):
    width = own_ref.shape[1]
    low = mask_ref[0:1, :] > 0.0
    own, got = own_ref[width:, :], got_ref[width:, :]
    first = jnp.where(low, own_ref[0:width, :], got_ref[0:width, :])
    total_ref[...] = mm(first, jnp.where(low, got, own)) + jnp.where(low, own, got)


def update_kernel(
    mask_ref, q_ref, q_other_ref, k_ref, k_other_ref, v_ref, g_ref, start_ref, inv_ref, spread_ref, rows_ref, scale_ref,
    q_scale_ref, u_ref, base_ref, score_grad_ref, start_t_ref, keep_ref, send_ref,
):
    half, length = q_ref.shape
    q_f = jnp.concatenate([q_ref[...], q_other_ref[...]], 0).astype(F32)
    k_t = jnp.concatenate([k_ref[...], k_other_ref[...]], 0)
    width = k_t.shape[0]
    row, lane = ids((length, length))
    eye = row == lane
    grow, rate_row = rows_ref[1:2, :], rows_ref[3:4, :]
    k_scale, k_norm = scale_ref[0:1, :], scale_ref[1:2, :]
    start = start_ref[...]
    start = jnp.where(mask_ref[2:3, :] > 0.0, start, pltpu.roll(start, half, 1))
    start_t = start.T
    grad = g_ref[...]
    grad_t = grad.astype(F32).T.astype(BF16)
    k_rows = k_t.astype(F32).T.astype(BF16)
    base = v_ref[...].astype(F32) - to_col(grow * k_scale, eye) * mm(k_rows, start, NT)
    u = to_col(k_scale, eye) * mm(inv_ref[...], to_col(k_norm * rate_row, eye) * base)
    score_grad = mm(grad, u, NT) * spread_ref[...]
    q_scale = q_scale_ref[...]
    dq = mm(k_t, score_grad * k_scale, NT) + grow * mm(start_t, grad_t)
    unit = q_f * (q_scale * width**0.5)
    dq = q_scale * (dq - unit * jnp.sum(unit * dq, 0, keepdims=True))
    keep_ref[...] = dq[0:half, :]
    send_ref[...] = dq[half:, :]
    u_ref[...] = u
    base_ref[...] = base
    score_grad_ref[...] = score_grad
    start_t_ref[...] = start_t


def local_kernel(
    mask_ref, q_ref, q_other_ref, k_ref, k_other_ref, g_ref, start_t_ref, inv_ref, score_ref, damp_ref, rows_ref, scale_ref,
    q_scale_ref, u_ref, score_grad_ref, ahead_ref, after_ref,
    uth_ref, utl_ref, uh_ref, ul_ref, ph_ref, pl_ref, pth_ref, ptl_ref, gh_ref, gl_ref, kh_ref, kl_ref, sym_ref, y_ref, dk_ref,
):
    length = q_ref.shape[1]
    q_f = jnp.concatenate([q_ref[...], q_other_ref[...]], 0).astype(F32)
    k_t = jnp.concatenate([k_ref[...], k_other_ref[...]], 0)
    width = k_t.shape[0]
    eye = jnp.equal(*ids((length, length)))
    grow, tail, rate_row = (rows_ref[i : i + 1, :] for i in range(1, 4))
    k_scale, k_norm = scale_ref[0:1, :], scale_ref[1:2, :]
    low = mask_ref[0:1, :] > 0.0
    ahead_map = jnp.where(low, ahead_ref[0:width, :], jnp.where(jnp.equal(*ids((width, width))), 1.0, 0.0))
    ahead = jnp.where(low, ahead_ref[width:, :], 0.0)
    grad_t = g_ref[...].astype(F32).T.astype(BF16)
    score = score_ref[...] * to_col(q_scale_ref[...], eye)
    u = u_ref[...]
    u_ts = split(u.T)
    inv = inv_ref[...]
    damp = damp_ref[...]
    psi_t = mm(k_t, inv * to_col(tail * k_scale * k_scale, eye)) * k_norm
    du_t = mm(grad_t, score) * (k_scale * k_scale)
    psi_s = split(psi_t.T)
    y_t = mm(du_t, inv) * k_norm
    sym = damp + damp.T
    sym_ref[...] = sym
    y_t = y_t + mm(ahead.T, psi_t)
    map_s = split(ahead_map)
    psi_far = mm(psi_s, map_s)
    uz_t = mm(ahead, u_ts)
    y = y_t.T
    y_ref[...] = y
    start_t = start_t_ref[...]
    start_s = split(start_t)
    inner = damp * mm(y, u_ts)
    k_s = split(k_t.astype(F32) * k_scale)
    dk = mm(q_f * q_scale_ref[...], score_grad_ref[...]) - mm(start_s, y_t * (grow * rate_row)) + tail * uz_t
    psi_far_s = split(psi_far)
    psi_far_t = psi_far.T
    ph_ref[0:length, :], pl_ref[0:length, :] = psi_far_s
    ph_ref[length:, :], pl_ref[length:, :] = map_s
    pth_ref[...], ptl_ref[...] = split(psi_far_t)
    gh_ref[...], gl_ref[...] = split(psi_far_t * (grow * rate_row))
    dk_ref[...] = dk + mm(k_s, inner + inner.T)
    uth_ref[...], utl_ref[...] = u_ts
    uh_ref[0:length, :], ul_ref[0:length, :] = split(u)
    uh_ref[length:, :], ul_ref[length:, :] = start_s
    kh_ref[...], kl_ref[...] = k_s


def far_kernel(
    mask_ref, got_ref, k_ref, k_other_ref, rows_ref, scale_ref,
    uth_ref, utl_ref, uh_ref, ul_ref, ph_ref, pl_ref, pth_ref, ptl_ref, gh_ref, gl_ref, kh_ref, kl_ref, sym_ref, dk_ref,
    send_ref, keep_ref,
):
    half, length = k_ref.shape
    k_scale = scale_ref[0:1, :]
    row, lane = ids((length, length))
    got_s = split(jnp.where(mask_ref[1:2, :] > 0.0, got_ref[...], 0.0))
    gu_s = split(mm(got_s, (uth_ref[...], utl_ref[...])))
    right = mm((uh_ref[...], ul_ref[...]), got_s, NT)
    upper = mm(right[0:length, :], (pth_ref[...], ptl_ref[...]))
    left = mm((ph_ref[...], pl_ref[...]), gu_s)
    inner = sym_ref[...] * jnp.where(lane < row, left[0:length, :], upper)
    dk = dk_ref[...] + rows_ref[2:3, :] * left[length:, :] - mm(right[length:, :], (gh_ref[...], gl_ref[...]))
    dk = dk + mm((kh_ref[...], kl_ref[...]), inner)
    unit = jnp.concatenate([k_ref[...], k_other_ref[...]], 0).astype(F32) * k_scale
    dk = k_scale * (dk - unit * jnp.sum(unit * dk, 0, keepdims=True))
    send_ref[...] = dk[half:, :]
    keep_ref[...] = dk[0:half, :]


def value_kernel(
    mask_ref, got_ref, ph_ref, pl_ref, y_ref, base_ref, kk_ref, spread_ref, scale_ref, rows_ref, u_ref, keep_ref, got_q_ref,
    value_ref, rate_out_ref, q_ref,
):
    length = y_ref.shape[0]
    row, lane = ids((length, length))
    eye = row == lane
    k_scale = scale_ref[0:1, :]
    got = jnp.where(mask_ref[1:2, :] > 0.0, got_ref[...], 0.0)
    low = jnp.where(lane < row, spread_ref[...] * kk_ref[...], 0.0) * (to_col(k_scale, eye) * k_scale)
    y = y_ref[...] + mm((ph_ref[0:length, :], pl_ref[0:length, :]), got)
    write = base_ref[...] - mm(low, u_ref[...])
    value_ref[...] = to_col(rows_ref[3:4, :], eye) * y
    rate_out_ref[...] = to_row(jnp.sum(y * write, 1, keepdims=True), eye)
    q_ref[...] = keep_ref[...] + got_q_ref[...]


def add_kernel(keep_ref, got_ref, k_ref):
    k_ref[...] = keep_ref[...] + got_ref[...]


def call(kernel, outs, *args, smem=(), cost=1.0):
    shapes = [out if isinstance(out[0], tuple) else (out, F32) for out in outs]
    return pl.pallas_call(
        kernel,
        out_shape=tuple(jax.ShapeDtypeStruct(shape, kind) for shape, kind in shapes),
        in_specs=[
            pl.BlockSpec(memory_space=pltpu.SMEM if i in smem else pltpu.VMEM) for i in range(len(args))
        ],
        out_specs=tuple(pl.BlockSpec(memory_space=pltpu.VMEM) for _ in outs),
        cost_estimate=pl.CostEstimate(flops=int(cost * 1e9), bytes_accessed=1 << 20, transcendentals=0),
        compiler_params=pltpu.CompilerParams(vmem_limit_bytes=24 << 20),
    )(*args)


def swap(x, axis, apart):
    return lax.ppermute(x, axis, [(i, i ^ 1 << apart) for i in range(lax.axis_size(axis))])


def far_scan(section, count, place):
    def dot(left, right):
        return jnp.dot(left, right, precision=lax.Precision.HIGHEST)

    width = section.shape[1]
    own_map, own = section[:width], section[width:]
    ahead_map, ahead = jnp.eye(width, dtype=F32), jnp.zeros_like(own)
    for bit in range(count.bit_length() - 2):
        got = swap(jnp.concatenate([own_map, own], 0), "seq", bit)
        got_map, got = got[:width], got[width:]
        low = (place >> bit) % 2 == 0
        ahead = jnp.where(low, dot(ahead_map, got) + ahead, ahead)
        ahead_map = jnp.where(low, dot(ahead_map, got_map), ahead_map)
        low_map, high_map = jnp.where(low, own_map, got_map), jnp.where(low, got_map, own_map)
        own = dot(low_map, jnp.where(low, got, own)) + jnp.where(low, own, got)
        own_map = dot(low_map, high_map)
    return own, jnp.concatenate([ahead_map, ahead], 0)


def per_device(queries, key_rows, values, log_decay, beta_rate, start_states, output_grad):
    count = lax.axis_size("seq")
    stages = count.bit_length() - 1
    assert count == 1 << stages and stages >= 2
    place = lax.axis_index("seq")
    parity = lax.axis_index("head") % 2
    q_t, k_t = queries.T, key_rows.T
    half, length = q_t.shape
    width = 2 * half
    depth = values.shape[1]
    start = start_states[0, 0]
    square, tall, wide, thin = (length, length), (length, depth), (width, length), (1, length)
    k_other = swap(k_t, "head", 0)
    q_other = swap(q_t, "head", 0)
    low_first = 1 - place % 2 if stages == 2 else place * 0 + 1
    low_last = 1 - (place >> (stages - 1)) % 2
    flags = jnp.stack([low_first, low_last, 1 - parity] + [parity] * 5).astype(F32)
    spread, damp, kk_own, qk_own, rows, mask = call(
        prep_kernel, [square, square, square, square, (8, length), (8, depth)],
        flags, q_t, k_t, log_decay, beta_rate, smem=(0,),
    )
    halves, w_t, kk, scale = call(
        inverse_kernel, [square, wide, square, (2, length)], k_t, k_other, kk_own, damp, rows
    )
    section, score, q_scale, inv = call(
        shift_kernel, [(2 * width, depth), square, thin, square],
        q_t, q_other, k_t, k_other, output_grad, qk_own, spread, rows, scale, w_t, halves,
    )
    if stages == 2:
        ahead = swap(section, "seq", 0)
        (total,) = call(join_kernel, [(width, depth)], mask, section, ahead)
    else:
        total, ahead = far_scan(section, count, place)
    arrived = swap(total, "seq", stages - 1)
    u, base, score_grad, start_t, keep_q, send_q = call(
        update_kernel, [tall, tall, square, (width, depth), (half, length), (half, length)],
        mask, q_t, q_other, k_t, k_other, values, output_grad, start, inv, spread, rows, scale, q_scale,
    )
    got_q = swap(send_q, "head", 0)
    shapes = [(depth, length), (length + width, depth), (length + width, width), wide, wide, wide]
    *packs, sym, y, dk = call(
        local_kernel, [(shape, BF16) for shape in shapes for _ in range(2)] + [square, tall, wide],
        mask, q_t, q_other, k_t, k_other, output_grad, start_t, inv, score, damp, rows, scale, q_scale, u, score_grad, ahead,
        total,
    )
    send, keep = call(
        far_kernel, [(half, length), (half, length)],
        mask, arrived, k_t, k_other, rows, scale, *packs, sym, dk,
    )
    got_k = swap(send, "head", 0)
    value_grad, rate_grad, query_grad = call(
        value_kernel, [tall, thin, (half, length)],
        mask, arrived, packs[4], packs[5], y, base, kk, spread, scale, rows, u, keep_q, got_q,
    )
    (key_grad,) = call(add_kernel, [(half, length)], keep, got_k)
    return (query_grad.T, key_grad.T, value_grad, rate_grad)


def solution(mesh):
    in_specs = (
        P("seq", "head"),
        P("seq", "head"),
        P("seq", "head"),
        P("head", "seq"),
        P("head", "seq"),
        P("seq", "head", None, None),
        P("seq", "head"),
    )
    out_specs = (P("seq", "head"), P("seq", "head"), P("seq", "head"), P("head", "seq"))

    return jax.shard_map(per_device, mesh=mesh, in_specs=in_specs, out_specs=out_specs, check_vma=False)
```

```python
import jax
import jax.numpy as jnp
from jax import lax
from jax.experimental import pallas as pl
from jax.experimental.pallas import tpu as pltpu
from jax.sharding import PartitionSpec as P

F32 = jnp.float32
BF16 = jnp.bfloat16
BASE = 32
PACK = 128
NN = (((1,), (0,)), ((), ()))
NT = (((1,), (1,)), ((), ()))


def split(x):
    high = x.astype(BF16)
    return (high, (x - high.astype(F32)).astype(BF16))


def mm(left, right, dims=NN):
    left = left if isinstance(left, tuple) else (left if left.dtype == BF16 else split(left))
    right = right if isinstance(right, tuple) else (right if right.dtype == BF16 else split(right))
    deep, out = (0, 1) if dims is NN else (1, 0)

    def one(a, b):
        return lax.dot_general(a, b, dims, preferred_element_type=F32)

    def join(parts, axis):
        return jnp.concatenate(parts, axis)

    pair_left, pair_right = isinstance(left, tuple), isinstance(right, tuple)
    shape = (right[0] if pair_right else right).shape
    shallow, thin = shape[deep] == PACK, shape[out] == PACK
    rows = (left[0] if pair_left else left).shape[0]
    if pair_left and pair_right:
        high, low = right
        if shallow and thin:
            block = join([join([high, low], out), join([high, jnp.zeros_like(low)], out)], deep)
            both = one(join(left, 1), block)
            return both[:, :PACK] + both[:, PACK:]
        if shallow:
            return one(join(left, 1), join([high, high], deep)) + one(left[0], low)
        if thin:
            both = one(join(left, 0), join(right, out))
            return both[:rows, :PACK] + (both[:rows, PACK:] + both[rows:, :PACK])
        both = one(join(left, 0), high)
        return both[:rows] + (both[rows:] + one(left[0], low))
    if pair_left:
        if shallow:
            return one(join(left, 1), join([right, right], deep))
        both = one(join(left, 0), right)
        return both[:rows] + both[rows:]
    if pair_right:
        if shallow:
            return one(join([left, left], 1), join(right, deep))
        if thin:
            both = one(left, join(right, out))
            return both[:, :PACK] + both[:, PACK:]
        return one(left, right[0]) + one(left, right[1])
    return one(left, right)


def ids(shape):
    return lax.broadcasted_iota(jnp.int32, shape, 0), lax.broadcasted_iota(jnp.int32, shape, 1)


def to_col(row, eye):
    return jnp.sum(jnp.where(eye, row, 0.0), 1, keepdims=True)


def to_row(col, eye):
    return jnp.sum(jnp.where(eye, col, 0.0), 0, keepdims=True)


def base_inverse(nil, base):
    size = nil.shape[0]
    count = size // base
    _, lane = ids((base, size))
    block = lane // base
    packed = jnp.zeros((base, size), F32)
    for b in range(count):
        packed = jnp.where(block == b, nil[b * base : (b + 1) * base, :], packed)
    row, lane = ids((8, size))
    first = lane // base * base
    tiles = range(base // 8)
    parts = [packed[8 * t : 8 * t + 8, :] for t in tiles]
    solved = [jnp.where(row + 8 * t == lane - first, 1.0, 0.0) for t in tiles]
    for j in range(base - 1):
        source = solved[j // 8][j % 8 : j % 8 + 1, :]
        for t in tiles[(j + 1) // 8 :]:
            factor = jnp.take_along_axis(parts[t], first + j, axis=1)
            if t == j // 8:
                factor = jnp.where(row + 8 * t > j, factor, 0.0)
            solved[t] = solved[t] + factor * source
    solved = jnp.concatenate(solved, 0)
    return jnp.concatenate([jnp.where(block == b, solved, 0.0) for b in range(count)], 0)


def inverses(nils):
    size = nils[0].shape[0]
    row, lane = ids((size, size))
    found = [base_inverse(nil, BASE) for nil in nils]
    width = BASE
    while width < size:
        factor = 4 if size >= 4 * width else 2
        wide = width * factor
        off = (row // wide == lane // wide) & (row // width != lane // width)
        known = [split(inv) for inv in found]
        steps = [split(mm(inv, jnp.where(off, nil, 0.0))) for inv, nil in zip(known, nils)]
        found = [inv + mm(step, pair) for inv, step, pair in zip(found, steps, known)]
        if factor == 4:
            steps = [mm(step, step) for step in steps]
            found = [inv + mm(step, inv) for inv, step in zip(found, steps)]
        width = wide
    return found


def head_terms(decay_row, rate_row, row, lane):
    cum_col = jnp.sum(jnp.where(lane <= row, decay_row, 0.0), 1, keepdims=True)
    eye = row == lane
    cum_row = to_row(cum_col, eye)
    rate_col = to_col(rate_row, eye)
    apart = cum_col - cum_row
    spread = jnp.exp(jnp.where(lane <= row, apart, -1e30))
    spread_t = jnp.exp(jnp.where(lane >= row, -apart, -1e30))
    damp = jnp.where(lane < row, spread, 0.0) * -rate_col
    tail = jnp.exp(cum_row[:, cum_row.shape[1] - 1 :] - cum_row)
    rows = jnp.concatenate([jnp.exp(cum_row), tail, rate_row, cum_row], 0)
    return spread, spread_t, damp, rows


def parts_of(x):
    high = x.astype(BF16).astype(F32)
    middle = (x - high).astype(BF16).astype(F32)
    return [high, middle, x - high - middle]


def pack_kernel(q_ref, k_ref, g_ref, decay_ref, rate_ref, out_ref):
    half, length = q_ref.shape
    mid = length // 2
    rows = parts_of(decay_ref[...]) + parts_of(rate_ref[...])
    out_ref[0:half, :] = k_ref[...]
    out_ref[half : 2 * half, :] = q_ref[...]
    out_ref[2 * half : 2 * half + mid, :] = jnp.concatenate([g_ref[0:mid, :], g_ref[mid:, :]], 1)
    out_ref[2 * half + mid :, :] = jnp.concatenate(rows + [jnp.zeros((10, length), F32)], 0).astype(BF16)


def unpack(pack_ref, half):
    length = pack_ref.shape[1]
    mid = length // 2
    grad = pack_ref[2 * half : 2 * half + mid, :]
    rows = pack_ref[2 * half + mid :, :].astype(F32)
    decay_row = rows[0:1, :] + rows[1:2, :] + rows[2:3, :]
    rate_row = rows[3:4, :] + rows[4:5, :] + rows[5:6, :]
    return jnp.concatenate([grad[:, 0:mid], grad[:, mid:]], 0), decay_row, rate_row


def prep_kernel(
    flag_ref, q_ref, k_ref, decay_ref, rate_ref, spread_ref, spread_t_ref, damp_ref, kk_ref, kq_ref, rows_ref, mask_ref,
):
    length = q_ref.shape[1]
    row, lane = ids((length, length))
    spread_ref[...], spread_t_ref[...], damp_ref[...], rows_ref[...] = head_terms(
        decay_ref[...], rate_ref[...], row, lane
    )
    k_rows = k_ref[...].astype(F32).T.astype(BF16)
    kk_ref[...] = mm(k_rows, k_ref[...])
    kq_ref[...] = mm(k_rows, q_ref[...])
    mask_ref[...] = jnp.concatenate([jnp.full((1, mask_ref.shape[1]), flag_ref[i], F32) for i in range(8)], 0)


def map_kernel(
    q_ref, k_ref, pack_ref, g_ref, kk_own_ref, kq_own_ref, damp_ref, spread_t_ref, rows_ref,
    section_ref, inv_ref, inv_b_ref, score_g_ref, score_g_b_ref, kk_ref, damp_b_ref, spread_b_ref, rows_b_ref, scale_ref,
):
    half, length = q_ref.shape
    mid = length // 2
    row, lane = ids((length, length))
    k_other, q_other = pack_ref[0:half, :], pack_ref[half : 2 * half, :]
    grad_b, decay_b, rate_b = unpack(pack_ref, half)
    k_t = jnp.concatenate([k_ref[...], k_other], 0)
    q_t = jnp.concatenate([q_ref[...], q_other], 0)
    width = 2 * half
    k_f, q_f = k_t.astype(F32), q_t.astype(F32)
    other_rows = k_other.astype(F32).T.astype(BF16)
    kk = kk_own_ref[...] + mm(other_rows, k_other)
    spread_b, spread_t_b, damp_b, rows_b = head_terms(decay_b, rate_b, row, lane)
    square = jnp.sum(k_f * k_f, 0, keepdims=True) + 1e-6
    k_scale = 1.0 / jnp.sqrt(square)
    q_scale = width ** (-0.5) / jnp.sqrt(jnp.sum(q_f * q_f, 0, keepdims=True) + 1e-6)
    scaled = kk * (k_scale * k_scale)
    nils = [damp_ref[...] * scaled, damp_b * scaled]
    rows = [rows_ref[...], rows_b]
    kq = (kq_own_ref[...] + mm(other_rows, q_other)) * q_scale
    grads = [g_ref[...], grad_b]
    score_g = [mm(spread * kq, grad) for spread, grad in zip((spread_t_ref[...], spread_t_b), grads)]
    direct = [mm(q_f * (q_scale * r[0:1, :]), grad) for r, grad in zip(rows, grads)]
    found = inverses([block for nil in nils for block in (nil[:mid, :mid], nil[mid:, mid:])])
    uppers, lowers = [split(x) for x in found[0::2]], [split(x) for x in found[1::2]]
    corners = [split(nil[mid:, :mid]) for nil in nils]
    keys = [k_f * (r[2:3, :] * r[0:1, :]) for r in rows]
    first = [mm(key[:, :mid], upper, NT) for key, upper in zip(keys, uppers)]
    below = [mm(lower, corner) for lower, corner in zip(lowers, corners)]
    second = [mm(f, corner, NT) + key[:, mid:] for f, corner, key in zip(first, corners, keys)]
    second = [mm(s, lower, NT) for s, lower in zip(second, lowers)]
    below = [mm(b, upper) for b, upper in zip(below, uppers)]
    w_t = [jnp.concatenate([f, s], 1) * (k_scale * k_scale) for f, s in zip(first, second)]
    eye = jnp.equal(*ids((width, width)))
    for i in range(2):
        ends = jnp.where(eye, rows[i][0:1, length - 1 :], 0.0)
        section_ref[2 * i * width : (2 * i + 1) * width, :] = ends - mm(w_t[i] * rows[i][1:2, :], k_t, NT)
        section_ref[(2 * i + 1) * width : (2 * i + 2) * width, :] = direct[i] - mm(w_t[i], score_g[i])
    for ref, upper, b, lower in zip((inv_ref, inv_b_ref), found[0::2], below, found[1::2]):
        ref[0:mid, :] = jnp.concatenate([upper, jnp.zeros_like(upper)], 1)
        ref[mid:, :] = jnp.concatenate([b, lower], 1)
    score_g_ref[...], score_g_b_ref[...] = score_g
    kk_ref[...] = kk
    damp_b_ref[...], spread_b_ref[...], rows_b_ref[...] = damp_b, spread_b, rows_b
    scale_ref[...] = jnp.concatenate([k_scale, square * k_scale, q_scale, q_scale], 0)


def join_kernel(mask_ref, own_ref, got_ref, total_ref):
    width = own_ref.shape[1]
    low = mask_ref[0:1, :] > 0.0
    for i in range(2):
        a, b = pl.ds(2 * i * width, width), pl.ds((2 * i + 1) * width, width)
        own, got = own_ref[b, :], got_ref[b, :]
        first = jnp.where(low, own_ref[a, :], got_ref[a, :])
        total_ref[pl.ds(i * width, width), :] = mm(first, jnp.where(low, got, own)) + jnp.where(low, own, got)


def update_kernel(
    mask_ref, k_ref, pack_ref, v_ref, v_b_ref, start_ref, start_b_ref, inv_ref, inv_b_ref, rows_ref, rows_b_ref, scale_ref,
    base_ref, u_ref, u_b_ref, psi_ref, psi_b_ref, start_t_ref, start_t_b_ref,
):
    half, length = k_ref.shape
    k_t = jnp.concatenate([k_ref[...], pack_ref[0:half, :]], 0)
    eye = jnp.equal(*ids((length, length)))
    k_scale, k_norm = scale_ref[0:1, :], scale_ref[1:2, :]
    scale_col, norm_col = to_col(k_scale, eye), to_col(k_norm, eye)
    k_rows = k_t.astype(F32).T.astype(BF16)
    rows = [rows_ref[...], rows_b_ref[...]]
    grow, tail, rate = ([to_col(r[i : i + 1, :], eye) for r in rows] for i in range(3))
    even = mask_ref[2:3, :] > 0.0
    starts = [jnp.where(even, ref[...], pltpu.roll(ref[...], half, 1)) for ref in (start_ref, start_b_ref)]
    values = [v_ref[...], v_b_ref[...]]
    invs = [inv_ref[...], inv_b_ref[...]]
    bases = [v.astype(F32) - g * scale_col * mm(k_rows, st, NT) for v, g, st in zip(values, grow, starts)]
    psis = [mm(k_t, inv * (t * scale_col * scale_col)) * k_norm for inv, t in zip(invs, tail)]
    us = [scale_col * mm(inv, norm_col * r * base) for inv, r, base in zip(invs, rate, bases)]
    start_t_ref[...], start_t_b_ref[...] = (st.T for st in starts)
    psi_ref[...], psi_b_ref[...] = psis
    base_ref[...] = bases[0]
    u_ref[...], u_b_ref[...] = us


def local_kernel(
    mask_ref, q_ref, k_ref, pack_ref, g_ref, inv_ref, inv_b_ref, score_g_ref, score_g_b_ref, kk_ref, damp_ref, damp_b_ref,
    spread_ref, spread_b_ref, rows_ref, rows_b_ref, scale_ref, base_ref, u_ref, u_b_ref, psi_ref, psi_b_ref, start_t_ref,
    start_t_b_ref, ahead_ref, after_ref,
    kh_ref, kl_ref, uth_ref, utl_ref, uh_ref, ul_ref, ph_ref, pl_ref, pth_ref, ptl_ref, gh_ref, gl_ref,
    uth_b_ref, utl_b_ref, uh_b_ref, ul_b_ref, ph_b_ref, pl_b_ref, pth_b_ref, ptl_b_ref, gh_b_ref, gl_b_ref,
    sym_ref, sym_b_ref, y_ref, write_ref, dk_ref, q_grad_ref,
):
    half, length = q_ref.shape
    k_t = jnp.concatenate([k_ref[...], pack_ref[0:half, :]], 0)
    q_f = jnp.concatenate([q_ref[...], pack_ref[half : 2 * half, :]], 0).astype(F32)
    width = 2 * half
    row, lane = ids((length, length))
    eye = row == lane
    k_scale, k_norm, q_scale = (scale_ref[i : i + 1, :] for i in range(3))
    rows = [rows_ref[...], rows_b_ref[...]]
    grow, tail, rate = ([r[i : i + 1, :] for r in rows] for i in range(3))
    low = mask_ref[0:1, :] > 0.0
    w_eye = jnp.where(jnp.equal(*ids((width, width))), 1.0, 0.0)
    maps = [split(jnp.where(low, ahead_ref[pl.ds(2 * i * width, width), :], w_eye)) for i in range(2)]
    ahead = [jnp.where(low, ahead_ref[pl.ds((2 * i + 1) * width, width), :], 0.0) for i in range(2)]
    grads = [g_ref[...], unpack(pack_ref, half)[0]]
    grads_t = [g.astype(F32).T.astype(BF16) for g in grads]
    us = [u_ref[...], u_b_ref[...]]
    us_t = [split(u.T) for u in us]
    psis_t = [psi_ref[...], psi_b_ref[...]]
    psis = [split(p.T) for p in psis_t]
    starts = [split(start_t_ref[...]), split(start_t_b_ref[...])]
    damps = [damp_ref[...], damp_b_ref[...]]
    sides = [sg.T * (k_scale * k_scale) for sg in (score_g_ref[...], score_g_b_ref[...])]
    ys_t = [mm(side, inv) * k_norm for side, inv in zip(sides, (inv_ref[...], inv_b_ref[...]))]
    score_grads = [mm(g, u) * spread for g, u, spread in zip(grads, us_t, (spread_ref[...], spread_b_ref[...]))]
    ys_t = [y + mm(a.T, p) for y, a, p in zip(ys_t, ahead, psis_t)]
    psi_far = [mm(p, m) for p, m in zip(psis, maps)]
    uz_t = [mm(a, u) for a, u in zip(ahead, us_t)]
    ys = [y.T for y in ys_t]
    inner = [d * mm(y, u) for d, y, u in zip(damps, ys, us_t)]
    score_grad = score_grads[0] + score_grads[1]
    dq = mm(k_t, score_grad * k_scale, NT)
    dq = dq + grow[0] * mm(starts[0], grads_t[0]) + grow[1] * mm(starts[1], grads_t[1])
    k_s = split(k_t.astype(F32) * k_scale)
    dk = mm(q_f * q_scale, score_grad)
    for i in range(2):
        dk = dk - mm(starts[i], ys_t[i] * (grow[i] * rate[i])) + tail[i] * uz_t[i]
    inner = inner[0] + inner[1]
    dk_ref[...] = dk + mm(k_s, inner + inner.T)
    unit = q_f * (q_scale * width**0.5)
    dq = q_scale * (dq - unit * jnp.sum(unit * dq, 0, keepdims=True))
    q_grad_ref[...] = dq[0:half, :]
    strict = jnp.where(lane < row, spread_ref[...] * kk_ref[...], 0.0) * (to_col(k_scale, eye) * k_scale)
    write_ref[...] = base_ref[...] - mm(strict, us[0])
    y_ref[...] = ys[0]
    kh_ref[...], kl_ref[...] = k_s
    outs = (
        (uth_ref, utl_ref, uh_ref, ul_ref, ph_ref, pl_ref, pth_ref, ptl_ref, gh_ref, gl_ref, sym_ref),
        (uth_b_ref, utl_b_ref, uh_b_ref, ul_b_ref, ph_b_ref, pl_b_ref, pth_b_ref, ptl_b_ref, gh_b_ref, gl_b_ref, sym_b_ref),
    )
    for i, refs in enumerate(outs):
        refs[0][...], refs[1][...] = us_t[i]
        refs[2][0:length, :], refs[3][0:length, :] = split(us[i])
        refs[2][length:, :], refs[3][length:, :] = starts[i]
        refs[4][0:length, :], refs[5][0:length, :] = split(psi_far[i])
        refs[4][length:, :], refs[5][length:, :] = maps[i]
        psi_far_t = psi_far[i].T
        refs[6][...], refs[7][...] = split(psi_far_t)
        refs[8][...], refs[9][...] = split(psi_far_t * (grow[i] * rate[i]))
        refs[10][...] = damps[i] + damps[i].T


def far_kernel(
    mask_ref, got_ref, k_ref, pack_ref, rows_ref, rows_b_ref, scale_ref,
    kh_ref, kl_ref, uth_ref, utl_ref, uh_ref, ul_ref, ph_ref, pl_ref, pth_ref, ptl_ref, gh_ref, gl_ref,
    uth_b_ref, utl_b_ref, uh_b_ref, ul_b_ref, ph_b_ref, pl_b_ref, pth_b_ref, ptl_b_ref, gh_b_ref, gl_b_ref,
    sym_ref, sym_b_ref, y_ref, write_ref, dk_ref,
    k_grad_ref, value_ref, rate_out_ref,
):
    half, length = k_ref.shape
    width = 2 * half
    row, lane = ids((length, length))
    eye = row == lane
    k_scale = scale_ref[0:1, :]
    on = mask_ref[1:2, :] > 0.0
    got = [split(jnp.where(on, got_ref[pl.ds(i * width, width), :], 0.0)) for i in range(2)]
    right_of = [(uth_ref[...], utl_ref[...]), (uth_b_ref[...], utl_b_ref[...])]
    rows_of = [(uh_ref[...], ul_ref[...]), (uh_b_ref[...], ul_b_ref[...])]
    psi_of = [(ph_ref[...], pl_ref[...]), (ph_b_ref[...], pl_b_ref[...])]
    psi_t_of = [(pth_ref[...], ptl_ref[...]), (pth_b_ref[...], ptl_b_ref[...])]
    far_of = [(gh_ref[...], gl_ref[...]), (gh_b_ref[...], gl_b_ref[...])]
    gu = [split(mm(z, u)) for z, u in zip(got, right_of)]
    right = [mm(u, z, NT) for u, z in zip(rows_of, got)]
    left = [mm(p, u) for p, u in zip(psi_of, gu)]
    upper = [mm(r[0:length, :], p) for r, p in zip(right, psi_t_of)]
    inner = sym_ref[...] * jnp.where(lane < row, left[0][0:length, :], upper[0])
    inner = inner + sym_b_ref[...] * jnp.where(lane < row, left[1][0:length, :], upper[1])
    dk = dk_ref[...]
    for i, r in enumerate((rows_ref, rows_b_ref)):
        dk = dk + r[1:2, :] * left[i][length:, :] - mm(right[i][length:, :], far_of[i])
    dk = dk + mm((kh_ref[...], kl_ref[...]), inner)
    y = y_ref[...] + mm((ph_ref[0:length, :], pl_ref[0:length, :]), got[0])
    unit = jnp.concatenate([k_ref[...], pack_ref[0:half, :]], 0).astype(F32) * k_scale
    dk = k_scale * (dk - unit * jnp.sum(unit * dk, 0, keepdims=True))
    k_grad_ref[...] = dk[0:half, :]
    value_ref[...] = to_col(rows_ref[2:3, :], eye) * y
    rate_out_ref[...] = to_row(jnp.sum(y * write_ref[...], 1, keepdims=True), eye)


def call(kernel, outs, *args, smem=(), cost=1.0):
    shapes = [out if isinstance(out[0], tuple) else (out, F32) for out in outs]
    return pl.pallas_call(
        kernel,
        out_shape=tuple(jax.ShapeDtypeStruct(shape, kind) for shape, kind in shapes),
        in_specs=[
            pl.BlockSpec(memory_space=pltpu.SMEM if i in smem else pltpu.VMEM) for i in range(len(args))
        ],
        out_specs=tuple(pl.BlockSpec(memory_space=pltpu.VMEM) for _ in outs),
        cost_estimate=pl.CostEstimate(flops=int(cost * 1e9), bytes_accessed=1 << 20, transcendentals=0),
        compiler_params=pltpu.CompilerParams(vmem_limit_bytes=24 << 20),
    )(*args)


def swap(x, axis, apart):
    return lax.ppermute(x, axis, [(i, i ^ 1 << apart) for i in range(lax.axis_size(axis))])


def far_scan(section, count, place):
    def dot(left, right):
        return jnp.dot(left, right, precision=lax.Precision.HIGHEST)

    width = section.shape[1]
    own_map, own = section[:width], section[width:]
    ahead_map, ahead = jnp.eye(width, dtype=F32), jnp.zeros_like(own)
    for bit in range(count.bit_length() - 2):
        got = swap(jnp.concatenate([own_map, own], 0), "seq", bit)
        got_map, got = got[:width], got[width:]
        low = (place >> bit) % 2 == 0
        ahead = jnp.where(low, dot(ahead_map, got) + ahead, ahead)
        ahead_map = jnp.where(low, dot(ahead_map, got_map), ahead_map)
        low_map, high_map = jnp.where(low, own_map, got_map), jnp.where(low, got_map, own_map)
        own = dot(low_map, jnp.where(low, got, own)) + jnp.where(low, own, got)
        own_map = dot(low_map, high_map)
    return own, jnp.concatenate([ahead_map, ahead], 0)


def per_device(queries, key_rows, values, log_decay, beta_rate, start_states, output_grad):
    count = lax.axis_size("seq")
    stages = count.bit_length() - 1
    assert count == 1 << stages and stages >= 2
    place = lax.axis_index("seq")
    parity = lax.axis_index("head") % 2
    q_t, k_t = queries.T, key_rows.T
    half, length = q_t.shape
    width = 2 * half
    depth = values.shape[1]
    start = start_states[0, 0]
    square, tall, wide = (length, length), (length, depth), (width, length)
    state = (width, depth)
    (pack,) = call(
        pack_kernel, [((width + length // 2 + 16, length), BF16)], q_t, k_t, output_grad, log_decay, beta_rate
    )
    pack = swap(pack, "head", 0)
    start_b = swap(start, "head", 0)
    values_b = swap(values, "head", 0)
    low_first = 1 - place % 2 if stages == 2 else place * 0 + 1
    low_last = 1 - (place >> (stages - 1)) % 2
    flags = jnp.stack([low_first, low_last, 1 - parity] + [parity] * 5).astype(F32)
    spread, spread_t, damp, kk_own, kq_own, rows, mask = call(
        prep_kernel, [square, square, square, square, square, (4, length), (8, depth)],
        flags, q_t, k_t, log_decay, beta_rate, smem=(0,),
    )
    section, inv, inv_b, score_g, score_g_b, kk, damp_b, spread_b, rows_b, scale = call(
        map_kernel,
        [(4 * width, depth), square, square, tall, tall, square, square, square, (4, length), (4, length)],
        q_t, k_t, pack, output_grad, kk_own, kq_own, damp, spread_t, rows,
    )
    if stages == 2:
        ahead = swap(section, "seq", 0)
        (total,) = call(join_kernel, [(2 * width, depth)], mask, section, ahead)
    else:
        scans = [far_scan(part, count, place) for part in (section[: 2 * width], section[2 * width :])]
        total, ahead = (jnp.concatenate(both, 0) for both in zip(*scans))
    arrived = swap(total, "seq", stages - 1)
    base, u, u_b, psi, psi_b, start_t, start_t_b = call(
        update_kernel, [tall, tall, tall, wide, wide, state, state],
        mask, k_t, pack, values, values_b, start, start_b, inv, inv_b, rows, rows_b, scale,
    )
    shapes = [(depth, length), (length + width, depth), (length + width, width), wide, wide]
    packs = [(shape, BF16) for shape in [wide] + shapes + shapes for _ in range(2)]
    *packs, query_grad = call(
        local_kernel, packs + [square, square, tall, tall, wide, (half, length)],
        mask, q_t, k_t, pack, output_grad, inv, inv_b, score_g, score_g_b, kk, damp, damp_b, spread, spread_b, rows, rows_b,
        scale, base, u, u_b, psi, psi_b, start_t, start_t_b, ahead, total,
    )
    key_grad, value_grad, rate_grad = call(
        far_kernel, [(half, length), tall, (1, length)], mask, arrived, k_t, pack, rows, rows_b, scale, *packs
    )
    return (query_grad.T, key_grad.T, value_grad, rate_grad)


def solution(mesh):
    in_specs = (
        P("seq", "head"),
        P("seq", "head"),
        P("seq", "head"),
        P("head", "seq"),
        P("head", "seq"),
        P("seq", "head", None, None),
        P("seq", "head"),
    )
    out_specs = (P("seq", "head"), P("seq", "head"), P("seq", "head"), P("head", "seq"))

    return jax.shard_map(per_device, mesh=mesh, in_specs=in_specs, out_specs=out_specs, check_vma=False)
```

```python
import jax
import jax.numpy as jnp
from jax import lax
from jax.experimental import pallas as pl
from jax.experimental.pallas import tpu as pltpu
from jax.sharding import PartitionSpec as P

F32 = jnp.float32
BF16 = jnp.bfloat16
BASE = 32
PACK = 128
NN = (((1,), (0,)), ((), ()))
NT = (((1,), (1,)), ((), ()))


def split(x):
    high = x.astype(BF16)
    return (high, (x - high.astype(F32)).astype(BF16))


def mm(left, right, dims=NN):
    left = left if isinstance(left, tuple) else (left if left.dtype == BF16 else split(left))
    right = right if isinstance(right, tuple) else (right if right.dtype == BF16 else split(right))
    deep, out = (0, 1) if dims is NN else (1, 0)

    def one(a, b):
        return lax.dot_general(a, b, dims, preferred_element_type=F32)

    def join(parts, axis):
        return jnp.concatenate(parts, axis)

    pair_left, pair_right = isinstance(left, tuple), isinstance(right, tuple)
    shape = (right[0] if pair_right else right).shape
    shallow, thin = shape[deep] == PACK, shape[out] == PACK
    rows = (left[0] if pair_left else left).shape[0]
    if pair_left and pair_right:
        high, low = right
        if shallow and thin:
            block = join([join([high, low], out), join([high, jnp.zeros_like(low)], out)], deep)
            both = one(join(left, 1), block)
            return both[:, :PACK] + both[:, PACK:]
        if shallow:
            return one(join(left, 1), join([high, high], deep)) + one(left[0], low)
        if thin:
            both = one(join(left, 0), join(right, out))
            return both[:rows, :PACK] + (both[:rows, PACK:] + both[rows:, :PACK])
        both = one(join(left, 0), high)
        return both[:rows] + (both[rows:] + one(left[0], low))
    if pair_left:
        if shallow:
            return one(join(left, 1), join([right, right], deep))
        both = one(join(left, 0), right)
        return both[:rows] + both[rows:]
    if pair_right:
        if shallow:
            return one(join([left, left], 1), join(right, deep))
        if thin:
            both = one(left, join(right, out))
            return both[:, :PACK] + both[:, PACK:]
        return one(left, right[0]) + one(left, right[1])
    return one(left, right)


def ids(shape):
    return lax.broadcasted_iota(jnp.int32, shape, 0), lax.broadcasted_iota(jnp.int32, shape, 1)


def to_col(row, eye):
    return jnp.sum(jnp.where(eye, row, 0.0), 1, keepdims=True)


def to_row(col, eye):
    return jnp.sum(jnp.where(eye, col, 0.0), 0, keepdims=True)


def base_inverse(nil, base):
    size = nil.shape[0]
    count = size // base
    _, lane = ids((base, size))
    block = lane // base
    packed = jnp.zeros((base, size), F32)
    for b in range(count):
        packed = jnp.where(block == b, nil[b * base : (b + 1) * base, :], packed)
    row, lane = ids((8, size))
    first = lane // base * base
    tiles = range(base // 8)
    parts = [packed[8 * t : 8 * t + 8, :] for t in tiles]
    solved = [jnp.where(row + 8 * t == lane - first, 1.0, 0.0) for t in tiles]
    for j in range(base - 1):
        source = solved[j // 8][j % 8 : j % 8 + 1, :]
        for t in tiles[(j + 1) // 8 :]:
            factor = jnp.take_along_axis(parts[t], first + j, axis=1)
            if t == j // 8:
                factor = jnp.where(row + 8 * t > j, factor, 0.0)
            solved[t] = solved[t] + factor * source
    solved = jnp.concatenate(solved, 0)
    return jnp.concatenate([jnp.where(block == b, solved, 0.0) for b in range(count)], 0)


def inverses(nils, keys, corner):
    size = nils[0].shape[0]
    row, lane = ids((size, size))
    found = [base_inverse(nil, BASE) for nil in nils]
    width = BASE
    while True:
        factor = 4 if size >= 4 * width else 2
        wide = width * factor
        off = (row // wide == lane // wide) & (row // width != lane // width)
        known = [split(inv) for inv in found]
        steps = [split(mm(inv, jnp.where(off, nil, 0.0))) for inv, nil in zip(known, nils)]
        if wide == size:
            moved = [mm(key, inv, NT) for key, inv in zip(keys, known)]
            below = mm(known[1], corner)
            moved = [m + mm(m, step, NT) for m, step in zip(moved, steps)]
            below = below + mm(steps[1], below)
        found = [inv + mm(step, pair) for inv, step, pair in zip(found, steps, known)]
        if factor == 4:
            steps = [split(mm(step, step)) for step in steps]
            if wide == size:
                moved = [m + mm(m, step, NT) for m, step in zip(moved, steps)]
                below = below + mm(steps[1], below)
            found = [inv + mm(step, inv) for inv, step in zip(found, steps)]
        if wide == size:
            return found, moved, below
        width = wide


def decays(decay_row, row, lane):
    cum_col = jnp.sum(jnp.where(lane <= row, decay_row, 0.0), 1, keepdims=True)
    return cum_col, to_row(cum_col, row == lane)


def prep_kernel(
    flag_ref, q_ref, k_ref, decay_ref, rate_ref, spread_ref, spread_t_ref, damp_ref, kk_ref, kq_ref, rows_ref, mask_ref,
):
    length = q_ref.shape[1]
    row, lane = ids((length, length))
    cum_col, cum_row = decays(decay_ref[...], row, lane)
    rate_row = rate_ref[...]
    apart = cum_col - cum_row
    spread = jnp.exp(jnp.where(lane <= row, apart, -1e30))
    spread_ref[...] = spread
    spread_t_ref[...] = jnp.exp(jnp.where(lane >= row, -apart, -1e30))
    damp_ref[...] = jnp.where(lane < row, spread, 0.0) * -to_col(rate_row, row == lane)
    k_f, q_f = k_ref[...].astype(F32), q_ref[...].astype(F32)
    k_rows = k_f.T.astype(BF16)
    kk_ref[...] = mm(k_rows, k_ref[...])
    kq_ref[...] = mm(k_rows, q_ref[...])
    grow = jnp.exp(cum_row)
    tail = jnp.exp(cum_row[:, length - 1 :] - cum_row)
    k_sum = jnp.sum(k_f * k_f, 0, keepdims=True)
    q_sum = jnp.sum(q_f * q_f, 0, keepdims=True)
    rows_ref[...] = jnp.concatenate([cum_row, grow, tail, rate_row, k_sum, q_sum, cum_row, cum_row], 0)
    mask_ref[...] = jnp.concatenate([jnp.full((1, mask_ref.shape[1]), flag_ref[i], F32) for i in range(8)], 0)


def inverse_kernel(k_ref, other_ref, kk_in_ref, damp_ref, rows_ref, inv_ref, w_ref, kk_ref, scale_ref, other_rows_ref):
    other = other_ref[...]
    other_f = other.astype(F32)
    other_rows = other_f.T.astype(BF16)
    kk = kk_in_ref[...] + mm(other_rows, other)
    k_t = jnp.concatenate([k_ref[...], other], 0)
    mid = k_t.shape[1] // 2
    grow, rate_row, k_sum = (rows_ref[i : i + 1, :] for i in (1, 3, 4))
    square = k_sum + jnp.sum(other_f * other_f, 0, keepdims=True) + 1e-6
    k_scale = 1.0 / jnp.sqrt(square)
    nil = damp_ref[...] * (kk * (k_scale * k_scale))
    keys = k_t.astype(F32) * (rate_row * grow)
    (upper, lower), (first, second), below = inverses(
        [nil[:mid, :mid], nil[mid:, mid:]], [keys[:, :mid], keys[:, mid:]], nil[mid:, :mid]
    )
    below = split(below)
    second = second + mm(first, below, NT)
    w_ref[...] = jnp.concatenate([first, second], 1) * (k_scale * k_scale)
    inv_ref[0:mid, :] = jnp.concatenate([upper, jnp.zeros_like(upper)], 1)
    inv_ref[mid:, :] = jnp.concatenate([mm(below, upper), lower], 1)
    kk_ref[...] = kk
    scale_ref[...] = jnp.concatenate([k_scale, square * k_scale], 0)
    other_rows_ref[...] = other_rows


def shift_kernel(
    q_ref, other_ref, k_ref, k_other_ref, k_rows_ref, g_ref, kq_ref, spread_t_ref, rows_ref, w_ref,
    map_ref, score_g_ref, q_scale_ref,
):
    other = other_ref[...]
    kq = kq_ref[...] + mm(k_rows_ref[...], other)
    other_f = other.astype(F32)
    k_t = jnp.concatenate([k_ref[...], k_other_ref[...]], 0)
    q_f = jnp.concatenate([q_ref[...].astype(F32), other_f], 0)
    width, length = k_t.shape
    grow, tail = rows_ref[1:2, :], rows_ref[2:3, :]
    q_sum = rows_ref[5:6, :] + jnp.sum(other_f * other_f, 0, keepdims=True)
    q_scale = width ** (-0.5) / jnp.sqrt(q_sum + 1e-6)
    grad = g_ref[...]
    score_g = mm(spread_t_ref[...] * (kq * q_scale), grad)
    w_t = w_ref[...]
    w_row, w_lane = ids((width, width))
    direct = mm(q_f * (q_scale * grow), grad)
    map_ref[0:width, :] = jnp.where(w_row == w_lane, grow[:, length - 1 :], 0.0) - mm(w_t * tail, k_t, NT)
    map_ref[width:, :] = direct - mm(w_t, score_g)
    score_g_ref[...] = score_g
    q_scale_ref[...] = q_scale


def join_kernel(mask_ref, own_ref, got_ref, total_ref):
    width = own_ref.shape[1]
    low = mask_ref[0:1, :] > 0.0
    own, got = own_ref[width:, :], got_ref[width:, :]
    first = jnp.where(low, own_ref[0:width, :], got_ref[0:width, :])
    total_ref[...] = mm(first, jnp.where(low, got, own)) + jnp.where(low, own, got)


def update_kernel(
    mask_ref, q_ref, q_other_ref, k_ref, k_other_ref, v_ref, g_ref, start_ref, inv_ref, spread_ref, rows_ref, scale_ref,
    q_scale_ref, u_ref, base_ref, score_grad_ref, start_t_ref, keep_ref, send_ref,
):
    half, length = q_ref.shape
    q_f = jnp.concatenate([q_ref[...], q_other_ref[...]], 0).astype(F32)
    k_t = jnp.concatenate([k_ref[...], k_other_ref[...]], 0)
    width = k_t.shape[0]
    row, lane = ids((length, length))
    eye = row == lane
    grow, rate_row = rows_ref[1:2, :], rows_ref[3:4, :]
    k_scale, k_norm = scale_ref[0:1, :], scale_ref[1:2, :]
    start = start_ref[...]
    start = jnp.where(mask_ref[2:3, :] > 0.0, start, pltpu.roll(start, half, 1))
    start_t = start.T
    grad = g_ref[...]
    grad_t = grad.astype(F32).T.astype(BF16)
    k_rows = k_t.astype(F32).T.astype(BF16)
    base = v_ref[...].astype(F32) - to_col(grow * k_scale, eye) * mm(k_rows, start, NT)
    u = to_col(k_scale, eye) * mm(inv_ref[...], to_col(k_norm * rate_row, eye) * base)
    score_grad = mm(grad, u, NT) * spread_ref[...]
    q_scale = q_scale_ref[...]
    dq = mm(k_t, score_grad * k_scale, NT) + grow * mm(start_t, grad_t)
    unit = q_f * (q_scale * width**0.5)
    dq = q_scale * (dq - unit * jnp.sum(unit * dq, 0, keepdims=True))
    keep_ref[...] = dq[0:half, :]
    send_ref[...] = dq[half:, :]
    u_ref[...] = u
    base_ref[...] = base
    score_grad_ref[...] = score_grad
    start_t_ref[...] = start_t


def local_kernel(
    mask_ref, q_ref, q_other_ref, k_ref, k_other_ref, start_t_ref, inv_ref, score_g_ref, damp_ref, rows_ref, scale_ref,
    q_scale_ref, u_ref, score_grad_ref, ahead_ref, after_ref,
    uth_ref, utl_ref, uh_ref, ul_ref, ph_ref, pl_ref, pth_ref, ptl_ref, gh_ref, gl_ref, kh_ref, kl_ref, sym_ref, y_ref, dk_ref,
):
    length = q_ref.shape[1]
    q_f = jnp.concatenate([q_ref[...], q_other_ref[...]], 0).astype(F32)
    k_t = jnp.concatenate([k_ref[...], k_other_ref[...]], 0)
    width = k_t.shape[0]
    eye = jnp.equal(*ids((length, length)))
    grow, tail, rate_row = (rows_ref[i : i + 1, :] for i in range(1, 4))
    k_scale, k_norm = scale_ref[0:1, :], scale_ref[1:2, :]
    low = mask_ref[0:1, :] > 0.0
    ahead_map = jnp.where(low, ahead_ref[0:width, :], jnp.where(jnp.equal(*ids((width, width))), 1.0, 0.0))
    ahead = jnp.where(low, ahead_ref[width:, :], 0.0)
    u = u_ref[...]
    u_ts = split(u.T)
    inv = inv_ref[...]
    damp = damp_ref[...]
    psi_t = mm(k_t, inv * to_col(tail * k_scale * k_scale, eye)) * k_norm
    du_t = score_g_ref[...].T * (k_scale * k_scale)
    psi_s = split(psi_t.T)
    y_t = mm(du_t, inv) * k_norm
    sym = damp + damp.T
    sym_ref[...] = sym
    y_t = y_t + mm(ahead.T, psi_t)
    map_s = split(ahead_map)
    psi_far = mm(psi_s, map_s)
    uz_t = mm(ahead, u_ts)
    y = y_t.T
    y_ref[...] = y
    start_t = start_t_ref[...]
    start_s = split(start_t)
    inner = damp * mm(y, u_ts)
    k_s = split(k_t.astype(F32) * k_scale)
    dk = mm(q_f * q_scale_ref[...], score_grad_ref[...]) - mm(start_s, y_t * (grow * rate_row)) + tail * uz_t
    psi_far_s = split(psi_far)
    psi_far_t = psi_far.T
    ph_ref[0:length, :], pl_ref[0:length, :] = psi_far_s
    ph_ref[length:, :], pl_ref[length:, :] = map_s
    pth_ref[...], ptl_ref[...] = split(psi_far_t)
    gh_ref[...], gl_ref[...] = split(psi_far_t * (grow * rate_row))
    dk_ref[...] = dk + mm(k_s, inner + inner.T)
    uth_ref[...], utl_ref[...] = u_ts
    uh_ref[0:length, :], ul_ref[0:length, :] = split(u)
    uh_ref[length:, :], ul_ref[length:, :] = start_s
    kh_ref[...], kl_ref[...] = k_s


def far_kernel(
    mask_ref, got_ref, k_ref, k_other_ref, rows_ref, scale_ref,
    uth_ref, utl_ref, uh_ref, ul_ref, ph_ref, pl_ref, pth_ref, ptl_ref, gh_ref, gl_ref, kh_ref, kl_ref, sym_ref, dk_ref,
    send_ref, keep_ref,
):
    half, length = k_ref.shape
    k_scale = scale_ref[0:1, :]
    row, lane = ids((length, length))
    got_s = split(jnp.where(mask_ref[1:2, :] > 0.0, got_ref[...], 0.0))
    gu_s = split(mm(got_s, (uth_ref[...], utl_ref[...])))
    right = mm((uh_ref[...], ul_ref[...]), got_s, NT)
    upper = mm(right[0:length, :], (pth_ref[...], ptl_ref[...]))
    left = mm((ph_ref[...], pl_ref[...]), gu_s)
    inner = sym_ref[...] * jnp.where(lane < row, left[0:length, :], upper)
    dk = dk_ref[...] + rows_ref[2:3, :] * left[length:, :] - mm(right[length:, :], (gh_ref[...], gl_ref[...]))
    dk = dk + mm((kh_ref[...], kl_ref[...]), inner)
    unit = jnp.concatenate([k_ref[...], k_other_ref[...]], 0).astype(F32) * k_scale
    dk = k_scale * (dk - unit * jnp.sum(unit * dk, 0, keepdims=True))
    send_ref[...] = dk[half:, :]
    keep_ref[...] = dk[0:half, :]


def value_kernel(
    mask_ref, got_ref, ph_ref, pl_ref, y_ref, base_ref, kk_ref, spread_ref, scale_ref, rows_ref, u_ref, keep_ref, got_q_ref,
    value_ref, rate_out_ref, q_ref,
):
    length = y_ref.shape[0]
    row, lane = ids((length, length))
    eye = row == lane
    k_scale = scale_ref[0:1, :]
    got = jnp.where(mask_ref[1:2, :] > 0.0, got_ref[...], 0.0)
    low = jnp.where(lane < row, spread_ref[...] * kk_ref[...], 0.0) * (to_col(k_scale, eye) * k_scale)
    y = y_ref[...] + mm((ph_ref[0:length, :], pl_ref[0:length, :]), got)
    write = base_ref[...] - mm(low, u_ref[...])
    value_ref[...] = to_col(rows_ref[3:4, :], eye) * y
    rate_out_ref[...] = to_row(jnp.sum(y * write, 1, keepdims=True), eye)
    q_ref[...] = keep_ref[...] + got_q_ref[...]


def add_kernel(keep_ref, got_ref, k_ref):
    k_ref[...] = keep_ref[...] + got_ref[...]


def call(kernel, outs, *args, smem=(), cost=1.0):
    shapes = [out if isinstance(out[0], tuple) else (out, F32) for out in outs]
    return pl.pallas_call(
        kernel,
        out_shape=tuple(jax.ShapeDtypeStruct(shape, kind) for shape, kind in shapes),
        in_specs=[
            pl.BlockSpec(memory_space=pltpu.SMEM if i in smem else pltpu.VMEM) for i in range(len(args))
        ],
        out_specs=tuple(pl.BlockSpec(memory_space=pltpu.VMEM) for _ in outs),
        cost_estimate=pl.CostEstimate(flops=int(cost * 1e9), bytes_accessed=1 << 20, transcendentals=0),
        compiler_params=pltpu.CompilerParams(vmem_limit_bytes=24 << 20),
    )(*args)


def swap(x, axis, apart):
    return lax.ppermute(x, axis, [(i, i ^ 1 << apart) for i in range(lax.axis_size(axis))])


def far_scan(section, count, place):
    def dot(left, right):
        return jnp.dot(left, right, precision=lax.Precision.HIGHEST)

    width = section.shape[1]
    own_map, own = section[:width], section[width:]
    ahead_map, ahead = jnp.eye(width, dtype=F32), jnp.zeros_like(own)
    for bit in range(count.bit_length() - 2):
        got = swap(jnp.concatenate([own_map, own], 0), "seq", bit)
        got_map, got = got[:width], got[width:]
        low = (place >> bit) % 2 == 0
        ahead = jnp.where(low, dot(ahead_map, got) + ahead, ahead)
        ahead_map = jnp.where(low, dot(ahead_map, got_map), ahead_map)
        low_map, high_map = jnp.where(low, own_map, got_map), jnp.where(low, got_map, own_map)
        own = dot(low_map, jnp.where(low, got, own)) + jnp.where(low, own, got)
        own_map = dot(low_map, high_map)
    return own, jnp.concatenate([ahead_map, ahead], 0)


def per_device(queries, key_rows, values, log_decay, beta_rate, start_states, output_grad):
    count = lax.axis_size("seq")
    stages = count.bit_length() - 1
    assert count == 1 << stages and stages >= 2
    place = lax.axis_index("seq")
    parity = lax.axis_index("head") % 2
    q_t, k_t = queries.T, key_rows.T
    half, length = q_t.shape
    width = 2 * half
    depth = values.shape[1]
    start = start_states[0, 0]
    square, tall, wide, thin = (length, length), (length, depth), (width, length), (1, length)
    k_other = swap(k_t, "head", 0)
    q_other = swap(q_t, "head", 0)
    low_first = 1 - place % 2 if stages == 2 else place * 0 + 1
    low_last = 1 - (place >> (stages - 1)) % 2
    flags = jnp.stack([low_first, low_last, 1 - parity] + [parity] * 5).astype(F32)
    spread, spread_t, damp, kk_own, kq_own, rows, mask = call(
        prep_kernel, [square, square, square, square, square, (8, length), (8, depth)],
        flags, q_t, k_t, log_decay, beta_rate, smem=(0,),
    )
    inv, w_t, kk, scale, k_rows = call(
        inverse_kernel, [square, wide, square, (2, length), ((length, half), BF16)], k_t, k_other, kk_own, damp, rows
    )
    section, score_g, q_scale = call(
        shift_kernel, [(2 * width, depth), tall, thin],
        q_t, q_other, k_t, k_other, k_rows, output_grad, kq_own, spread_t, rows, w_t,
    )
    if stages == 2:
        ahead = swap(section, "seq", 0)
        (total,) = call(join_kernel, [(width, depth)], mask, section, ahead)
    else:
        total, ahead = far_scan(section, count, place)
    arrived = swap(total, "seq", stages - 1)
    u, base, score_grad, start_t, keep_q, send_q = call(
        update_kernel, [tall, tall, square, (width, depth), (half, length), (half, length)],
        mask, q_t, q_other, k_t, k_other, values, output_grad, start, inv, spread, rows, scale, q_scale,
    )
    got_q = swap(send_q, "head", 0)
    shapes = [(depth, length), (length + width, depth), (length + width, width), wide, wide, wide]
    *packs, sym, y, dk = call(
        local_kernel, [(shape, BF16) for shape in shapes for _ in range(2)] + [square, tall, wide],
        mask, q_t, q_other, k_t, k_other, start_t, inv, score_g, damp, rows, scale, q_scale, u, score_grad, ahead,
        total,
    )
    send, keep = call(
        far_kernel, [(half, length), (half, length)],
        mask, arrived, k_t, k_other, rows, scale, *packs, sym, dk,
    )
    got_k = swap(send, "head", 0)
    value_grad, rate_grad, query_grad = call(
        value_kernel, [tall, thin, (half, length)],
        mask, arrived, packs[4], packs[5], y, base, kk, spread, scale, rows, u, keep_q, got_q,
    )
    (key_grad,) = call(add_kernel, [(half, length)], keep, got_k)
    return (query_grad.T, key_grad.T, value_grad, rate_grad)


def solution(mesh):
    in_specs = (
        P("seq", "head"),
        P("seq", "head"),
        P("seq", "head"),
        P("head", "seq"),
        P("head", "seq"),
        P("seq", "head", None, None),
        P("seq", "head"),
    )
    out_specs = (P("seq", "head"), P("seq", "head"), P("seq", "head"), P("head", "seq"))

    return jax.shard_map(per_device, mesh=mesh, in_specs=in_specs, out_specs=out_specs, check_vma=False)
```

```python
import jax
import jax.numpy as jnp
from jax import lax
from jax.experimental import pallas as pl
from jax.experimental.pallas import tpu as pltpu
from jax.sharding import PartitionSpec as P

F32 = jnp.float32
BF16 = jnp.bfloat16
BASE = 32
PACK = 128
NN = (((1,), (0,)), ((), ()))
NT = (((1,), (1,)), ((), ()))


def split(x):
    high = x.astype(BF16)
    return (high, (x - high.astype(F32)).astype(BF16))


def mm(left, right, dims=NN):
    left = left if isinstance(left, tuple) else (left if left.dtype == BF16 else split(left))
    right = right if isinstance(right, tuple) else (right if right.dtype == BF16 else split(right))
    deep, out = (0, 1) if dims is NN else (1, 0)

    def one(a, b):
        return lax.dot_general(a, b, dims, preferred_element_type=F32)

    def join(parts, axis):
        return jnp.concatenate(parts, axis)

    pair_left, pair_right = isinstance(left, tuple), isinstance(right, tuple)
    shape = (right[0] if pair_right else right).shape
    shallow, thin = shape[deep] == PACK, shape[out] == PACK
    rows = (left[0] if pair_left else left).shape[0]
    if pair_left and pair_right:
        high, low = right
        if shallow and thin:
            block = join([join([high, low], out), join([high, jnp.zeros_like(low)], out)], deep)
            both = one(join(left, 1), block)
            return both[:, :PACK] + both[:, PACK:]
        if shallow:
            return one(join(left, 1), join([high, high], deep)) + one(left[0], low)
        if thin:
            both = one(join(left, 0), join(right, out))
            return both[:rows, :PACK] + (both[:rows, PACK:] + both[rows:, :PACK])
        both = one(join(left, 0), high)
        return both[:rows] + (both[rows:] + one(left[0], low))
    if pair_left:
        if shallow:
            return one(join(left, 1), join([right, right], deep))
        both = one(join(left, 0), right)
        return both[:rows] + both[rows:]
    if pair_right:
        if shallow:
            return one(join([left, left], 1), join(right, deep))
        if thin:
            both = one(left, join(right, out))
            return both[:, :PACK] + both[:, PACK:]
        return one(left, right[0]) + one(left, right[1])
    return one(left, right)


def ids(shape):
    return lax.broadcasted_iota(jnp.int32, shape, 0), lax.broadcasted_iota(jnp.int32, shape, 1)


def to_col(row, eye):
    return jnp.sum(jnp.where(eye, row, 0.0), 1, keepdims=True)


def to_row(col, eye):
    return jnp.sum(jnp.where(eye, col, 0.0), 0, keepdims=True)


def base_inverses(nils, base):
    size = nils[0].shape[0]
    count = size // base
    _, lane = ids((base, size))
    block = lane // base
    row, lane = ids((8, size))
    first = lane // base * base
    tiles = range(base // 8)
    parts, solved = [], []
    for nil in nils:
        packed = jnp.where(block == 0, nil[0:base, :], 0.0)
        for b in range(1, count):
            packed = jnp.where(block == b, nil[b * base : (b + 1) * base, :], packed)
        parts.append([packed[8 * t : 8 * t + 8, :] for t in tiles])
        solved.append([jnp.where(row + 8 * t == lane - first, 1.0, 0.0) for t in tiles])
    for j in range(base - 1):
        at = first + j
        for part, done in zip(parts, solved):
            source = done[j // 8][j % 8 : j % 8 + 1, :]
            for t in tiles[(j + 1) // 8 :]:
                factor = jnp.take_along_axis(part[t], at, axis=1)
                if t == j // 8:
                    factor = jnp.where(row + 8 * t > j, factor, 0.0)
                done[t] = done[t] + factor * source
    solved = [jnp.concatenate(done, 0) for done in solved]
    return [jnp.concatenate([jnp.where(block == b, done, 0.0) for b in range(count)], 0) for done in solved]


def inverses(nils, keys, corner):
    size = nils[0].shape[0]
    row, lane = ids((size, size))
    found = base_inverses(nils, BASE)
    width = BASE
    while True:
        factor = 4 if size >= 4 * width else 2
        wide = width * factor
        off = (row // wide == lane // wide) & (row // width != lane // width)
        known = [split(inv) for inv in found]
        steps = [split(mm(inv, jnp.where(off, nil, 0.0))) for inv, nil in zip(known, nils)]
        last = wide == size
        if last:
            moved = [mm(key, inv, NT) for key, inv in zip(keys, known)]
            below = mm(known[1], corner)
        twice = [split(mm(step, step)) for step in steps] if factor == 4 else []
        if last:
            below = below + mm(steps[1], below)
            moved = [m + mm(m, step, NT) for m, step in zip(moved, steps)]
        found = [inv + mm(step, pair) for inv, step, pair in zip(found, steps, known)]
        if last and twice:
            below = below + mm(twice[1], below)
            moved = [m + mm(m, step, NT) for m, step in zip(moved, twice)]
        if last:
            below = split(below)
            moved[1] = moved[1] + mm(moved[0], below, NT)
        if twice:
            found = [inv + mm(step, inv) for inv, step in zip(found, twice)]
        if last:
            return found, moved, below
        width = wide


def decays(decay_row, row, lane):
    cum_col = jnp.sum(jnp.where(lane <= row, decay_row, 0.0), 1, keepdims=True)
    return cum_col, to_row(cum_col, row == lane)


def prep_kernel(
    flag_ref, q_ref, k_ref, decay_ref, rate_ref, spread_ref, spread_t_ref, damp_ref, kk_ref, kq_ref, rows_ref, mask_ref,
):
    length = q_ref.shape[1]
    row, lane = ids((length, length))
    cum_col, cum_row = decays(decay_ref[...], row, lane)
    rate_row = rate_ref[...]
    apart = cum_col - cum_row
    spread = jnp.exp(jnp.where(lane <= row, apart, -1e30))
    spread_ref[...] = spread
    spread_t_ref[...] = jnp.exp(jnp.where(lane >= row, -apart, -1e30))
    damp_ref[...] = jnp.where(lane < row, spread, 0.0) * -to_col(rate_row, row == lane)
    k_f, q_f = k_ref[...].astype(F32), q_ref[...].astype(F32)
    k_rows = k_f.T.astype(BF16)
    kk_ref[...] = mm(k_rows, k_ref[...])
    kq_ref[...] = mm(k_rows, q_ref[...])
    grow = jnp.exp(cum_row)
    tail = jnp.exp(cum_row[:, length - 1 :] - cum_row)
    k_sum = jnp.sum(k_f * k_f, 0, keepdims=True)
    q_sum = jnp.sum(q_f * q_f, 0, keepdims=True)
    rows_ref[...] = jnp.concatenate([cum_row, grow, tail, rate_row, k_sum, q_sum, cum_row, cum_row], 0)
    mask_ref[...] = jnp.concatenate([jnp.full((1, mask_ref.shape[1]), flag_ref[i], F32) for i in range(8)], 0)


def inverse_kernel(k_ref, other_ref, kk_in_ref, damp_ref, rows_ref, inv_ref, w_ref, kk_ref, scale_ref, other_rows_ref):
    other = other_ref[...]
    other_f = other.astype(F32)
    other_rows = other_f.T.astype(BF16)
    k_t = jnp.concatenate([k_ref[...], other], 0)
    mid = k_t.shape[1] // 2
    grow, rate_row, k_sum = (rows_ref[i : i + 1, :] for i in (1, 3, 4))
    square = k_sum + jnp.sum(other_f * other_f, 0, keepdims=True) + 1e-6
    k_scale = 1.0 / jnp.sqrt(square)
    both = k_scale * k_scale
    upper = kk_in_ref[0:mid, 0:mid] + mm(other_rows[0:mid, :], other[:, 0:mid])
    lower = kk_in_ref[mid:, :] + mm(other_rows[mid:, :], other)
    kk_ref[0:mid, 0:mid] = upper
    kk_ref[0:mid, mid:] = jnp.zeros_like(upper)
    kk_ref[mid:, :] = lower
    upper = damp_ref[0:mid, 0:mid] * (upper * both[:, 0:mid])
    lower = damp_ref[mid:, :] * (lower * both)
    keys = k_t.astype(F32) * (rate_row * grow)
    (upper, lower), moved, below = inverses(
        [upper, lower[:, mid:]], [keys[:, :mid], keys[:, mid:]], lower[:, :mid]
    )
    w_ref[...] = jnp.concatenate(moved, 1) * both
    inv_ref[0:mid, :] = jnp.concatenate([upper, jnp.zeros_like(upper)], 1)
    inv_ref[mid:, :] = jnp.concatenate([mm(below, upper), lower], 1)
    scale_ref[...] = jnp.concatenate([k_scale, square * k_scale], 0)
    other_rows_ref[...] = other_rows


def shift_kernel(
    q_ref, other_ref, k_ref, k_other_ref, k_rows_ref, g_ref, kq_ref, spread_t_ref, rows_ref, w_ref,
    map_ref, score_g_ref, q_scale_ref,
):
    other = other_ref[...]
    kq = kq_ref[...] + mm(k_rows_ref[...], other)
    other_f = other.astype(F32)
    k_t = jnp.concatenate([k_ref[...], k_other_ref[...]], 0)
    q_f = jnp.concatenate([q_ref[...].astype(F32), other_f], 0)
    width, length = k_t.shape
    grow, tail = rows_ref[1:2, :], rows_ref[2:3, :]
    q_sum = rows_ref[5:6, :] + jnp.sum(other_f * other_f, 0, keepdims=True)
    q_scale = width ** (-0.5) / jnp.sqrt(q_sum + 1e-6)
    grad = g_ref[...]
    score_g = mm(spread_t_ref[...] * (kq * q_scale), grad)
    w_t = w_ref[...]
    w_row, w_lane = ids((width, width))
    direct = mm(q_f * (q_scale * grow), grad)
    map_ref[0:width, :] = jnp.where(w_row == w_lane, grow[:, length - 1 :], 0.0) - mm(w_t * tail, k_t, NT)
    map_ref[width:, :] = direct - mm(w_t, score_g)
    score_g_ref[...] = score_g
    q_scale_ref[...] = q_scale


def join_kernel(mask_ref, own_ref, got_ref, total_ref):
    width = own_ref.shape[1]
    low = mask_ref[0:1, :] > 0.0
    own, got = own_ref[width:, :], got_ref[width:, :]
    first = jnp.where(low, own_ref[0:width, :], got_ref[0:width, :])
    total_ref[...] = mm(first, jnp.where(low, got, own)) + jnp.where(low, own, got)


def update_kernel(
    mask_ref, q_ref, q_other_ref, k_ref, k_other_ref, v_ref, g_ref, start_ref, inv_ref, spread_ref, rows_ref, scale_ref,
    q_scale_ref, u_ref, base_ref, score_grad_ref, start_t_ref, keep_ref, send_ref,
):
    half, length = q_ref.shape
    q_f = jnp.concatenate([q_ref[...], q_other_ref[...]], 0).astype(F32)
    k_t = jnp.concatenate([k_ref[...], k_other_ref[...]], 0)
    width = k_t.shape[0]
    row, lane = ids((length, length))
    eye = row == lane
    grow, rate_row = rows_ref[1:2, :], rows_ref[3:4, :]
    k_scale, k_norm = scale_ref[0:1, :], scale_ref[1:2, :]
    start = start_ref[...]
    start = jnp.where(mask_ref[2:3, :] > 0.0, start, pltpu.roll(start, half, 1))
    start_t = start.T
    grad = g_ref[...]
    grad_t = grad.astype(F32).T.astype(BF16)
    k_rows = k_t.astype(F32).T.astype(BF16)
    base = v_ref[...].astype(F32) - to_col(grow * k_scale, eye) * mm(k_rows, start, NT)
    u = to_col(k_scale, eye) * mm(inv_ref[...], to_col(k_norm * rate_row, eye) * base)
    score_grad = mm(grad, u, NT) * spread_ref[...]
    q_scale = q_scale_ref[...]
    dq = mm(k_t, score_grad * k_scale, NT) + grow * mm(start_t, grad_t)
    unit = q_f * (q_scale * width**0.5)
    dq = q_scale * (dq - unit * jnp.sum(unit * dq, 0, keepdims=True))
    keep_ref[...] = dq[0:half, :]
    send_ref[...] = dq[half:, :]
    u_ref[...] = u
    base_ref[...] = base
    score_grad_ref[...] = score_grad
    start_t_ref[...] = start_t


def local_kernel(
    mask_ref, q_ref, q_other_ref, k_ref, k_other_ref, start_t_ref, inv_ref, score_g_ref, damp_ref, rows_ref, scale_ref,
    q_scale_ref, u_ref, score_grad_ref, ahead_ref, after_ref,
    uth_ref, utl_ref, uh_ref, ul_ref, ph_ref, pl_ref, pth_ref, ptl_ref, gh_ref, gl_ref, kh_ref, kl_ref, sym_ref, y_ref, dk_ref,
):
    length = q_ref.shape[1]
    q_f = jnp.concatenate([q_ref[...], q_other_ref[...]], 0).astype(F32)
    k_t = jnp.concatenate([k_ref[...], k_other_ref[...]], 0)
    width = k_t.shape[0]
    eye = jnp.equal(*ids((length, length)))
    grow, tail, rate_row = (rows_ref[i : i + 1, :] for i in range(1, 4))
    k_scale, k_norm = scale_ref[0:1, :], scale_ref[1:2, :]
    low = mask_ref[0:1, :] > 0.0
    ahead_map = jnp.where(low, ahead_ref[0:width, :], jnp.where(jnp.equal(*ids((width, width))), 1.0, 0.0))
    ahead = jnp.where(low, ahead_ref[width:, :], 0.0)
    u = u_ref[...]
    u_ts = split(u.T)
    inv = inv_ref[...]
    damp = damp_ref[...]
    psi_t = mm(k_t, inv * to_col(tail * k_scale * k_scale, eye)) * k_norm
    du_t = score_g_ref[...].T * (k_scale * k_scale)
    psi_s = split(psi_t.T)
    y_t = mm(du_t, inv) * k_norm
    sym = damp + damp.T
    sym_ref[...] = sym
    y_t = y_t + mm(ahead.T, psi_t)
    map_s = split(ahead_map)
    psi_far = mm(psi_s, map_s)
    uz_t = mm(ahead, u_ts)
    y = y_t.T
    y_ref[...] = y
    start_t = start_t_ref[...]
    start_s = split(start_t)
    inner = damp * mm(y, u_ts)
    k_s = split(k_t.astype(F32) * k_scale)
    dk = mm(q_f * q_scale_ref[...], score_grad_ref[...]) - mm(start_s, y_t * (grow * rate_row)) + tail * uz_t
    psi_far_s = split(psi_far)
    psi_far_t = psi_far.T
    ph_ref[0:length, :], pl_ref[0:length, :] = psi_far_s
    ph_ref[length:, :], pl_ref[length:, :] = map_s
    pth_ref[...], ptl_ref[...] = split(psi_far_t)
    gh_ref[...], gl_ref[...] = split(psi_far_t * (grow * rate_row))
    dk_ref[...] = dk + mm(k_s, inner + inner.T)
    uth_ref[...], utl_ref[...] = u_ts
    uh_ref[0:length, :], ul_ref[0:length, :] = split(u)
    uh_ref[length:, :], ul_ref[length:, :] = start_s
    kh_ref[...], kl_ref[...] = k_s


def far_kernel(
    mask_ref, got_ref, k_ref, k_other_ref, rows_ref, scale_ref,
    uth_ref, utl_ref, uh_ref, ul_ref, ph_ref, pl_ref, pth_ref, ptl_ref, gh_ref, gl_ref, kh_ref, kl_ref, sym_ref, dk_ref,
    send_ref, keep_ref,
):
    half, length = k_ref.shape
    k_scale = scale_ref[0:1, :]
    row, lane = ids((length, length))
    got_s = split(jnp.where(mask_ref[1:2, :] > 0.0, got_ref[...], 0.0))
    gu_s = split(mm(got_s, (uth_ref[...], utl_ref[...])))
    right = mm((uh_ref[...], ul_ref[...]), got_s, NT)
    upper = mm(right[0:length, :], (pth_ref[...], ptl_ref[...]))
    left = mm((ph_ref[...], pl_ref[...]), gu_s)
    inner = sym_ref[...] * jnp.where(lane < row, left[0:length, :], upper)
    dk = dk_ref[...] + rows_ref[2:3, :] * left[length:, :] - mm(right[length:, :], (gh_ref[...], gl_ref[...]))
    dk = dk + mm((kh_ref[...], kl_ref[...]), inner)
    unit = jnp.concatenate([k_ref[...], k_other_ref[...]], 0).astype(F32) * k_scale
    dk = k_scale * (dk - unit * jnp.sum(unit * dk, 0, keepdims=True))
    send_ref[...] = dk[half:, :]
    keep_ref[...] = dk[0:half, :]


def value_kernel(
    mask_ref, got_ref, ph_ref, pl_ref, y_ref, base_ref, kk_ref, spread_ref, scale_ref, rows_ref, u_ref, keep_ref, got_q_ref,
    value_ref, rate_out_ref, q_ref,
):
    length = y_ref.shape[0]
    row, lane = ids((length, length))
    eye = row == lane
    k_scale = scale_ref[0:1, :]
    got = jnp.where(mask_ref[1:2, :] > 0.0, got_ref[...], 0.0)
    low = jnp.where(lane < row, spread_ref[...] * kk_ref[...], 0.0) * (to_col(k_scale, eye) * k_scale)
    y = y_ref[...] + mm((ph_ref[0:length, :], pl_ref[0:length, :]), got)
    write = base_ref[...] - mm(low, u_ref[...])
    value_ref[...] = to_col(rows_ref[3:4, :], eye) * y
    rate_out_ref[...] = to_row(jnp.sum(y * write, 1, keepdims=True), eye)
    q_ref[...] = keep_ref[...] + got_q_ref[...]


def add_kernel(keep_ref, got_ref, k_ref):
    k_ref[...] = keep_ref[...] + got_ref[...]


def call(kernel, outs, *args, smem=(), cost=1.0):
    shapes = [out if isinstance(out[0], tuple) else (out, F32) for out in outs]
    return pl.pallas_call(
        kernel,
        out_shape=tuple(jax.ShapeDtypeStruct(shape, kind) for shape, kind in shapes),
        in_specs=[
            pl.BlockSpec(memory_space=pltpu.SMEM if i in smem else pltpu.VMEM) for i in range(len(args))
        ],
        out_specs=tuple(pl.BlockSpec(memory_space=pltpu.VMEM) for _ in outs),
        cost_estimate=pl.CostEstimate(flops=int(cost * 1e9), bytes_accessed=1 << 20, transcendentals=0),
        compiler_params=pltpu.CompilerParams(vmem_limit_bytes=24 << 20),
    )(*args)


def swap(x, axis, apart):
    return lax.ppermute(x, axis, [(i, i ^ 1 << apart) for i in range(lax.axis_size(axis))])


def far_scan(section, count, place):
    def dot(left, right):
        return jnp.dot(left, right, precision=lax.Precision.HIGHEST)

    width = section.shape[1]
    own_map, own = section[:width], section[width:]
    ahead_map, ahead = jnp.eye(width, dtype=F32), jnp.zeros_like(own)
    for bit in range(count.bit_length() - 2):
        got = swap(jnp.concatenate([own_map, own], 0), "seq", bit)
        got_map, got = got[:width], got[width:]
        low = (place >> bit) % 2 == 0
        ahead = jnp.where(low, dot(ahead_map, got) + ahead, ahead)
        ahead_map = jnp.where(low, dot(ahead_map, got_map), ahead_map)
        low_map, high_map = jnp.where(low, own_map, got_map), jnp.where(low, got_map, own_map)
        own = dot(low_map, jnp.where(low, got, own)) + jnp.where(low, own, got)
        own_map = dot(low_map, high_map)
    return own, jnp.concatenate([ahead_map, ahead], 0)


def per_device(queries, key_rows, values, log_decay, beta_rate, start_states, output_grad):
    count = lax.axis_size("seq")
    stages = count.bit_length() - 1
    assert count == 1 << stages and stages >= 2
    place = lax.axis_index("seq")
    parity = lax.axis_index("head") % 2
    q_t, k_t = queries.T, key_rows.T
    half, length = q_t.shape
    width = 2 * half
    depth = values.shape[1]
    start = start_states[0, 0]
    square, tall, wide, thin = (length, length), (length, depth), (width, length), (1, length)
    k_other = swap(k_t, "head", 0)
    q_other = swap(q_t, "head", 0)
    low_first = 1 - place % 2 if stages == 2 else place * 0 + 1
    low_last = 1 - (place >> (stages - 1)) % 2
    flags = jnp.stack([low_first, low_last, 1 - parity] + [parity] * 5).astype(F32)
    spread, spread_t, damp, kk_own, kq_own, rows, mask = call(
        prep_kernel, [square, square, square, square, square, (8, length), (8, depth)],
        flags, q_t, k_t, log_decay, beta_rate, smem=(0,),
    )
    inv, w_t, kk, scale, k_rows = call(
        inverse_kernel, [square, wide, square, (2, length), ((length, half), BF16)], k_t, k_other, kk_own, damp, rows
    )
    section, score_g, q_scale = call(
        shift_kernel, [(2 * width, depth), tall, thin],
        q_t, q_other, k_t, k_other, k_rows, output_grad, kq_own, spread_t, rows, w_t,
    )
    if stages == 2:
        ahead = swap(section, "seq", 0)
        (total,) = call(join_kernel, [(width, depth)], mask, section, ahead)
    else:
        total, ahead = far_scan(section, count, place)
    arrived = swap(total, "seq", stages - 1)
    u, base, score_grad, start_t, keep_q, send_q = call(
        update_kernel, [tall, tall, square, (width, depth), (half, length), (half, length)],
        mask, q_t, q_other, k_t, k_other, values, output_grad, start, inv, spread, rows, scale, q_scale,
    )
    got_q = swap(send_q, "head", 0)
    shapes = [(depth, length), (length + width, depth), (length + width, width), wide, wide, wide]
    *packs, sym, y, dk = call(
        local_kernel, [(shape, BF16) for shape in shapes for _ in range(2)] + [square, tall, wide],
        mask, q_t, q_other, k_t, k_other, start_t, inv, score_g, damp, rows, scale, q_scale, u, score_grad, ahead,
        total,
    )
    send, keep = call(
        far_kernel, [(half, length), (half, length)],
        mask, arrived, k_t, k_other, rows, scale, *packs, sym, dk,
    )
    got_k = swap(send, "head", 0)
    value_grad, rate_grad, query_grad = call(
        value_kernel, [tall, thin, (half, length)],
        mask, arrived, packs[4], packs[5], y, base, kk, spread, scale, rows, u, keep_q, got_q,
    )
    (key_grad,) = call(add_kernel, [(half, length)], keep, got_k)
    return (query_grad.T, key_grad.T, value_grad, rate_grad)


def solution(mesh):
    in_specs = (
        P("seq", "head"),
        P("seq", "head"),
        P("seq", "head"),
        P("head", "seq"),
        P("head", "seq"),
        P("seq", "head", None, None),
        P("seq", "head"),
    )
    out_specs = (P("seq", "head"), P("seq", "head"), P("seq", "head"), P("head", "seq"))

    return jax.shard_map(per_device, mesh=mesh, in_specs=in_specs, out_specs=out_specs, check_vma=False)
```

```python
import jax
import jax.numpy as jnp
from jax import lax
from jax.experimental import pallas as pl
from jax.experimental.pallas import tpu as pltpu
from jax.sharding import PartitionSpec as P

F32 = jnp.float32
BF16 = jnp.bfloat16
BASE = 16
PACK = 128
NN = (((1,), (0,)), ((), ()))
NT = (((1,), (1,)), ((), ()))
TN = (((0,), (0,)), ((), ()))


def split(x):
    high = x.astype(BF16)
    return (high, (x - high.astype(F32)).astype(BF16))


def mm(left, right, dims=NN):
    left = left if isinstance(left, tuple) else (left if left.dtype == BF16 else split(left))
    right = right if isinstance(right, tuple) else (right if right.dtype == BF16 else split(right))
    deep, out = (0, 1) if dims is NN else (1, 0)

    def one(a, b):
        return lax.dot_general(a, b, dims, preferred_element_type=F32)

    def join(parts, axis):
        return jnp.concatenate(parts, axis)

    pair_left, pair_right = isinstance(left, tuple), isinstance(right, tuple)
    shape = (right[0] if pair_right else right).shape
    shallow, thin = shape[deep] == PACK, shape[out] == PACK
    rows = (left[0] if pair_left else left).shape[0]
    if pair_left and pair_right:
        high, low = right
        if shallow and thin:
            block = join([join([high, low], out), join([high, jnp.zeros_like(low)], out)], deep)
            both = one(join(left, 1), block)
            return both[:, :PACK] + both[:, PACK:]
        if shallow:
            return one(join(left, 1), join([high, high], deep)) + one(left[0], low)
        if thin:
            both = one(join(left, 0), join(right, out))
            return both[:rows, :PACK] + (both[:rows, PACK:] + both[rows:, :PACK])
        both = one(join(left, 0), high)
        return both[:rows] + (both[rows:] + one(left[0], low))
    if pair_left:
        if shallow:
            return one(join(left, 1), join([right, right], deep))
        both = one(join(left, 0), right)
        return both[:rows] + both[rows:]
    if pair_right:
        if shallow:
            return one(join([left, left], 1), join(right, deep))
        if thin:
            both = one(left, join(right, out))
            return both[:, :PACK] + both[:, PACK:]
        return one(left, right[0]) + one(left, right[1])
    return one(left, right)


def ids(shape):
    return lax.broadcasted_iota(jnp.int32, shape, 0), lax.broadcasted_iota(jnp.int32, shape, 1)


def to_col(row, eye):
    return jnp.sum(jnp.where(eye, row, 0.0), 1, keepdims=True)


def to_row(col, eye):
    return jnp.sum(jnp.where(eye, col, 0.0), 0, keepdims=True)


def base_inverses(nils, base):
    size = nils[0].shape[0]
    count = size // base
    _, lane = ids((base, size))
    block = lane // base
    row, lane = ids((8, size))
    first = lane // base * base
    tiles = range(base // 8)
    parts, solved = [], []
    for nil in nils:
        packed = jnp.where(block == 0, nil[0:base, :], 0.0)
        for b in range(1, count):
            packed = jnp.where(block == b, nil[b * base : (b + 1) * base, :], packed)
        parts.append([packed[8 * t : 8 * t + 8, :] for t in tiles])
        solved.append([jnp.where(row + 8 * t == lane - first, 1.0, 0.0) for t in tiles])
    for j in range(base - 1):
        at = first + j
        for part, done in zip(parts, solved):
            source = done[j // 8][j % 8 : j % 8 + 1, :]
            for t in tiles[(j + 1) // 8 :]:
                factor = jnp.take_along_axis(part[t], at, axis=1)
                if t == j // 8:
                    factor = jnp.where(row + 8 * t > j, factor, 0.0)
                done[t] = done[t] + factor * source
    solved = [jnp.concatenate(done, 0) for done in solved]
    return [jnp.concatenate([jnp.where(block == b, done, 0.0) for b in range(count)], 0) for done in solved]


def inverses(nils, keys, corner):
    size = nils[0].shape[0]
    row, lane = ids((size, size))
    found = base_inverses(nils, BASE)
    width = BASE
    while True:
        factor = 4 if size >= 4 * width else 2
        wide = width * factor
        off = (row // wide == lane // wide) & (row // width != lane // width)
        known = [split(inv) for inv in found]
        steps = [split(mm(inv, jnp.where(off, nil, 0.0))) for inv, nil in zip(known, nils)]
        last = wide == size
        if last:
            moved = [mm(key, inv, NT) for key, inv in zip(keys, known)]
            below = mm(known[1], corner)
        twice = [split(mm(step, step)) for step in steps] if factor == 4 else []
        if last:
            below = below + mm(steps[1], below)
            moved = [m + mm(m, step, NT) for m, step in zip(moved, steps)]
        found = [inv + mm(step, pair) for inv, step, pair in zip(found, steps, known)]
        if last and twice:
            below = below + mm(twice[1], below)
            moved = [m + mm(m, step, NT) for m, step in zip(moved, twice)]
        if last:
            moved[1] = moved[1] + mm(moved[0], below, NT)
        if twice:
            found = [inv + mm(step, inv) for inv, step in zip(found, twice)]
        if last:
            return found, moved, below
        width = wide


def decays(decay_row, row, lane):
    cum_col = jnp.sum(jnp.where(lane <= row, decay_row, 0.0), 1, keepdims=True)
    return cum_col, to_row(cum_col, row == lane)


def prep_kernel(
    flag_ref, q_ref, k_ref, decay_ref, rate_ref, spread_ref, spread_t_ref, damp_ref, kk_ref, kq_ref, rows_ref, mask_ref,
):
    length = q_ref.shape[1]
    row, lane = ids((length, length))
    cum_col, cum_row = decays(decay_ref[...], row, lane)
    rate_row = rate_ref[...]
    apart = cum_col - cum_row
    spread = jnp.exp(jnp.where(lane <= row, apart, -1e30))
    spread_ref[...] = spread
    spread_t_ref[...] = jnp.exp(jnp.where(lane >= row, -apart, -1e30))
    damp_ref[...] = jnp.where(lane < row, spread, 0.0) * -to_col(rate_row, row == lane)
    k_f, q_f = k_ref[...].astype(F32), q_ref[...].astype(F32)
    k_rows = k_f.T.astype(BF16)
    kk_ref[...] = mm(k_rows, k_ref[...])
    kq_ref[...] = mm(k_rows, q_ref[...])
    grow = jnp.exp(cum_row)
    tail = jnp.exp(cum_row[:, length - 1 :] - cum_row)
    k_sum = jnp.sum(k_f * k_f, 0, keepdims=True)
    q_sum = jnp.sum(q_f * q_f, 0, keepdims=True)
    rows_ref[...] = jnp.concatenate([cum_row, grow, tail, rate_row, k_sum, q_sum, cum_row, cum_row], 0)
    mask_ref[...] = jnp.concatenate([jnp.full((1, mask_ref.shape[1]), flag_ref[i], F32) for i in range(8)], 0)


def gram(left, right):
    return lax.dot_general(left, right, TN, preferred_element_type=F32)


def inverse_kernel(k_ref, other_ref, kk_ref, damp_ref, rows_ref, half_ref, w_ref, scale_ref):
    other = other_ref[...]
    k_t = jnp.concatenate([k_ref[...], other], 0)
    mid = k_t.shape[1] // 2
    upper = kk_ref[0:mid, 0:mid] + gram(other[:, 0:mid], other[:, 0:mid])
    lower = kk_ref[mid:, :] + gram(other[:, mid:], other)
    grow, rate_row, k_sum = (rows_ref[i : i + 1, :] for i in (1, 3, 4))
    other_f = other.astype(F32)
    square = k_sum + jnp.sum(other_f * other_f, 0, keepdims=True) + 1e-6
    k_scale = 1.0 / jnp.sqrt(square)
    both = k_scale * k_scale
    upper = damp_ref[0:mid, 0:mid] * (upper * both[:, 0:mid])
    lower = damp_ref[mid:, :] * (lower * both)
    keys = k_t.astype(F32) * (rate_row * grow)
    (upper, lower), moved, below = inverses(
        [upper, lower[:, mid:]], [keys[:, :mid], keys[:, mid:]], lower[:, :mid]
    )
    w_ref[...] = jnp.concatenate(moved, 1) * both
    half_ref[0:mid, :] = upper
    half_ref[mid : 2 * mid, :] = lower
    half_ref[2 * mid :, :] = below
    scale_ref[...] = jnp.concatenate([k_scale, square * k_scale], 0)


def shift_kernel(
    q_ref, other_ref, k_ref, k_other_ref, g_ref, kq_ref, spread_t_ref, rows_ref, w_ref,
    map_ref, score_g_ref, q_scale_ref,
):
    other = other_ref[...]
    kq = kq_ref[...] + gram(k_other_ref[...], other)
    other_f = other.astype(F32)
    k_t = jnp.concatenate([k_ref[...], k_other_ref[...]], 0)
    q_f = jnp.concatenate([q_ref[...].astype(F32), other_f], 0)
    width, length = k_t.shape
    grow, tail = rows_ref[1:2, :], rows_ref[2:3, :]
    q_sum = rows_ref[5:6, :] + jnp.sum(other_f * other_f, 0, keepdims=True)
    q_scale = width ** (-0.5) / jnp.sqrt(q_sum + 1e-6)
    grad = g_ref[...]
    score_g = mm(spread_t_ref[...] * (kq * q_scale), grad)
    w_t = w_ref[...]
    w_row, w_lane = ids((width, width))
    direct = mm(q_f * (q_scale * grow), grad)
    map_ref[0:width, :] = jnp.where(w_row == w_lane, grow[:, length - 1 :], 0.0) - mm(w_t * tail, k_t, NT)
    map_ref[width:, :] = direct - mm(w_t, score_g)
    score_g_ref[...] = score_g
    q_scale_ref[...] = q_scale


def join_kernel(mask_ref, own_ref, got_ref, total_ref):
    width = own_ref.shape[1]
    low = mask_ref[0:1, :] > 0.0
    own, got = own_ref[width:, :], got_ref[width:, :]
    first = jnp.where(low, own_ref[0:width, :], got_ref[0:width, :])
    total_ref[...] = mm(first, jnp.where(low, got, own)) + jnp.where(low, own, got)


def update_kernel(
    mask_ref, q_ref, q_other_ref, k_ref, k_other_ref, v_ref, g_ref, start_ref, half_ref, spread_ref, rows_ref, scale_ref,
    q_scale_ref, u_ref, base_ref, score_grad_ref, start_t_ref, keep_ref, send_ref,
):
    half, length = q_ref.shape
    q_f = jnp.concatenate([q_ref[...], q_other_ref[...]], 0).astype(F32)
    k_t = jnp.concatenate([k_ref[...], k_other_ref[...]], 0)
    width = k_t.shape[0]
    row, lane = ids((length, length))
    eye = row == lane
    grow, rate_row = rows_ref[1:2, :], rows_ref[3:4, :]
    k_scale, k_norm = scale_ref[0:1, :], scale_ref[1:2, :]
    start = start_ref[...]
    start = jnp.where(mask_ref[2:3, :] > 0.0, start, pltpu.roll(start, half, 1))
    start_t = start.T
    grad = g_ref[...]
    grad_t = grad.astype(F32).T.astype(BF16)
    k_rows = k_t.astype(F32).T.astype(BF16)
    base = v_ref[...].astype(F32) - to_col(grow * k_scale, eye) * mm(k_rows, start, NT)
    mid = length // 2
    write = to_col(k_norm * rate_row, eye) * base
    first = mm(half_ref[0:mid, :], write[0:mid, :])
    second = mm(half_ref[mid : 2 * mid, :], write[mid:, :]) + mm(half_ref[2 * mid :, :], first)
    u = to_col(k_scale, eye) * jnp.concatenate([first, second], 0)
    score_grad = mm(grad, u, NT) * spread_ref[...]
    q_scale = q_scale_ref[...]
    dq = mm(k_t, score_grad * k_scale, NT) + grow * mm(start_t, grad_t)
    unit = q_f * (q_scale * width**0.5)
    dq = q_scale * (dq - unit * jnp.sum(unit * dq, 0, keepdims=True))
    keep_ref[...] = dq[0:half, :]
    send_ref[...] = dq[half:, :]
    u_ref[...] = u
    base_ref[...] = base
    score_grad_ref[...] = score_grad
    start_t_ref[...] = start_t


def local_kernel(
    mask_ref, q_ref, q_other_ref, k_ref, k_other_ref, start_t_ref, half_ref, score_g_ref, damp_ref, rows_ref, scale_ref,
    q_scale_ref, u_ref, score_grad_ref, ahead_ref, after_ref,
    uth_ref, utl_ref, uh_ref, ul_ref, ph_ref, pl_ref, pth_ref, ptl_ref, gh_ref, gl_ref, kh_ref, kl_ref, sym_ref, y_ref, dk_ref,
):
    length = q_ref.shape[1]
    q_f = jnp.concatenate([q_ref[...], q_other_ref[...]], 0).astype(F32)
    k_t = jnp.concatenate([k_ref[...], k_other_ref[...]], 0)
    width = k_t.shape[0]
    eye = jnp.equal(*ids((length, length)))
    grow, tail, rate_row = (rows_ref[i : i + 1, :] for i in range(1, 4))
    k_scale, k_norm = scale_ref[0:1, :], scale_ref[1:2, :]
    low = mask_ref[0:1, :] > 0.0
    ahead_map = jnp.where(low, ahead_ref[0:width, :], jnp.where(jnp.equal(*ids((width, width))), 1.0, 0.0))
    ahead = jnp.where(low, ahead_ref[width:, :], 0.0)
    u = u_ref[...]
    u_ts = split(u.T)
    damp = damp_ref[...]
    mid = length // 2
    solve = jnp.concatenate([score_g_ref[...].T, k_t.astype(F32) * tail], 0) * (k_scale * k_scale)
    second = split(solve[:, mid:])
    first = solve[:, 0:mid] + mm(second, half_ref[2 * mid :, :])
    second = mm(second, half_ref[mid : 2 * mid, :])
    first = mm(first, half_ref[0:mid, :])
    solve = jnp.concatenate([first, second], 1) * k_norm
    depth = solve.shape[0] - width
    y_t, psi_t = solve[0:depth, :], solve[depth:, :]
    psi_s = split(psi_t.T)
    sym = damp + damp.T
    sym_ref[...] = sym
    y_t = y_t + mm(ahead.T, psi_t)
    map_s = split(ahead_map)
    psi_far = mm(psi_s, map_s)
    uz_t = mm(ahead, u_ts)
    y = y_t.T
    y_ref[...] = y
    start_t = start_t_ref[...]
    start_s = split(start_t)
    inner = damp * mm(y, u_ts)
    k_s = split(k_t.astype(F32) * k_scale)
    dk = mm(q_f * q_scale_ref[...], score_grad_ref[...]) - mm(start_s, y_t * (grow * rate_row)) + tail * uz_t
    psi_far_s = split(psi_far)
    psi_far_t = psi_far.T
    ph_ref[0:length, :], pl_ref[0:length, :] = psi_far_s
    ph_ref[length:, :], pl_ref[length:, :] = map_s
    pth_ref[...], ptl_ref[...] = split(psi_far_t)
    gh_ref[...], gl_ref[...] = split(psi_far_t * (grow * rate_row))
    dk_ref[...] = dk + mm(k_s, inner + inner.T)
    uth_ref[...], utl_ref[...] = u_ts
    uh_ref[0:length, :], ul_ref[0:length, :] = split(u)
    uh_ref[length:, :], ul_ref[length:, :] = start_s
    kh_ref[...], kl_ref[...] = k_s


def far_kernel(
    mask_ref, got_ref, k_ref, k_other_ref, rows_ref, scale_ref,
    uth_ref, utl_ref, uh_ref, ul_ref, ph_ref, pl_ref, pth_ref, ptl_ref, gh_ref, gl_ref, kh_ref, kl_ref, sym_ref, dk_ref,
    send_ref, keep_ref,
):
    half, length = k_ref.shape
    k_scale = scale_ref[0:1, :]
    row, lane = ids((length, length))
    got_s = split(jnp.where(mask_ref[1:2, :] > 0.0, got_ref[...], 0.0))
    gu_s = split(mm(got_s, (uth_ref[...], utl_ref[...])))
    right = mm((uh_ref[...], ul_ref[...]), got_s, NT)
    upper = mm(right[0:length, :], (pth_ref[...], ptl_ref[...]))
    left = mm((ph_ref[...], pl_ref[...]), gu_s)
    inner = sym_ref[...] * jnp.where(lane < row, left[0:length, :], upper)
    dk = dk_ref[...] + rows_ref[2:3, :] * left[length:, :] - mm(right[length:, :], (gh_ref[...], gl_ref[...]))
    dk = dk + mm((kh_ref[...], kl_ref[...]), inner)
    unit = jnp.concatenate([k_ref[...], k_other_ref[...]], 0).astype(F32) * k_scale
    dk = k_scale * (dk - unit * jnp.sum(unit * dk, 0, keepdims=True))
    send_ref[...] = dk[half:, :]
    keep_ref[...] = dk[0:half, :]


def value_kernel(
    mask_ref, got_ref, k_ref, k_other_ref, ph_ref, pl_ref, y_ref, base_ref, spread_ref, scale_ref, rows_ref, u_ref, keep_ref, got_q_ref,
    value_ref, rate_out_ref, q_ref,
):
    length = y_ref.shape[0]
    row, lane = ids((length, length))
    eye = row == lane
    k_scale = scale_ref[0:1, :]
    got = jnp.where(mask_ref[1:2, :] > 0.0, got_ref[...], 0.0)
    k_t = jnp.concatenate([k_ref[...], k_other_ref[...]], 0)
    low = jnp.where(lane < row, spread_ref[...] * gram(k_t, k_t), 0.0) * (to_col(k_scale, eye) * k_scale)
    y = y_ref[...] + mm((ph_ref[0:length, :], pl_ref[0:length, :]), got)
    write = base_ref[...] - mm(low, u_ref[...])
    value_ref[...] = to_col(rows_ref[3:4, :], eye) * y
    rate_out_ref[...] = to_row(jnp.sum(y * write, 1, keepdims=True), eye)
    q_ref[...] = keep_ref[...] + got_q_ref[...]


def add_kernel(keep_ref, got_ref, k_ref):
    k_ref[...] = keep_ref[...] + got_ref[...]


def call(kernel, outs, *args, smem=(), cost=1.0):
    shapes = [out if isinstance(out[0], tuple) else (out, F32) for out in outs]
    return pl.pallas_call(
        kernel,
        out_shape=tuple(jax.ShapeDtypeStruct(shape, kind) for shape, kind in shapes),
        in_specs=[
            pl.BlockSpec(memory_space=pltpu.SMEM if i in smem else pltpu.VMEM) for i in range(len(args))
        ],
        out_specs=tuple(pl.BlockSpec(memory_space=pltpu.VMEM) for _ in outs),
        cost_estimate=pl.CostEstimate(flops=int(cost * 1e9), bytes_accessed=1 << 20, transcendentals=0),
        compiler_params=pltpu.CompilerParams(vmem_limit_bytes=24 << 20),
    )(*args)


def swap(x, axis, apart):
    return lax.ppermute(x, axis, [(i, i ^ 1 << apart) for i in range(lax.axis_size(axis))])


def far_scan(section, count, place):
    def dot(left, right):
        return jnp.dot(left, right, precision=lax.Precision.HIGHEST)

    width = section.shape[1]
    own_map, own = section[:width], section[width:]
    ahead_map, ahead = jnp.eye(width, dtype=F32), jnp.zeros_like(own)
    for bit in range(count.bit_length() - 2):
        got = swap(jnp.concatenate([own_map, own], 0), "seq", bit)
        got_map, got = got[:width], got[width:]
        low = (place >> bit) % 2 == 0
        ahead = jnp.where(low, dot(ahead_map, got) + ahead, ahead)
        ahead_map = jnp.where(low, dot(ahead_map, got_map), ahead_map)
        low_map, high_map = jnp.where(low, own_map, got_map), jnp.where(low, got_map, own_map)
        own = dot(low_map, jnp.where(low, got, own)) + jnp.where(low, own, got)
        own_map = dot(low_map, high_map)
    return own, jnp.concatenate([ahead_map, ahead], 0)


def per_device(queries, key_rows, values, log_decay, beta_rate, start_states, output_grad):
    count = lax.axis_size("seq")
    stages = count.bit_length() - 1
    assert count == 1 << stages and stages >= 2
    place = lax.axis_index("seq")
    parity = lax.axis_index("head") % 2
    q_t, k_t = queries.T, key_rows.T
    half, length = q_t.shape
    width = 2 * half
    depth = values.shape[1]
    start = start_states[0, 0]
    square, tall, wide, thin = (length, length), (length, depth), (width, length), (1, length)
    k_other = swap(k_t, "head", 0)
    q_other = swap(q_t, "head", 0)
    low_first = 1 - place % 2 if stages == 2 else place * 0 + 1
    low_last = 1 - (place >> (stages - 1)) % 2
    flags = jnp.stack([low_first, low_last, 1 - parity] + [parity] * 5).astype(F32)
    spread, spread_t, damp, kk_own, kq_own, rows, mask = call(
        prep_kernel, [square, square, square, square, square, (8, length), (8, depth)],
        flags, q_t, k_t, log_decay, beta_rate, smem=(0,),
    )
    halves, w_t, scale = call(
        inverse_kernel, [(length + length // 2, length // 2), wide, (2, length)], k_t, k_other, kk_own, damp, rows
    )
    section, score_g, q_scale = call(
        shift_kernel, [(2 * width, depth), tall, thin],
        q_t, q_other, k_t, k_other, output_grad, kq_own, spread_t, rows, w_t,
    )
    if stages == 2:
        ahead = swap(section, "seq", 0)
        (total,) = call(join_kernel, [(width, depth)], mask, section, ahead)
    else:
        total, ahead = far_scan(section, count, place)
    arrived = swap(total, "seq", stages - 1)
    u, base, score_grad, start_t, keep_q, send_q = call(
        update_kernel, [tall, tall, square, (width, depth), (half, length), (half, length)],
        mask, q_t, q_other, k_t, k_other, values, output_grad, start, halves, spread, rows, scale, q_scale,
    )
    got_q = swap(send_q, "head", 0)
    shapes = [(depth, length), (length + width, depth), (length + width, width), wide, wide, wide]
    *packs, sym, y, dk = call(
        local_kernel, [(shape, BF16) for shape in shapes for _ in range(2)] + [square, tall, wide],
        mask, q_t, q_other, k_t, k_other, start_t, halves, score_g, damp, rows, scale, q_scale, u, score_grad, ahead,
        total,
    )
    send, keep = call(
        far_kernel, [(half, length), (half, length)],
        mask, arrived, k_t, k_other, rows, scale, *packs, sym, dk,
    )
    got_k = swap(send, "head", 0)
    value_grad, rate_grad, query_grad = call(
        value_kernel, [tall, thin, (half, length)],
        mask, arrived, k_t, k_other, packs[4], packs[5], y, base, spread, scale, rows, u, keep_q, got_q,
    )
    (key_grad,) = call(add_kernel, [(half, length)], keep, got_k)
    return (query_grad.T, key_grad.T, value_grad, rate_grad)


def solution(mesh):
    in_specs = (
        P("seq", "head"),
        P("seq", "head"),
        P("seq", "head"),
        P("head", "seq"),
        P("head", "seq"),
        P("seq", "head", None, None),
        P("seq", "head"),
    )
    out_specs = (P("seq", "head"), P("seq", "head"), P("seq", "head"), P("head", "seq"))

    return jax.shard_map(per_device, mesh=mesh, in_specs=in_specs, out_specs=out_specs, check_vma=False)
```

```python
import jax
import jax.numpy as jnp
from jax import lax
from jax.experimental import pallas as pl
from jax.experimental.pallas import tpu as pltpu
from jax.sharding import PartitionSpec as P

F32 = jnp.float32
BF16 = jnp.bfloat16
BASE = 16
PACK = 128
NN = (((1,), (0,)), ((), ()))
NT = (((1,), (1,)), ((), ()))
TN = (((0,), (0,)), ((), ()))


def split(x):
    high = x.astype(BF16)
    return (high, (x - high.astype(F32)).astype(BF16))


def mm(left, right, dims=NN):
    left = left if isinstance(left, tuple) else (left if left.dtype == BF16 else split(left))
    right = right if isinstance(right, tuple) else (right if right.dtype == BF16 else split(right))
    deep, out = (0, 1) if dims is NN else (1, 0)

    def one(a, b):
        return lax.dot_general(a, b, dims, preferred_element_type=F32)

    def join(parts, axis):
        return jnp.concatenate(parts, axis)

    pair_left, pair_right = isinstance(left, tuple), isinstance(right, tuple)
    shape = (right[0] if pair_right else right).shape
    shallow, thin = shape[deep] == PACK, shape[out] == PACK
    rows = (left[0] if pair_left else left).shape[0]
    if pair_left and pair_right:
        high, low = right
        if shallow and thin:
            block = join([join([high, low], out), join([high, jnp.zeros_like(low)], out)], deep)
            both = one(join(left, 1), block)
            return both[:, :PACK] + both[:, PACK:]
        if shallow:
            return one(join(left, 1), join([high, high], deep)) + one(left[0], low)
        if thin:
            both = one(join(left, 0), join(right, out))
            return both[:rows, :PACK] + (both[:rows, PACK:] + both[rows:, :PACK])
        both = one(join(left, 0), high)
        return both[:rows] + (both[rows:] + one(left[0], low))
    if pair_left:
        if shallow:
            return one(join(left, 1), join([right, right], deep))
        both = one(join(left, 0), right)
        return both[:rows] + both[rows:]
    if pair_right:
        if shallow:
            return one(join([left, left], 1), join(right, deep))
        if thin:
            both = one(left, join(right, out))
            return both[:, :PACK] + both[:, PACK:]
        return one(left, right[0]) + one(left, right[1])
    return one(left, right)


def ids(shape):
    return lax.broadcasted_iota(jnp.int32, shape, 0), lax.broadcasted_iota(jnp.int32, shape, 1)


def to_col(row, eye):
    return jnp.sum(jnp.where(eye, row, 0.0), 1, keepdims=True)


def to_row(col, eye):
    return jnp.sum(jnp.where(eye, col, 0.0), 0, keepdims=True)


def base_inverses(nils, base):
    size = nils[0].shape[0]
    count = size // base
    _, lane = ids((base, size))
    block = lane // base
    row, lane = ids((8, size))
    first = lane // base * base
    tiles = range(base // 8)
    parts, solved = [], []
    for nil in nils:
        packed = jnp.where(block == 0, nil[0:base, :], 0.0)
        for b in range(1, count):
            packed = jnp.where(block == b, nil[b * base : (b + 1) * base, :], packed)
        parts.append([packed[8 * t : 8 * t + 8, :] for t in tiles])
        solved.append([jnp.where(row + 8 * t == lane - first, 1.0, 0.0) for t in tiles])
    for j in range(base - 1):
        at = first + j
        for part, done in zip(parts, solved):
            source = done[j // 8][j % 8 : j % 8 + 1, :]
            for t in tiles[(j + 1) // 8 :]:
                factor = jnp.take_along_axis(part[t], at, axis=1)
                if t == j // 8:
                    factor = jnp.where(row + 8 * t > j, factor, 0.0)
                done[t] = done[t] + factor * source
    solved = [jnp.concatenate(done, 0) for done in solved]
    return [jnp.concatenate([jnp.where(block == b, done, 0.0) for b in range(count)], 0) for done in solved]


def inverses(nils, keys, corner):
    size = nils[0].shape[0]
    row, lane = ids((size, size))
    found = base_inverses(nils, BASE)
    width = BASE
    while True:
        factor = 4 if size >= 4 * width else 2
        wide = width * factor
        off = (row // wide == lane // wide) & (row // width != lane // width)
        known = [split(inv) for inv in found]
        steps = [split(mm(inv, jnp.where(off, nil, 0.0))) for inv, nil in zip(known, nils)]
        last = wide == size
        if last:
            moved = [mm(key, inv, NT) for key, inv in zip(keys, known)]
            below = mm(known[1], corner)
        twice = [split(mm(step, step)) for step in steps] if factor == 4 else []
        if last:
            below = below + mm(steps[1], below)
            moved = [m + mm(m, step, NT) for m, step in zip(moved, steps)]
        found = [inv + mm(step, pair) for inv, step, pair in zip(found, steps, known)]
        if last and twice:
            below = below + mm(twice[1], below)
            moved = [m + mm(m, step, NT) for m, step in zip(moved, twice)]
        if last:
            moved[1] = moved[1] + mm(moved[0], below, NT)
        if twice:
            found = [inv + mm(step, inv) for inv, step in zip(found, twice)]
        if last:
            return found, moved, below
        width = wide


def decays(decay_row, row, lane):
    cum_col = jnp.sum(jnp.where(lane <= row, decay_row, 0.0), 1, keepdims=True)
    return cum_col, to_row(cum_col, row == lane)


def prep_kernel(
    flag_ref, q_ref, k_ref, decay_ref, rate_ref, spread_ref, spread_t_ref, damp_ref, kk_ref, kq_ref, rows_ref, mask_ref,
):
    length = q_ref.shape[1]
    row, lane = ids((length, length))
    cum_col, cum_row = decays(decay_ref[...], row, lane)
    rate_row = rate_ref[...]
    apart = cum_col - cum_row
    spread = jnp.exp(jnp.where(lane <= row, apart, -1e30))
    spread_ref[...] = spread
    spread_t_ref[...] = jnp.exp(jnp.where(lane >= row, -apart, -1e30))
    damp_ref[...] = jnp.where(lane < row, spread, 0.0) * -to_col(rate_row, row == lane)
    k_f, q_f = k_ref[...].astype(F32), q_ref[...].astype(F32)
    k_rows = k_f.T.astype(BF16)
    kk_ref[...] = mm(k_rows, k_ref[...])
    kq_ref[...] = mm(k_rows, q_ref[...])
    grow = jnp.exp(cum_row)
    tail = jnp.exp(cum_row[:, length - 1 :] - cum_row)
    k_sum = jnp.sum(k_f * k_f, 0, keepdims=True)
    q_sum = jnp.sum(q_f * q_f, 0, keepdims=True)
    rows_ref[...] = jnp.concatenate([cum_row, grow, tail, rate_row, k_sum, q_sum, cum_row, cum_row], 0)
    mask_ref[...] = jnp.concatenate([jnp.full((1, mask_ref.shape[1]), flag_ref[i], F32) for i in range(8)], 0)


def gram(left, right):
    return lax.dot_general(left, right, TN, preferred_element_type=F32)


def inverse_kernel(
    k_ref, other_ref, kk_ref, damp_ref, rows_ref, half_ref, w_ref, scale_ref, other_rows_ref,
):
    other = other_ref[...]
    k_t = jnp.concatenate([k_ref[...], other], 0)
    mid = k_t.shape[1] // 2
    upper = kk_ref[0:mid, 0:mid] + gram(other[:, 0:mid], other[:, 0:mid])
    lower = kk_ref[mid:, :] + gram(other[:, mid:], other)
    grow, rate_row, k_sum = (rows_ref[i : i + 1, :] for i in (1, 3, 4))
    other_f = other.astype(F32)
    square = k_sum + jnp.sum(other_f * other_f, 0, keepdims=True) + 1e-6
    k_scale = 1.0 / jnp.sqrt(square)
    both = k_scale * k_scale
    upper = damp_ref[0:mid, 0:mid] * (upper * both[:, 0:mid])
    lower = damp_ref[mid:, :] * (lower * both)
    keys = k_t.astype(F32) * (rate_row * grow)
    (upper, lower), moved, below = inverses(
        [upper, lower[:, mid:]], [keys[:, :mid], keys[:, mid:]], lower[:, :mid]
    )
    w_t = jnp.concatenate(moved, 1) * both
    w_ref[...] = w_t
    other_rows_ref[...] = other_f.T.astype(BF16)
    half_ref[0:mid, :] = upper
    half_ref[mid : 2 * mid, :] = lower
    half_ref[2 * mid :, :] = below
    scale_ref[...] = jnp.concatenate([k_scale, square * k_scale], 0)


def shift_kernel(
    q_ref, other_ref, k_ref, k_other_ref, k_rows_ref, g_ref, kq_ref, spread_t_ref, rows_ref, w_ref,
    map_ref, score_g_ref, q_scale_ref,
):
    other = other_ref[...]
    mid = other.shape[1] // 2
    top = kq_ref[0:mid, :] + mm(k_rows_ref[0:mid, :], other)
    bottom = kq_ref[mid:, mid:] + mm(k_rows_ref[mid:, :], other[:, mid:])
    other_f = other.astype(F32)
    q_sum = rows_ref[5:6, :] + jnp.sum(other_f * other_f, 0, keepdims=True)
    width = w_ref.shape[0]
    k_t = jnp.concatenate([k_ref[...], k_other_ref[...]], 0)
    ends = jnp.where(jnp.equal(*ids((width, width))), rows_ref[1:2, 2 * mid - 1 :], 0.0)
    own_map = ends - mm(w_ref[...] * rows_ref[2:3, :], k_t, NT)
    q_scale = width ** (-0.5) / jnp.sqrt(q_sum + 1e-6)
    grad = g_ref[...]
    top = mm(spread_t_ref[0:mid, :] * (top * q_scale), grad)
    bottom = mm(spread_t_ref[mid:, mid:] * (bottom * q_scale[:, mid:]), grad[mid:, :])
    score_g = jnp.concatenate([top, bottom], 0)
    q_f = jnp.concatenate([q_ref[...].astype(F32), other_f], 0)
    direct = mm(q_f * (q_scale * rows_ref[1:2, :]), grad)
    map_ref[width:, :] = direct - mm(w_ref[...], score_g)
    map_ref[0:width, :] = own_map
    score_g_ref[...] = score_g
    q_scale_ref[...] = q_scale


def join_kernel(mask_ref, own_ref, got_ref, total_ref):
    width = own_ref.shape[1]
    low = mask_ref[0:1, :] > 0.0
    own, got = own_ref[width:, :], got_ref[width:, :]
    first = jnp.where(low, own_ref[0:width, :], got_ref[0:width, :])
    total_ref[...] = mm(first, jnp.where(low, got, own)) + jnp.where(low, own, got)


def update_kernel(
    mask_ref, q_ref, q_other_ref, k_ref, k_other_ref, v_ref, g_ref, start_ref, half_ref, spread_ref, rows_ref, scale_ref,
    q_scale_ref, u_ref, base_ref, score_grad_ref, start_t_ref, keep_ref, send_ref,
):
    half, length = q_ref.shape
    q_f = jnp.concatenate([q_ref[...], q_other_ref[...]], 0).astype(F32)
    k_t = jnp.concatenate([k_ref[...], k_other_ref[...]], 0)
    width = k_t.shape[0]
    row, lane = ids((length, length))
    eye = row == lane
    grow, rate_row = rows_ref[1:2, :], rows_ref[3:4, :]
    k_scale, k_norm = scale_ref[0:1, :], scale_ref[1:2, :]
    start = start_ref[...]
    start = jnp.where(mask_ref[2:3, :] > 0.0, start, pltpu.roll(start, half, 1))
    start_t = start.T
    grad = g_ref[...]
    grad_t = grad.astype(F32).T.astype(BF16)
    k_rows = k_t.astype(F32).T.astype(BF16)
    base = v_ref[...].astype(F32) - to_col(grow * k_scale, eye) * mm(k_rows, start, NT)
    mid = length // 2
    write = to_col(k_norm * rate_row, eye) * base
    first = mm(half_ref[0:mid, :], write[0:mid, :])
    second = mm(half_ref[mid : 2 * mid, :], write[mid:, :]) + mm(half_ref[2 * mid :, :], first)
    u = to_col(k_scale, eye) * jnp.concatenate([first, second], 0)
    score_grad = mm(grad, u, NT) * spread_ref[...]
    q_scale = q_scale_ref[...]
    dq = mm(k_t, score_grad * k_scale, NT) + grow * mm(start_t, grad_t)
    unit = q_f * (q_scale * width**0.5)
    dq = q_scale * (dq - unit * jnp.sum(unit * dq, 0, keepdims=True))
    keep_ref[...] = dq[0:half, :]
    send_ref[...] = dq[half:, :]
    u_ref[...] = u
    base_ref[...] = base
    score_grad_ref[...] = score_grad
    start_t_ref[...] = start_t


def local_kernel(
    mask_ref, q_ref, q_other_ref, k_ref, k_other_ref, start_t_ref, half_ref, score_g_ref, damp_ref, rows_ref, scale_ref,
    q_scale_ref, u_ref, score_grad_ref, ahead_ref, after_ref,
    uth_ref, utl_ref, uh_ref, ul_ref, ph_ref, pl_ref, pth_ref, ptl_ref, gh_ref, gl_ref, kh_ref, kl_ref, sym_ref, y_ref, dk_ref,
):
    length = q_ref.shape[1]
    q_f = jnp.concatenate([q_ref[...], q_other_ref[...]], 0).astype(F32)
    k_t = jnp.concatenate([k_ref[...], k_other_ref[...]], 0)
    width = k_t.shape[0]
    eye = jnp.equal(*ids((length, length)))
    grow, tail, rate_row = (rows_ref[i : i + 1, :] for i in range(1, 4))
    k_scale, k_norm = scale_ref[0:1, :], scale_ref[1:2, :]
    low = mask_ref[0:1, :] > 0.0
    ahead_map = jnp.where(low, ahead_ref[0:width, :], jnp.where(jnp.equal(*ids((width, width))), 1.0, 0.0))
    ahead = jnp.where(low, ahead_ref[width:, :], 0.0)
    u = u_ref[...]
    u_ts = split(u.T)
    damp = damp_ref[...]
    mid = length // 2
    solve = jnp.concatenate([score_g_ref[...].T, k_t.astype(F32) * tail], 0) * (k_scale * k_scale)
    second = split(solve[:, mid:])
    first = solve[:, 0:mid] + mm(second, half_ref[2 * mid :, :])
    second = mm(second, half_ref[mid : 2 * mid, :])
    first = mm(first, half_ref[0:mid, :])
    solve = jnp.concatenate([first, second], 1) * k_norm
    depth = solve.shape[0] - width
    y_t, psi_t = solve[0:depth, :], solve[depth:, :]
    psi_s = split(psi_t.T)
    sym = damp + damp.T
    sym_ref[...] = sym
    y_t = y_t + mm(ahead.T, psi_t)
    map_s = split(ahead_map)
    psi_far = mm(psi_s, map_s)
    uz_t = mm(ahead, u_ts)
    y = y_t.T
    y_ref[...] = y
    start_t = start_t_ref[...]
    start_s = split(start_t)
    inner = damp * mm(y, u_ts)
    k_s = split(k_t.astype(F32) * k_scale)
    dk = mm(q_f * q_scale_ref[...], score_grad_ref[...]) - mm(start_s, y_t * (grow * rate_row)) + tail * uz_t
    psi_far_s = split(psi_far)
    psi_far_t = psi_far.T
    ph_ref[0:length, :], pl_ref[0:length, :] = psi_far_s
    ph_ref[length:, :], pl_ref[length:, :] = map_s
    pth_ref[...], ptl_ref[...] = split(psi_far_t)
    gh_ref[...], gl_ref[...] = split(psi_far_t * (grow * rate_row))
    dk_ref[...] = dk + mm(k_s, inner + inner.T)
    uth_ref[...], utl_ref[...] = u_ts
    uh_ref[0:length, :], ul_ref[0:length, :] = split(u)
    uh_ref[length:, :], ul_ref[length:, :] = start_s
    kh_ref[...], kl_ref[...] = k_s


def far_kernel(
    mask_ref, got_ref, k_ref, k_other_ref, rows_ref, scale_ref,
    uth_ref, utl_ref, uh_ref, ul_ref, ph_ref, pl_ref, pth_ref, ptl_ref, gh_ref, gl_ref, kh_ref, kl_ref, sym_ref, dk_ref,
    send_ref, keep_ref,
):
    half, length = k_ref.shape
    k_scale = scale_ref[0:1, :]
    row, lane = ids((length, length))
    got_s = split(jnp.where(mask_ref[1:2, :] > 0.0, got_ref[...], 0.0))
    gu_s = split(mm(got_s, (uth_ref[...], utl_ref[...])))
    right = mm((uh_ref[...], ul_ref[...]), got_s, NT)
    mid = length // 2
    low = lane[:mid, :mid] < row[:mid, :mid]
    gu_left = (gu_s[0][:, :mid], gu_s[1][:, :mid])
    left_top = mm((ph_ref[0:mid, :], pl_ref[0:mid, :]), gu_left)
    left = mm((ph_ref[mid:, :], pl_ref[mid:, :]), gu_s)
    upper = mm(right[0:mid, :], (pth_ref[...], ptl_ref[...]))
    upper_low = mm(right[mid:length, :], (pth_ref[:, mid:], ptl_ref[:, mid:]))
    inner = jnp.concatenate(
        [
            jnp.concatenate([jnp.where(low, left_top, upper[:, :mid]), upper[:, mid:]], 1),
            jnp.concatenate([left[0:mid, :mid], jnp.where(low, left[0:mid, mid:], upper_low)], 1),
        ],
        0,
    )
    inner = sym_ref[...] * inner
    dk = dk_ref[...] + rows_ref[2:3, :] * left[mid:, :] - mm(right[length:, :], (gh_ref[...], gl_ref[...]))
    dk = dk + mm((kh_ref[...], kl_ref[...]), inner)
    unit = jnp.concatenate([k_ref[...], k_other_ref[...]], 0).astype(F32) * k_scale
    dk = k_scale * (dk - unit * jnp.sum(unit * dk, 0, keepdims=True))
    send_ref[...] = dk[half:, :]
    keep_ref[...] = dk[0:half, :]


def value_kernel(
    mask_ref, got_ref, k_ref, k_other_ref, ph_ref, pl_ref, y_ref, base_ref, spread_ref, scale_ref, rows_ref, u_ref, keep_ref, got_q_ref,
    value_ref, rate_out_ref, q_ref,
):
    length = y_ref.shape[0]
    row, lane = ids((length, length))
    eye = row == lane
    k_scale = scale_ref[0:1, :]
    got = jnp.where(mask_ref[1:2, :] > 0.0, got_ref[...], 0.0)
    k_t = jnp.concatenate([k_ref[...], k_other_ref[...]], 0)
    low = jnp.where(lane < row, spread_ref[...] * gram(k_t, k_t), 0.0) * (to_col(k_scale, eye) * k_scale)
    y = y_ref[...] + mm((ph_ref[0:length, :], pl_ref[0:length, :]), got)
    write = base_ref[...] - mm(low, u_ref[...])
    value_ref[...] = to_col(rows_ref[3:4, :], eye) * y
    rate_out_ref[...] = to_row(jnp.sum(y * write, 1, keepdims=True), eye)
    q_ref[...] = keep_ref[...] + got_q_ref[...]


def add_kernel(keep_ref, got_ref, k_ref):
    k_ref[...] = keep_ref[...] + got_ref[...]


def call(kernel, outs, *args, smem=(), cost=1.0):
    shapes = [out if isinstance(out[0], tuple) else (out, F32) for out in outs]
    return pl.pallas_call(
        kernel,
        out_shape=tuple(jax.ShapeDtypeStruct(shape, kind) for shape, kind in shapes),
        in_specs=[
            pl.BlockSpec(memory_space=pltpu.SMEM if i in smem else pltpu.VMEM) for i in range(len(args))
        ],
        out_specs=tuple(pl.BlockSpec(memory_space=pltpu.VMEM) for _ in outs),
        cost_estimate=pl.CostEstimate(flops=int(cost * 1e9), bytes_accessed=1 << 20, transcendentals=0),
        compiler_params=pltpu.CompilerParams(vmem_limit_bytes=24 << 20),
    )(*args)


def swap(x, axis, apart):
    return lax.ppermute(x, axis, [(i, i ^ 1 << apart) for i in range(lax.axis_size(axis))])


def far_scan(section, count, place):
    def dot(left, right):
        return jnp.dot(left, right, precision=lax.Precision.HIGHEST)

    width = section.shape[1]
    own_map, own = section[:width], section[width:]
    ahead_map, ahead = jnp.eye(width, dtype=F32), jnp.zeros_like(own)
    for bit in range(count.bit_length() - 2):
        got = swap(jnp.concatenate([own_map, own], 0), "seq", bit)
        got_map, got = got[:width], got[width:]
        low = (place >> bit) % 2 == 0
        ahead = jnp.where(low, dot(ahead_map, got) + ahead, ahead)
        ahead_map = jnp.where(low, dot(ahead_map, got_map), ahead_map)
        low_map, high_map = jnp.where(low, own_map, got_map), jnp.where(low, got_map, own_map)
        own = dot(low_map, jnp.where(low, got, own)) + jnp.where(low, own, got)
        own_map = dot(low_map, high_map)
    return own, jnp.concatenate([ahead_map, ahead], 0)


def per_device(queries, key_rows, values, log_decay, beta_rate, start_states, output_grad):
    count = lax.axis_size("seq")
    stages = count.bit_length() - 1
    assert count == 1 << stages and stages >= 2
    place = lax.axis_index("seq")
    parity = lax.axis_index("head") % 2
    q_t, k_t = queries.T, key_rows.T
    half, length = q_t.shape
    width = 2 * half
    depth = values.shape[1]
    start = start_states[0, 0]
    square, tall, wide, thin = (length, length), (length, depth), (width, length), (1, length)
    k_other = swap(k_t, "head", 0)
    q_other = swap(q_t, "head", 0)
    low_first = 1 - place % 2 if stages == 2 else place * 0 + 1
    low_last = 1 - (place >> (stages - 1)) % 2
    flags = jnp.stack([low_first, low_last, 1 - parity] + [parity] * 5).astype(F32)
    spread, spread_t, damp, kk_own, kq_own, rows, mask = call(
        prep_kernel, [square, square, square, square, square, (8, length), (8, depth)],
        flags, q_t, k_t, log_decay, beta_rate, smem=(0,),
    )
    halves, w_t, scale, k_rows = call(
        inverse_kernel,
        [(length + length // 2, length // 2), wide, (2, length), ((length, half), BF16)],
        k_t, k_other, kk_own, damp, rows,
    )
    section, score_g, q_scale = call(
        shift_kernel, [(2 * width, depth), tall, thin],
        q_t, q_other, k_t, k_other, k_rows, output_grad, kq_own, spread_t, rows, w_t,
    )
    if stages == 2:
        ahead = swap(section, "seq", 0)
        (total,) = call(join_kernel, [(width, depth)], mask, section, ahead)
    else:
        total, ahead = far_scan(section, count, place)
    arrived = swap(total, "seq", stages - 1)
    u, base, score_grad, start_t, keep_q, send_q = call(
        update_kernel, [tall, tall, square, (width, depth), (half, length), (half, length)],
        mask, q_t, q_other, k_t, k_other, values, output_grad, start, halves, spread, rows, scale, q_scale,
    )
    got_q = swap(send_q, "head", 0)
    shapes = [(depth, length), (length + width, depth), (length + width, width), wide, wide, wide]
    *packs, sym, y, dk = call(
        local_kernel, [(shape, BF16) for shape in shapes for _ in range(2)] + [square, tall, wide],
        mask, q_t, q_other, k_t, k_other, start_t, halves, score_g, damp, rows, scale, q_scale, u, score_grad, ahead,
        total,
    )
    send, keep = call(
        far_kernel, [(half, length), (half, length)],
        mask, arrived, k_t, k_other, rows, scale, *packs, sym, dk,
    )
    got_k = swap(send, "head", 0)
    value_grad, rate_grad, query_grad = call(
        value_kernel, [tall, thin, (half, length)],
        mask, arrived, k_t, k_other, packs[4], packs[5], y, base, spread, scale, rows, u, keep_q, got_q,
    )
    (key_grad,) = call(add_kernel, [(half, length)], keep, got_k)
    return (query_grad.T, key_grad.T, value_grad, rate_grad)


def solution(mesh):
    in_specs = (
        P("seq", "head"),
        P("seq", "head"),
        P("seq", "head"),
        P("head", "seq"),
        P("head", "seq"),
        P("seq", "head", None, None),
        P("seq", "head"),
    )
    out_specs = (P("seq", "head"), P("seq", "head"), P("seq", "head"), P("head", "seq"))

    return jax.shard_map(per_device, mesh=mesh, in_specs=in_specs, out_specs=out_specs, check_vma=False)
```
